256 devices in a mesh: probe: 4 (over y_lo, core), tile: 32 (over z, x), level: 2 (over y_hi).
Axes of the slice: x: 4, y: 4 (y_hi: 2, y_lo: 2; y = y_hi * 2 + y_lo), z: 8, core: 2. Of those that a mesh axis runs over, the one named last changes fastest.
Arguments:
- probe_bits: int32 [4, 64, 256, 256], P('probe', 'level', 'tile'), may hold values from 0 to 1
- kappa_sq: float32 [64, 256, 256], P('level', 'tile'), may hold values from 0.25 to 4
- observed: float32 [64, 256, 256], P('level', 'tile'), may hold values from -0.6 to 0.6
Outputs:
- gradient: float32 [64, 256, 256], P('level', 'tile', 'probe')
The draws below stay inside these ranges and needn't reach their ends.
Inputs may be any that keep to these rules, and one draw needn't show every extreme that they name: `probe_bits`: a probe's sign is 2 times its bit minus 1.
All inputs are finite; a program needn't handle non-finite values.
Results may differ from the reference program's by a relative error of at most 0.0003.
Values sent between devices are 32-bit elements; how exact they have to be, the bound alone decides.
A program may use at most 64 MiB of HBM per device.

```python
import math
import jax
import jax.numpy as jnp
from jax import lax

NY = 256
ITERS = 4
PROBES = 4
NZ = 64
NX = 256


def plant(entries, own_key, smallest, high):
    dims = entries.shape
    spot = [jax.random.randint(jax.random.fold_in(own_key, axis), (), 0, dims[axis]) for axis in range(len(dims))]
    entries = entries.at[tuple(spot)].set(smallest)
    longest = dims.index(max(dims))
    spot[longest] = (spot[longest] + 1) % dims[longest]
    return entries.at[tuple(spot)].set(high)


def level_of(key, shape, split, smallest, top_value):
    def one(position, parts):
        heights = jax.random.uniform(jax.random.fold_in(jax.random.fold_in(key, 6), position), (parts,), jnp.float32, smallest / len(split), top_value / len(split))
        return jnp.repeat(jnp.exp(heights), shape[position] // parts).reshape((-1,) + (1,) * (len(shape) - position - 1))

    loudness = one(*split[0])
    for cut in split[1:]:
        loudness = loudness * one(*cut)
    return loudness


def noise(key, shape, deviation, most, pieces=(), kind=jnp.bfloat16):
    result = deviation * jax.random.normal(key, shape, jnp.float32)
    if pieces:
        result = result * level_of(key, shape, pieces, -0.22, 0.18)
    return jnp.clip(result, -most, most).astype(kind)


def setup_inputs(seed: int = 0) -> dict:
    keys = jax.random.split(jax.random.key(seed), 4)
    return {
        "probe_bits": plant(jax.random.randint(keys[0], (PROBES, NZ, NX, NY), 0, 2), jax.random.fold_in(keys[0], 1), 0, 1).astype(jnp.int32),
        "kappa_sq": jnp.clip(jnp.exp(math.log(4.0) - 2.7725887 * jax.random.uniform(keys[1], (NZ, NX, NY), jnp.float32) ** level_of(keys[1], (NZ, NX, NY), ((0, 2), (1, 32)), -0.2, 0.2)), 0.25, 4.0),
        "observed": noise(keys[2], (NZ, NX, NY), 0.1, 0.6, ((0, 2), (1, 32)), jnp.float32),
    }


VERTICAL = 2.0


def shift_levels(values, stride, level_dim, fill_value):
    level_count = values.shape[level_dim]
    widths = [(0, 0)] * values.ndim
    if stride > 0:
        widths[level_dim] = (stride, 0)
        padded = jnp.pad(values, widths, constant_values=fill_value)
        return lax.slice_in_dim(padded, 0, level_count, axis=level_dim)
    widths[level_dim] = (0, -stride)
    padded = jnp.pad(values, widths, constant_values=fill_value)
    return lax.slice_in_dim(padded, -stride, level_count - stride, axis=level_dim)


def reduction_tables(kappa_sq):
    level_count = kappa_sq.shape[0]
    level_ids = lax.broadcasted_iota(jnp.int32, kappa_sq.shape, 0)
    diagonal = kappa_sq + (4.0 + 2.0 * VERTICAL)
    lower = jnp.where(level_ids > 0, -VERTICAL, 0.0).astype(jnp.float32)
    upper = jnp.where(level_ids < level_count - 1, -VERTICAL, 0.0).astype(jnp.float32)
    tables = []
    stride = 1
    while stride < level_count:
        lower_ratio = -lower / shift_levels(diagonal, stride, 0, 1.0)
        upper_ratio = -upper / shift_levels(diagonal, -stride, 0, 1.0)
        new_diagonal = diagonal + lower_ratio * shift_levels(upper, stride, 0, 0.0) + upper_ratio * shift_levels(lower, -stride, 0, 0.0)
        new_lower = lower_ratio * shift_levels(lower, stride, 0, 0.0)
        upper = upper_ratio * shift_levels(upper, -stride, 0, 0.0)
        lower = new_lower
        diagonal = new_diagonal
        tables.append((lower_ratio, upper_ratio, stride))
        stride = stride * 2
    return tables, 1.0 / diagonal


def vertical_solve(values, tables, inverse_diagonal):
    for lower_ratio, upper_ratio, stride in tables:
        values = values + lower_ratio * shift_levels(values, stride, 1, 0.0) + upper_ratio * shift_levels(values, -stride, 1, 0.0)
    return values * inverse_diagonal


def stencil(padded, values, kappa_sq):
    beside_x = padded[:, 1:-1, 2:, 1:-1] + padded[:, 1:-1, :-2, 1:-1]
    beside_y = padded[:, 1:-1, 1:-1, 2:] + padded[:, 1:-1, 1:-1, :-2]
    beside_z = padded[:, 2:, 1:-1, 1:-1] + padded[:, :-2, 1:-1, 1:-1]
    return (kappa_sq + (4.0 + 2.0 * VERTICAL)) * values - beside_x - beside_y - VERTICAL * beside_z


def apply_k(values, kappa_sq):
    padded = jnp.pad(values, ((0, 0), (1, 1), (1, 1), (1, 1)))
    return stencil(padded, values, kappa_sq)


def reference(probe_bits, kappa_sq, observed):
    tables, inverse_diagonal = reduction_tables(kappa_sq)

    def apply_m(values):
        return vertical_solve(vertical_solve(values, tables, inverse_diagonal), tables, inverse_diagonal)

    def apply_q(values):
        return apply_k(apply_k(values, kappa_sq), kappa_sq)

    def one_probe(running, probe_row):
        sign_field = (2 * probe_row - 1).astype(jnp.float32)[None]
        solution = jnp.zeros_like(sign_field)
        residual = sign_field
        precond = apply_m(residual)
        rho_now = jnp.sum(residual * precond)
        direction = precond
        for iteration in range(ITERS):
            image_field = apply_q(direction)
            step_size = rho_now / jnp.sum(direction * image_field)
            solution = solution + step_size * direction
            if iteration + 1 < ITERS:
                residual = residual - step_size * image_field
                precond = apply_m(residual)
                rho_next = jnp.sum(residual * precond)
                direction = precond + (rho_next / rho_now) * direction
                rho_now = rho_next
        contribution = solution * apply_k(sign_field, kappa_sq) + apply_k(solution, kappa_sq) * sign_field
        return running + contribution[0], None

    trace_sum, unused = lax.scan(one_probe, jnp.zeros(kappa_sq.shape, jnp.float32), probe_bits)
    k_observed = apply_k(observed[None], kappa_sq)[0]
    return kappa_sq * (trace_sum / PROBES - 2.0 * observed * k_observed)
```

```python
import functools

import jax
import jax.numpy as jnp
from jax import lax
from jax.experimental import pallas as pl
from jax.experimental.pallas import tpu as pltpu
from jax.sharding import PartitionSpec as P

MESH = pl.DeviceIdType.MESH
STEPS = 4
F32 = jnp.float32
X_CHIPS = 4

PAIRS = [(i, j) for j in range(STEPS) for i in range(j + 1)]
ROW = {pair: n for n, pair in enumerate(PAIRS)}
N_ROWS = 16


def kernel(
    dims,
    bits_hbm, kap_hbm, obs_hbm, out_ref,
    bits_v, kap_v, obs_v,
    s_m, s_h, d_m, d_h, o_m, o_h,
    m_m, m_h, hg_m, hg_h,
    v_m, v_h, u_m, u_h, r_m, r_h, f_m, f_h, ks, data,
    halo_out, halo_in, xs_out, xs_in,
    setup_m_out, setup_m_in, setup_h_out, setup_h_in,
    pl_out, pl_in,
    gram, red_a, red_b, rs_out, rs_in,
    in_sem, send_sem, recv_sem, sa_sem, ra_sem, sb_sem, rb_sem, sp_sem, rp_sem,
):
    probes, tiles, levels, x_chips, L, Y = dims
    z_chips = tiles // x_chips
    probe = lax.axis_index("probe")
    tile = lax.axis_index("tile")
    half = lax.axis_index("level")
    zc = tile // x_chips
    xc = tile % x_chips
    nxt = lax.rem(tile + 1, tiles)
    prv = lax.rem(tile + tiles - 1, tiles)
    other = 1 - half
    grp = half * x_chips + xc
    n_a = levels * x_chips

    loads = [
        pltpu.make_async_copy(kap_hbm, kap_v, in_sem.at[0]),
        pltpu.make_async_copy(bits_hbm.at[0], bits_v, in_sem.at[1]),
        pltpu.make_async_copy(obs_hbm, obs_v, in_sem.at[2]),
    ]
    for copy in loads:
        copy.start()

    a_peers = []
    for k in range(1, n_a):
        g = lax.rem(grp + k, n_a)
        a_peers.append((g, {"tile": zc * x_chips + g % x_chips, "level": g // x_chips}))
    b_peers = []
    for k in range(1, z_chips):
        g = lax.rem(zc + k, z_chips)
        b_peers.append((g, {"tile": g * x_chips + xc}))
    p_peers = []
    for k in range(1, probes):
        g = lax.rem(probe + k, probes)
        p_peers.append((g, {"probe": g}))

    barrier = pltpu.get_barrier_semaphore()
    greet = [{"tile": nxt}, {"tile": prv}, {"level": other},
             {"tile": nxt, "level": other}, {"tile": prv, "level": other}]
    greet += [d for _, d in a_peers] + [d for _, d in b_peers] + [d for _, d in p_peers]
    for dev in greet:
        pl.semaphore_signal(barrier, inc=1, device_id=dev, device_id_type=MESH)

    sub = lax.broadcasted_iota(jnp.int32, (8, Y), 0)
    lane = lax.broadcasted_iota(jnp.int32, (8, Y), 1)
    lane_h = lax.broadcasted_iota(jnp.int32, (8, 128), 1)
    has_next = (tile < tiles - 1).astype(F32)
    has_prev = (tile > 0).astype(F32)
    mask_h = jnp.where(sub < 2, has_next, jnp.where(sub >= 6, has_prev, 0.0))
    zero = jnp.zeros((8, Y), F32)

    def src(l):
        return half * (L - 1) + (1 - 2 * half) * l

    def send(src_ref, dst_ref, ssem, rsem, dev):
        copy = pltpu.make_async_remote_copy(
            src_ref=src_ref, dst_ref=dst_ref, send_sem=ssem, recv_sem=rsem,
            device_id=dev, device_id_type=MESH)
        copy.start()
        return copy

    started = []
    counter = [0]

    def post(src_ref, dst_ref, dev):
        n = counter[0]
        counter[0] += 1
        copy = send(src_ref, dst_ref, send_sem.at[n], recv_sem.at[n], dev)
        started.append(copy)
        return copy

    def loop(n, chunk, body, init=0):
        chunk = min(chunk, n)

        def step(b, carry):
            for k in range(chunk):
                carry = body(b * chunk + k, carry)
            return carry

        return lax.fori_loop(0, n // chunk, step, init)

    def each(n, chunk, body):
        def step(l, carry):
            body(l)
            return carry
        loop(n, chunk, step)

    def pack(read, up_ref, dn_ref):
        def body(g):
            rows = [read(4 * g + k) for k in range(4)]
            up = rows[3]
            dn = pltpu.roll(rows[3], 6, 0)
            for k in (2, 1, 0):
                up = jnp.where(sub < 2 * k + 2, pltpu.roll(rows[k], 2 * k + 2, 0), up)
                dn = jnp.where(sub < 2 * k + 2, pltpu.roll(rows[k], 2 * k, 0) if k else rows[k], dn)
            up_ref[g] = up
            dn_ref[g] = dn
        each(L // 4, 2, body)

    def unpack(a_ref, b_ref, write):
        def body(g):
            a = a_ref[g]
            b = b_ref[g]
            for k in range(4):
                ra = pltpu.roll(a, 6 - 2 * k, 0) if k < 3 else a
                rb = pltpu.roll(b, 8 - 2 * k, 0) if k else b
                write(4 * g + k, jnp.where(sub >= 4, ra, rb))
        each(L // 4, 2, body)

    def beside(a, b):
        up = jnp.where(sub == 0, pltpu.roll(b, 1, 0), pltpu.roll(a, 1, 0))
        dn = jnp.where(sub == 7, pltpu.roll(b, 7, 0), pltpu.roll(a, 7, 0))
        left = jnp.where(lane == 0, 0.0, pltpu.roll(a, 1, 1))
        right = jnp.where(lane == Y - 1, 0.0, pltpu.roll(a, Y - 1, 1))
        return (up + dn) + (left + right)

    def factor(d_ref, m_ref, hg_ref):
        m_ref[0] = zero

        def up(l, m):
            m = 2.0 / (d_ref[l] - 2.0 * m)
            m_ref[l + 1] = m
            return m
        last = loop(L, 4, up, zero)

        def down(k, h):
            l = L - 1 - k
            h = m_ref[l + 1] * h
            hg_ref[l] = h
            return h
        loop(L, 4, down, zero + 1.0)

        def again(l, g):
            g = 0.5 * hg_ref[l] + m_ref[l] * g
            hg_ref[l] = g
            return g
        return last, loop(L, 4, again, zero)

    def passes(read, m_ref, f_ref):
        def fwd(l, f):
            f = 0.5 * read(l) + m_ref[l] * f
            f_ref[l] = f
            return f
        first = loop(L, 8, fwd, zero)

        def back(k, y):
            l = L - 1 - k
            y = m_ref[l + 1] * (f_ref[l] + y)
            f_ref[l] = y
            return y
        loop(L, 8, back, zero)

        def again(l, g):
            g = 0.5 * f_ref[l] + m_ref[l] * g
            f_ref[l] = g
            return g
        return first, loop(L, 8, again, zero)

    def join(const, own, far):
        mo, ho, mp, hp, inv = const
        (fo, go), (fp, gp) = own, far
        x = mo * (fo + mp * fp) * inv
        xi = mp * (fp + mo * fo) * inv
        g = go + xi * ho
        gf = gp + x * hp
        w = mo * (g + mp * gf) * inv
        eta = mp * (gf + mo * g) * inv
        return xi, w, eta

    loads[0].wait()

    def put_d(l):
        d_m[l] = kap_v[src(l)] + 8.0
    each(L, 4, put_d)
    pack(lambda l: d_m[l], halo_out.at[0, 0], halo_out.at[1, 0])
    loads[1].wait()

    def put_s(l):
        s_m[l + 1] = (2 * bits_v[src(l)] - 1).astype(F32)
    each(L, 4, put_s)
    pack(lambda l: s_m[l + 1], halo_out.at[0, 1], halo_out.at[1, 1])
    loads[2].wait()

    def put_o(l):
        o_m[l + 1] = obs_v[src(l)]
    each(L, 4, put_o)
    pack(lambda l: o_m[l + 1], halo_out.at[0, 2], halo_out.at[1, 2])

    pl.semaphore_wait(barrier, len(greet))
    first = pl.ds(0, 2)
    halo = [
        post(halo_out.at[0, first], halo_in.at[0, first], {"tile": nxt}),
        post(halo_out.at[1, first], halo_in.at[1, first], {"tile": prv}),
    ]
    s_m[0] = zero
    o_m[0] = zero
    for j in range(STEPS):
        v_m[j, 0] = zero
        u_m[j, 0] = zero
    v_h[0] = zero

    mo_m, ho_m = factor(d_m, m_m, hg_m)
    own_m = passes(lambda l: s_m[l + 1], m_m, f_m)
    for n, plane in enumerate((mo_m, ho_m, d_m[L - 1], own_m[0], own_m[1], s_m[L], o_m[L])):
        setup_m_out[n] = plane
    far_m = post(setup_m_out, setup_m_in, {"level": other})
    late = [
        post(halo_out.at[0, 2], halo_in.at[0, 2], {"tile": nxt}),
        post(halo_out.at[1, 2], halo_in.at[1, 2], {"tile": prv}),
    ]

    for copy in halo:
        copy.wait_recv()

    def put_dh(l, x):
        d_h[l] = jnp.where(mask_h > 0.0, x, 8.0)
    unpack(halo_in.at[0, 0], halo_in.at[1, 0], put_dh)

    def put_sh(l, x):
        s_h[l] = x * mask_h
    unpack(halo_in.at[0, 1], halo_in.at[1, 1], put_sh)
    mo_h, ho_h = factor(d_h, m_h, hg_h)
    own_h = passes(lambda l: s_h[l], m_h, f_h)
    for n, plane in enumerate((mo_h, ho_h, own_h[0], own_h[1])):
        setup_h_out[n] = plane
    far_h = post(setup_h_out, setup_h_in, {"level": other})

    far_m.wait_recv()
    mp_m, hp_m, dp_m, fp_m, gp_m = (setup_m_in[n] for n in range(5))
    d_m[L] = dp_m
    s_m[L + 1] = setup_m_in[5]
    o_m[L + 1] = setup_m_in[6]
    far_h.wait_recv()
    mp_h, hp_h, fp_h, gp_h = (setup_h_in[n] for n in range(4))
    const_m = (mo_m, ho_m, mp_m, hp_m, 1.0 / (1.0 - mo_m * mp_m))
    const_h = (mo_h, ho_h, mp_h, hp_h, 1.0 / (1.0 - mo_h * mp_h))

    def finish(j, own_m, own_h, fp_m, gp_m, fp_h, gp_h):
        xi, w, eta = join(const_m, own_m, (fp_m, gp_m))
        beyond = 0.5 * (dp_m * eta - xi) - w
        v_m[j, L + 1] = eta if j == 0 else eta - v_m[j - 1, L + 1]
        v_m[j, L + 2] = beyond if j == 0 else beyond - v_m[j - 1, L + 2]

        def down_m(k, w):
            l = L - 1 - k
            w = m_m[l + 1] * ((f_m[l] + xi * hg_m[l]) + w)
            v_m[j, l + 1] = w if j == 0 else w - v_m[j - 1, l + 1]
            return w
        loop(L, 8, down_m, eta)

        xi_h, w_h, eta_h = join(const_h, own_h, (fp_h, gp_h))
        v_h[L + 1] = eta_h if j == 0 else eta_h - v_h[L + 1]

        def down_h(k, w):
            l = L - 1 - k
            w = m_h[l + 1] * ((f_h[l] + xi_h * hg_h[l]) + w)
            v_h[l + 1] = w if j == 0 else w - v_h[l + 1]
            return w
        loop(L, 8, down_h, eta_h)

    def apply_k(j):
        last = j == STEPS - 1

        def body(l):
            a = v_m[j, l + 1]
            b = v_h[l + 1]
            u_m[j, l + 1] = d_m[l] * a - beside(a, b) - 2.0 * (v_m[j, l] + v_m[j, l + 2])
            if not last:
                u_h[l] = mask_h * (d_h[l] * b - beside(b, a) - 2.0 * (v_h[l] + v_h[l + 2]))

        def end(l):
            a = v_m[j, l + 1]
            u_m[j, l + 1] = d_m[l] * a - beside(a, v_h[l + 1]) - 2.0 * (v_m[j, l] + v_m[j, l + 2])
        each(L, 4, body)
        if not last:
            end(L)

    def again_k(j):
        def body(l):
            a = u_m[j, l + 1]
            r_m[l] = d_m[l] * a - beside(a, u_h[l]) - 2.0 * (u_m[j, l] + u_m[j, l + 2])
        each(L, 4, body)

    def fold(acc):
        row = jnp.sum(acc, axis=0, keepdims=True)
        total = row[:, :128]
        for n in range(1, Y // 128):
            total = total + row[:, n * 128:(n + 1) * 128]
        return total

    def dots(j):
        def body(l, carry):
            u = u_m[j, l + 1]
            out = [carry[0] + v_m[j, l + 1] * s_m[l + 1]]
            for i in range(j + 1):
                out.append(carry[i + 1] + u * u_m[i, l + 1])
            return tuple(out)
        sums = loop(L, 4, body, (zero,) * (j + 2))
        gram[len(PAIRS) + j:len(PAIRS) + j + 1] = fold(sums[0])
        for i in range(j + 1):
            n = ROW[i, j]
            gram[n:n + 1] = fold(sums[i + 1])

    def side_terms():
        for copy in late:
            copy.wait_recv()

        def put_oh(l, x):
            o_h[l] = x * mask_h
        unpack(halo_in.at[0, 2], halo_in.at[1, 2], put_oh)

        def body(l):
            a = s_m[l + 1]
            ks[l] = d_m[l] * a - beside(a, s_h[l]) - 2.0 * (s_m[l] + s_m[l + 2])
            b = o_m[l + 1]
            ko = d_m[l] * b - beside(b, o_h[l]) - 2.0 * (o_m[l] + o_m[l + 2])
            data[l] = 2.0 * b * ko
        each(L, 4, body)

    finish(0, own_m, own_h, fp_m, gp_m, fp_h, gp_h)
    apply_k(0)
    for j in range(1, STEPS):
        n = j - 1
        again_k(j - 1)
        pack(lambda l: r_m[l], xs_out.at[n, 0], xs_out.at[n, 1])
        rows = [
            post(xs_out.at[n, 0], xs_in.at[n, 0], {"tile": nxt}),
            post(xs_out.at[n, 1], xs_in.at[n, 1], {"tile": prv}),
        ]
        own_m = passes(lambda l: r_m[l], m_m, f_m)
        pl_out[n, 0] = own_m[0]
        pl_out[n, 1] = own_m[1]
        planes = [
            post(pl_out.at[n], pl_in.at[n, 0], {"tile": nxt, "level": other}),
            post(pl_out.at[n], pl_in.at[n, 1], {"tile": prv, "level": other}),
            post(pl_out.at[n], pl_in.at[n, 2], {"level": other}),
        ]
        dots(j - 1)
        if j == 1:
            side_terms()
        for copy in rows:
            copy.wait_recv()

        def put_rh(l, x):
            r_h[l] = x * mask_h
        unpack(xs_in.at[n, 0], xs_in.at[n, 1], put_rh)
        own_h = passes(lambda l: r_h[l], m_h, f_h)
        for copy in planes:
            copy.wait_recv()
        fp_h = mask_h * jnp.where(sub >= 4, pl_in[n, 0, 0], pl_in[n, 1, 0])
        gp_h = mask_h * jnp.where(sub >= 4, pl_in[n, 0, 1], pl_in[n, 1, 1])
        finish(j, own_m, own_h, pl_in[n, 2, 0], pl_in[n, 2, 1], fp_h, gp_h)
        apply_k(j)
    for n in range(len(PAIRS) + STEPS, N_ROWS):
        gram[n:n + 1] = jnp.zeros((1, 128), F32)
    dots(STEPS - 1)

    red_a[grp] = gram[...]
    copies = [send(gram, red_a.at[grp], sa_sem.at[g], ra_sem.at[grp], dev) for g, dev in a_peers]
    started.extend(copies)
    for g, dev in a_peers:
        pltpu.make_async_remote_copy(
            src_ref=gram, dst_ref=red_a.at[g], send_sem=sa_sem.at[g], recv_sem=ra_sem.at[g],
            device_id=dev, device_id_type=MESH).wait_recv()
    red_b[zc] = sum((red_a[g] for g in range(1, n_a)), red_a[0])
    for g, dev in b_peers:
        started.append(send(red_b.at[zc], red_b.at[zc], sb_sem.at[g], rb_sem.at[zc], dev))
    for g, dev in b_peers:
        pltpu.make_async_remote_copy(
            src_ref=red_b.at[zc], dst_ref=red_b.at[g], send_sem=sb_sem.at[g], recv_sem=rb_sem.at[g],
            device_id=dev, device_id_type=MESH).wait_recv()
    total = sum((red_b[g] for g in range(1, z_chips)), red_b[0])
    total = jnp.broadcast_to(jnp.sum(total, axis=1, keepdims=True), (N_ROWS, Y))

    a = {}
    for (i, j), n in ROW.items():
        a[i, j] = total[n:n + 1]
    c = [total[len(PAIRS) + j:len(PAIRS) + j + 1] for j in range(STEPS)]
    pivot = []
    ratio = {}
    for j in range(STEPS):
        pivot.append(1.0 / a[j, j])
        for i in range(j + 1, STEPS):
            ratio[j, i] = a[j, i] * pivot[j]
        for i in range(j + 1, STEPS):
            c[i] = c[i] - ratio[j, i] * c[j]
            for k in range(i, STEPS):
                a[i, k] = a[i, k] - ratio[j, i] * a[j, k]
    for j in range(STEPS - 1, -1, -1):
        c[j] = c[j] * pivot[j]
        for i in range(j + 1, STEPS):
            c[j] = c[j] - ratio[j, i] * c[i]
    c = [jnp.broadcast_to(x, (8, Y)) for x in c]

    def term(l):
        x = c[0] * v_m[0, l + 1]
        kx = c[0] * u_m[0, l + 1]
        for j in range(1, STEPS):
            x = x + c[j] * v_m[j, l + 1]
            kx = kx + c[j] * u_m[j, l + 1]
        return x * ks[l] + kx * s_m[l + 1]

    low = lane_h < 64
    H = L // 2

    def fill(l):
        top, bot = term(l), term(l + H)
        for q in range(Y // 128):
            p, b = top[:, q * 128:(q + 1) * 128], bot[:, q * 128:(q + 1) * 128]
            rs_out[2 * q, l] = jnp.where(low, p, pltpu.roll(b, 64, 1))
            rs_out[2 * q + 1, l] = jnp.where(low, pltpu.roll(p, 64, 1), b)
    each(H, 2, fill)
    for g, dev in p_peers:
        started.append(send(rs_out.at[g], rs_in.at[probe], sp_sem.at[g], rp_sem.at[probe], dev))

    odd = lax.rem(probe, 2) == 1
    cols = pl.ds(pl.multiple_of((probe // 2) * 128, 128), 128)
    keep = jnp.where(odd, jnp.where(low, 0, 1), jnp.where(low, 1, 0)) == 1

    def mine(ref, l, k):
        p, b = ref[l, :, cols], ref[k, :, cols]
        at_top = jnp.where(keep, p, pltpu.roll(p, 64, 1))
        at_bot = jnp.where(keep, b, pltpu.roll(b, 64, 1))
        return jnp.where(low, at_top, at_bot)

    for g, dev in p_peers:
        pltpu.make_async_remote_copy(
            src_ref=rs_out.at[g], dst_ref=rs_in.at[g], send_sem=sp_sem.at[g], recv_sem=rp_sem.at[g],
            device_id=dev, device_id_type=MESH).wait_recv()

    def write(l):
        acc = rs_out[probe, l]
        for g, _ in p_peers:
            acc = acc + rs_in[g, l]
        kap = mine(kap_v, src(l), src(l + H))
        res = kap * (acc * (1.0 / probes) - mine(data, l, l + H))
        out_ref[src(l)] = res[:, :64]
        out_ref[src(l + H)] = pltpu.roll(res, 64, 1)[:, :64]
    each(H, 2, write)
    for copy in started:
        copy.wait_send()


def solution(mesh):
    probes, tiles, levels = (mesh.shape[a] for a in ("probe", "tile", "level"))
    x_chips = min(X_CHIPS, tiles)
    z_chips = tiles // x_chips

    def step(bits, kap, obs):
        _, L, rows, Y = bits.shape
        dims = (probes, tiles, levels, x_chips, L, Y)
        vm = lambda *lead: pltpu.VMEM((*lead, 8, Y), F32)
        dma = lambda n: pltpu.SemaphoreType.DMA((n,))
        G = L // 4
        scratch = [
            pltpu.VMEM((L, 8, Y), jnp.int32), vm(L), vm(L),
            vm(L + 2), vm(L), vm(L + 1), vm(L), vm(L + 2), vm(L),
            vm(L + 1), vm(L + 1), vm(L), vm(L),
            vm(STEPS, L + 3), vm(L + 2), vm(STEPS, L + 2), vm(L), vm(L), vm(L), vm(L), vm(L), vm(L), vm(L),
            vm(2, 3, G), vm(2, 3, G), vm(STEPS - 1, 2, G), vm(STEPS - 1, 2, G),
            vm(7), vm(7), vm(4), vm(4),
            vm(STEPS - 1, 2), vm(STEPS - 1, 3, 2),
            pltpu.VMEM((N_ROWS, 128), F32),
            pltpu.VMEM((levels * x_chips, N_ROWS, 128), F32),
            pltpu.VMEM((z_chips, N_ROWS, 128), F32),
            pltpu.VMEM((probes, L // 2, 8, 128), F32),
            pltpu.VMEM((probes, L // 2, 8, 128), F32),
            dma(3), dma(21), dma(21),
            dma(levels * x_chips), dma(levels * x_chips), dma(z_chips), dma(z_chips), dma(probes), dma(probes),
        ]
        return pl.pallas_call(
            functools.partial(kernel, dims),
            out_shape=jax.ShapeDtypeStruct((L, rows, Y // probes), F32),
            in_specs=[pl.BlockSpec(memory_space=pl.ANY)] * 3,
            out_specs=pl.BlockSpec(memory_space=pltpu.VMEM),
            scratch_shapes=scratch,
            compiler_params=pltpu.CompilerParams(collective_id=0, has_side_effects=True),
        )(bits, kap, obs)

    return jax.shard_map(
        step,
        mesh=mesh,
        in_specs=(P("probe", "level", "tile", None), P("level", "tile", None), P("level", "tile", None)),
        out_specs=P("level", "tile", "probe"),
        check_vma=False,
    )
```

```python
import functools

import jax
import jax.numpy as jnp
from jax import lax
from jax.experimental import pallas as pl
from jax.experimental.pallas import tpu as pltpu
from jax.sharding import PartitionSpec as P

MESH = pl.DeviceIdType.MESH
STEPS = 4
F32 = jnp.float32
X_CHIPS = 4

PAIRS = [(i, j) for j in range(STEPS) for i in range(j + 1)]
ROW = {pair: n for n, pair in enumerate(PAIRS)}
N_ROWS = 16


def kernel(
    dims,
    bits_hbm, kap_hbm, obs_hbm, out_ref,
    bits_v, kap_v, obs_v,
    s_m, s_h, d_m, d_h, o_m, o_h,
    m_m, m_h, hg_m, hg_h,
    v_m, v_h, u_m, u_h, r_m, r_h, f_m, f_h, ks,
    halo_out, halo_in, xs_out, xs_in,
    first_out, first_in, pl_out, pl_in,
    gram, red_out, red_a, red_b, t_out, t_in, kap_q, sub_q, data,
    in_sem, send_sem, recv_sem,
):
    probes, tiles, levels, x_chips, L, Y = dims
    z_chips = tiles // x_chips
    H = L // 2
    probe = lax.axis_index("probe")
    tile = lax.axis_index("tile")
    half = lax.axis_index("level")
    zc = tile // x_chips
    xc = tile % x_chips
    nxt = lax.rem(tile + 1, tiles)
    prv = lax.rem(tile + tiles - 1, tiles)
    other = 1 - half
    n_a = probes * levels * x_chips
    spot = (probe * levels + half) * x_chips + xc

    loads = [
        pltpu.make_async_copy(kap_hbm, kap_v, in_sem.at[0]),
        pltpu.make_async_copy(bits_hbm.at[0], bits_v, in_sem.at[1]),
        pltpu.make_async_copy(obs_hbm, obs_v, in_sem.at[2]),
    ]
    for copy in loads:
        copy.start()

    a_peers = []
    for k in range(1, n_a):
        g = lax.rem(spot + k, n_a)
        a_peers.append({
            "probe": g // (levels * x_chips),
            "tile": zc * x_chips + g % x_chips,
            "level": (g // x_chips) % levels,
        })
    b_peers = [{"tile": lax.rem(zc + k, z_chips) * x_chips + xc} for k in range(1, z_chips)]
    p_peers = [lax.rem(probe + k, probes) for k in range(1, probes)]

    barrier = pltpu.get_barrier_semaphore()
    greet = [{"tile": nxt}, {"tile": prv}, {"tile": nxt, "level": other}, {"tile": prv, "level": other}]
    greet += a_peers + b_peers
    for dev in greet:
        pl.semaphore_signal(barrier, inc=1, device_id=dev, device_id_type=MESH)

    sub = lax.broadcasted_iota(jnp.int32, (8, Y), 0)
    lane_h = lax.broadcasted_iota(jnp.int32, (8, 128), 1)
    sub_h = lax.broadcasted_iota(jnp.int32, (8, 128), 0)
    has_next = (tile < tiles - 1).astype(F32)
    has_prev = (tile > 0).astype(F32)
    mask_h = jnp.where(sub < 2, has_next, jnp.where(sub >= 6, has_prev, 0.0))
    zero = jnp.zeros((8, Y), F32)

    def src(l):
        return half * (L - 1) + (1 - 2 * half) * l

    def send(src_ref, dst_ref, ssem, rsem, dev):
        copy = pltpu.make_async_remote_copy(
            src_ref=src_ref, dst_ref=dst_ref, send_sem=ssem, recv_sem=rsem,
            device_id=dev, device_id_type=MESH)
        copy.start()
        return copy

    started = []
    counter = [0]

    def post(src_ref, dst_ref, dev):
        n = counter[0]
        counter[0] += 1
        copy = send(src_ref, dst_ref, send_sem.at[n], recv_sem.at[n], dev)
        started.append(copy)
        return copy

    def loop(n, chunk, body, init=0):
        chunk = min(chunk, n)

        def step(b, carry):
            for k in range(chunk):
                carry = body(b * chunk + k, carry)
            return carry

        return lax.fori_loop(0, n // chunk, step, init)

    def each(n, chunk, body):
        def step(l, carry):
            body(l)
            return carry
        loop(n, chunk, step)

    def pack_rows(rows, g, up_ref, dn_ref):
        up = rows[3]
        dn = pltpu.roll(rows[3], 6, 0)
        for k in (2, 1, 0):
            up = jnp.where(sub < 2 * k + 2, pltpu.roll(rows[k], 2 * k + 2, 0), up)
            dn = jnp.where(sub < 2 * k + 2, pltpu.roll(rows[k], 2 * k, 0) if k else rows[k], dn)
        up_ref[g] = up
        dn_ref[g] = dn

    def pack(put, up_ref, dn_ref):
        each(L // 4, 2, lambda g: pack_rows([put(4 * g + k) for k in range(4)], g, up_ref, dn_ref))

    def unpack(a_ref, b_ref, write):
        def body(g):
            a = a_ref[g]
            b = b_ref[g]
            for k in range(4):
                ra = pltpu.roll(a, 6 - 2 * k, 0) if k < 3 else a
                rb = pltpu.roll(b, 8 - 2 * k, 0) if k else b
                write(4 * g + k, jnp.where(sub >= 4, ra, rb))
        each(L // 4, 2, body)

    first_lane = lane_h == 0
    last_lane = lane_h == 127

    def sides(a):
        parts = [a[:, n * 128:(n + 1) * 128] for n in range(Y // 128)]
        right = [pltpu.roll(x, 1, 1) for x in parts]
        left = [pltpu.roll(x, 127, 1) for x in parts]
        out = []
        for n in range(len(parts)):
            before = jnp.where(first_lane, right[n - 1] if n else 0.0, right[n])
            after = jnp.where(last_lane, left[n + 1] if n + 1 < len(parts) else 0.0, left[n])
            out.append(before + after)
        return jnp.concatenate(out, axis=1)

    def beside(a, b):
        up = jnp.where(sub == 0, pltpu.roll(b, 1, 0), pltpu.roll(a, 1, 0))
        dn = jnp.where(sub == 7, pltpu.roll(b, 7, 0), pltpu.roll(a, 7, 0))
        return (up + dn) + sides(a)

    def factor(d_ref, m_ref, hg_ref):
        m_ref[0] = zero

        def up(l, m):
            m = 2.0 / (d_ref[l] - 2.0 * m)
            m_ref[l + 1] = m
            return m
        last = loop(L, 8, up, zero)

        def down(k, h):
            l = L - 1 - k
            h = m_ref[l + 1] * h
            hg_ref[l] = h
            return h
        loop(L, 8, down, zero + 1.0)

        def again(l, g):
            g = 0.5 * hg_ref[l] + m_ref[l] * g
            hg_ref[l] = g
            return g
        return last, loop(L, 8, again, zero)

    def passes(read, m_ref, f_ref):
        def fwd(l, f):
            f = 0.5 * read(l) + m_ref[l] * f
            f_ref[l] = f
            return f
        first = loop(L, 16, fwd, zero)

        def back(k, y):
            l = L - 1 - k
            y = m_ref[l + 1] * (f_ref[l] + y)
            f_ref[l] = y
            return y
        loop(L, 16, back, zero)

        def again(l, g):
            g = 0.5 * f_ref[l] + m_ref[l] * g
            f_ref[l] = g
            return g
        return first, loop(L, 16, again, zero)

    def join(const, own, far):
        mo, ho, mp, hp, inv = const
        (fo, go), (fp, gp) = own, far
        x = mo * (fo + mp * fp) * inv
        xi = mp * (fp + mo * fo) * inv
        g = go + xi * ho
        gf = gp + x * hp
        w = mo * (g + mp * gf) * inv
        eta = mp * (gf + mo * g) * inv
        return xi, w, eta

    def finish_m(j, const, own, far, dp):
        xi, w, eta = join(const, own, far)
        beyond = 0.5 * (dp * eta - xi) - w
        v_m[j, L + 1] = eta if j == 0 else eta - v_m[j - 1, L + 1]
        v_m[j, L + 2] = beyond if j == 0 else beyond - v_m[j - 1, L + 2]

        def down(k, w):
            l = L - 1 - k
            w = m_m[l + 1] * ((f_m[l] + xi * hg_m[l]) + w)
            v_m[j, l + 1] = w if j == 0 else w - v_m[j - 1, l + 1]
            return w
        loop(L, 16, down, eta)

    def finish_h(j, const, own, far):
        xi, w, eta = join(const, own, far)
        v_h[L + 1] = eta if j == 0 else eta - v_h[L + 1]

        def down(k, w):
            l = L - 1 - k
            w = m_h[l + 1] * ((f_h[l] + xi * hg_h[l]) + w)
            v_h[l + 1] = w if j == 0 else w - v_h[l + 1]
            return w
        loop(L, 16, down, eta)

    def inner_k(j):
        def body(l):
            a = v_m[j, l + 1]
            rows = jnp.where(sub == 0, 0.0, pltpu.roll(a, 1, 0)) + jnp.where(sub == 7, 0.0, pltpu.roll(a, 7, 0))
            u_m[j, l + 1] = (d_m[l] * a - (rows + sides(a))) - 2.0 * (v_m[j, l] + v_m[j, l + 2])
        each(L, 8, body)
        if j < STEPS - 1:
            body(L)

    def outer_k(j):
        def fix(l, b):
            add = jnp.where(sub == 0, pltpu.roll(b, 1, 0), jnp.where(sub == 7, pltpu.roll(b, 7, 0), 0.0))
            u_m[j, l + 1] = u_m[j, l + 1] - add

        def body(l):
            b = v_h[l + 1]
            fix(l, b)
            if j < STEPS - 1:
                u = (d_h[l] * b - beside(b, v_m[j, l + 1])) - 2.0 * (v_h[l] + v_h[l + 2])
                u_h[l] = mask_h * u
        each(L, 8, body)
        if j < STEPS - 1:
            fix(L, v_h[L + 1])

    def again_k(j, l):
        a = u_m[j, l + 1]
        r = (d_m[l] * a - beside(a, u_h[l])) - 2.0 * (u_m[j, l] + u_m[j, l + 2])
        r_m[l] = r
        return r

    def fold(acc):
        row = jnp.sum(acc, axis=0, keepdims=True)
        total = row[:, :128]
        for n in range(1, Y // 128):
            total = total + row[:, n * 128:(n + 1) * 128]
        return total

    def dots(j):
        def body(l, carry):
            u = u_m[j, l + 1]
            out = [carry[0] + v_m[j, l + 1] * s_m[l + 1]]
            for i in range(j + 1):
                out.append(carry[i + 1] + u * u_m[i, l + 1])
            return tuple(out)
        sums = loop(L, 8, body, (zero,) * (j + 2))
        gram[len(PAIRS) + j:len(PAIRS) + j + 1] = fold(sums[0])
        for i in range(j + 1):
            n = ROW[i, j]
            gram[n:n + 1] = fold(sums[i + 1])

    low = lane_h < 64

    def quarter(q, top, bot):
        n = q // 2
        p, b = top[:, n * 128:(n + 1) * 128], bot[:, n * 128:(n + 1) * 128]
        if q % 2 == 0:
            return jnp.where(low, p, pltpu.roll(b, 64, 1))
        return jnp.where(low, pltpu.roll(p, 64, 1), b)

    def fill_t(j):
        def body(l):
            top = v_m[j, l + 1] * ks[l] + u_m[j, l + 1] * s_m[l + 1]
            k = l + H
            bot = v_m[j, k + 1] * ks[k] + u_m[j, k + 1] * s_m[k + 1]
            for q in range(probes):
                t_out[j, q, l] = quarter(q, top, bot)
            t_in[j, probe, l] = t_out[j, probe, l]
        each(H, 2, body)

    trace_parts = []

    def send_t(j):
        for g in p_peers:
            trace_parts.append(post(t_out.at[j, g], t_in.at[j, probe], {"probe": g}))

    loads[0].wait()

    def put_d(l):
        d = kap_v[src(l)] + 8.0
        d_m[l] = d
        return d
    pack(put_d, halo_out.at[0, 0], halo_out.at[0, 1])
    pl.semaphore_wait(barrier, len(greet))
    halo_d = [
        post(halo_out.at[0, 0], halo_in.at[0, 0], {"tile": nxt}),
        post(halo_out.at[0, 1], halo_in.at[0, 1], {"tile": prv}),
    ]
    loads[1].wait()

    def put_s(l):
        s = (2 * bits_v[src(l)] - 1).astype(F32)
        s_m[l + 1] = s
        return s
    pack(put_s, halo_out.at[1, 0], halo_out.at[1, 1])
    halo_s = [
        post(halo_out.at[1, 0], halo_in.at[1, 0], {"tile": nxt}),
        post(halo_out.at[1, 1], halo_in.at[1, 1], {"tile": prv}),
    ]
    s_m[0] = zero
    o_m[0] = zero
    for j in range(STEPS):
        v_m[j, 0] = zero
        u_m[j, 0] = zero
    v_h[0] = zero

    mo_m, ho_m = factor(d_m, m_m, hg_m)
    own_m = passes(lambda l: s_m[l + 1], m_m, f_m)
    loads[2].wait()
    for n, plane in enumerate((mo_m, ho_m, own_m[0], own_m[1], d_m[L - 1], s_m[L], obs_v[src(L - 1)])):
        first_out[n] = plane
    far = [
        post(first_out.at[pl.ds(0, 4)], first_in.at[0, pl.ds(0, 4)], {"tile": nxt, "level": other}),
        post(first_out.at[pl.ds(0, 4)], first_in.at[1, pl.ds(0, 4)], {"tile": prv, "level": other}),
        post(first_out, first_in.at[2], {"level": other}),
    ]

    def put_o(l):
        o = obs_v[src(l)]
        o_m[l + 1] = o
        return o
    pack(put_o, halo_out.at[2, 0], halo_out.at[2, 1])
    halo_o = [
        post(halo_out.at[2, 0], halo_in.at[2, 0], {"tile": nxt}),
        post(halo_out.at[2, 1], halo_in.at[2, 1], {"tile": prv}),
    ]

    for copy in halo_d:
        copy.wait_recv()

    def put_dh(l, x):
        d_h[l] = jnp.where(mask_h > 0.0, x, 8.0)
    unpack(halo_in.at[0, 0], halo_in.at[0, 1], put_dh)
    mo_h, ho_h = factor(d_h, m_h, hg_h)

    far[2].wait_recv()
    mp_m, hp_m, fp_m, gp_m, dp_m = (first_in[2, n] for n in range(5))
    d_m[L] = dp_m
    s_m[L + 1] = first_in[2, 5]
    o_m[L + 1] = first_in[2, 6]
    const_m = (mo_m, ho_m, mp_m, hp_m, 1.0 / (1.0 - mo_m * mp_m))
    finish_m(0, const_m, own_m, (fp_m, gp_m), dp_m)
    inner_k(0)

    for copy in halo_s:
        copy.wait_recv()

    def put_sh(l, x):
        s_h[l] = x * mask_h
    unpack(halo_in.at[1, 0], halo_in.at[1, 1], put_sh)
    own_h = passes(lambda l: s_h[l], m_h, f_h)
    for copy in far[:2]:
        copy.wait_recv()

    def beyond_rows(a, b):
        return jnp.where(sub >= 4, a, b)
    mp_h, hp_h, fp_h, gp_h = (beyond_rows(first_in[0, n], first_in[1, n]) for n in range(4))
    const_h = (mo_h, ho_h, mp_h, hp_h, 1.0 / (1.0 - mo_h * mp_h))
    finish_h(0, const_h, own_h, (mask_h * fp_h, mask_h * gp_h))
    outer_k(0)

    odd = lax.rem(probe, 2) == 1
    upper = probe // 2 == 1

    def mine(top, bot):
        out = [jnp.where(odd, quarter(2 * n + 1, top, bot), quarter(2 * n, top, bot)) for n in range(Y // 128)]
        return jnp.where(upper, out[1], out[0])

    def side_terms():
        for copy in halo_o:
            copy.wait_recv()

        def put_oh(l, x):
            o_h[l] = x * mask_h
        unpack(halo_in.at[2, 0], halo_in.at[2, 1], put_oh)

        def body(l):
            a = s_m[l + 1]
            ks[l] = (d_m[l] * a - beside(a, s_h[l])) - 2.0 * (s_m[l] + s_m[l + 2])
            b = o_m[l + 1]
            ko = (d_m[l] * b - beside(b, o_h[l])) - 2.0 * (o_m[l] + o_m[l + 2])
            data[l] = kap_v[src(l)] * (2.0 * b * ko)
        each(L, 4, body)

    def quarters():
        def body(l):
            kap_q[l] = mine(kap_v[src(l)], kap_v[src(l + H)]) * (1.0 / probes)
            sub_q[l] = mine(data[l], data[l + H])
        each(H, 2, body)

    for j in range(1, STEPS):
        n = j - 1
        pack(lambda l: again_k(j - 1, l), xs_out.at[n, 0], xs_out.at[n, 1])
        rows = [
            post(xs_out.at[n, 0], xs_in.at[n, 0], {"tile": nxt}),
            post(xs_out.at[n, 1], xs_in.at[n, 1], {"tile": prv}),
        ]
        own_m = passes(lambda l: r_m[l], m_m, f_m)
        pl_out[n, 0] = own_m[0]
        pl_out[n, 1] = own_m[1]
        planes = [
            post(pl_out.at[n], pl_in.at[n, 0], {"tile": nxt, "level": other}),
            post(pl_out.at[n], pl_in.at[n, 1], {"tile": prv, "level": other}),
            post(pl_out.at[n], pl_in.at[n, 2], {"level": other}),
        ]
        dots(j - 1)
        if j == 1:
            side_terms()
        if j == 2:
            quarters()
        fill_t(j - 1)
        planes[2].wait_recv()
        finish_m(j, const_m, own_m, (pl_in[n, 2, 0], pl_in[n, 2, 1]), dp_m)
        inner_k(j)
        for copy in rows:
            copy.wait_recv()

        def put_rh(l, x):
            r_h[l] = x * mask_h
        unpack(xs_in.at[n, 0], xs_in.at[n, 1], put_rh)
        own_h = passes(lambda l: r_h[l], m_h, f_h)
        for copy in planes[:2]:
            copy.wait_recv()
        send_t(j - 1)
        fp_h = mask_h * beyond_rows(pl_in[n, 0, 0], pl_in[n, 1, 0])
        gp_h = mask_h * beyond_rows(pl_in[n, 0, 1], pl_in[n, 1, 1])
        finish_h(j, const_h, own_h, (fp_h, gp_h))
        outer_k(j)
    for n in range(len(PAIRS) + STEPS, N_ROWS):
        gram[n:n + 1] = jnp.zeros((1, 128), F32)
    dots(STEPS - 1)

    wide = lax.broadcasted_iota(jnp.int32, (N_ROWS, 128), 1) == lax.broadcasted_iota(jnp.int32, (N_ROWS, 128), 0)
    each_sum = jnp.sum(gram[...], axis=1, keepdims=True)
    packed = jnp.sum(jnp.where(wide, each_sum, 0.0), axis=0, keepdims=True)
    red_out[...] = packed
    red_a[spot] = packed
    plane = [post(red_out, red_a.at[spot], dev) for dev in a_peers]
    fill_t(STEPS - 1)
    send_t(STEPS - 1)
    for copy in plane:
        copy.wait_recv()
    for p in range(probes):
        base = p * levels * x_chips
        part = red_a[base]
        for k in range(1, levels * x_chips):
            part = part + red_a[base + k]
        red_b[zc, p] = part
    line = [post(red_b.at[zc], red_b.at[zc], dev) for dev in b_peers]
    for copy in line:
        copy.wait_recv()
    total = None
    for p in range(probes):
        part = red_b[0, p]
        for k in range(1, z_chips):
            part = part + red_b[k, p]
        part = jnp.broadcast_to(part, (8, 128))
        total = part if p == 0 else jnp.where(sub_h == p, part, total)

    def column(n):
        return jnp.broadcast_to(total[:, n:n + 1], (8, 128))
    a = {pair: column(n) for pair, n in ROW.items()}
    c = [column(len(PAIRS) + j) for j in range(STEPS)]
    pivot = []
    ratio = {}
    for j in range(STEPS):
        pivot.append(1.0 / a[j, j])
        for i in range(j + 1, STEPS):
            ratio[j, i] = a[j, i] * pivot[j]
        for i in range(j + 1, STEPS):
            c[i] = c[i] - ratio[j, i] * c[j]
            for k in range(i, STEPS):
                a[i, k] = a[i, k] - ratio[j, i] * a[j, k]
    for j in range(STEPS - 1, -1, -1):
        c[j] = c[j] * pivot[j]
        for i in range(j + 1, STEPS):
            c[j] = c[j] - ratio[j, i] * c[i]
    weight = {(p, j): jnp.broadcast_to(c[j][p:p + 1], (8, 128)) for p in range(probes) for j in range(STEPS)}

    for copy in trace_parts:
        copy.wait_recv()

    def write(l):
        acc = None
        for j in range(STEPS):
            for p in range(probes):
                part = weight[p, j] * t_in[j, p, l]
                acc = part if acc is None else acc + part
        res = kap_q[l] * acc - sub_q[l]
        out_ref[src(l)] = res[:, :64]
        out_ref[src(l + H)] = pltpu.roll(res, 64, 1)[:, :64]
    each(H, 4, write)
    for copy in started:
        copy.wait_send()


def solution(mesh):
    probes, tiles, levels = (mesh.shape[a] for a in ("probe", "tile", "level"))
    x_chips = min(X_CHIPS, tiles)
    z_chips = tiles // x_chips

    def step(bits, kap, obs):
        _, L, rows, Y = bits.shape
        dims = (probes, tiles, levels, x_chips, L, Y)
        vm = lambda *lead: pltpu.VMEM((*lead, 8, Y), F32)
        dma = lambda n: pltpu.SemaphoreType.DMA((n,))
        G = L // 4
        n_sems = 9 + 5 * (STEPS - 1) + (probes * levels * x_chips - 1) + (z_chips - 1) + STEPS * (probes - 1)
        part = lambda *lead: pltpu.VMEM((*lead, L // 2, 8, 128), F32)
        scratch = [
            pltpu.VMEM((L, 8, Y), jnp.int32), vm(L), vm(L),
            vm(L + 2), vm(L), vm(L + 1), vm(L), vm(L + 2), vm(L),
            vm(L + 1), vm(L + 1), vm(L), vm(L),
            vm(STEPS, L + 3), vm(L + 2), vm(STEPS, L + 2), vm(L), vm(L), vm(L), vm(L), vm(L), vm(L),
            vm(3, 2, G), vm(3, 2, G), vm(STEPS - 1, 2, G), vm(STEPS - 1, 2, G),
            vm(7), vm(3, 7), vm(STEPS - 1, 2), vm(STEPS - 1, 3, 2),
            pltpu.VMEM((N_ROWS, 128), F32),
            pltpu.VMEM((1, 128), F32),
            pltpu.VMEM((probes * levels * x_chips, 1, 128), F32),
            pltpu.VMEM((z_chips, probes, 1, 128), F32),
            part(STEPS, probes), part(STEPS, probes), part(), part(), vm(L),
            dma(3), dma(n_sems), dma(n_sems),
        ]
        return pl.pallas_call(
            functools.partial(kernel, dims),
            out_shape=jax.ShapeDtypeStruct((L, rows, Y // probes), F32),
            in_specs=[pl.BlockSpec(memory_space=pl.ANY)] * 3,
            out_specs=pl.BlockSpec(memory_space=pltpu.VMEM),
            scratch_shapes=scratch,
            compiler_params=pltpu.CompilerParams(collective_id=0, has_side_effects=True),
        )(bits, kap, obs)

    return jax.shard_map(
        step,
        mesh=mesh,
        in_specs=(P("probe", "level", "tile", None), P("level", "tile", None), P("level", "tile", None)),
        out_specs=P("level", "tile", "probe"),
        check_vma=False,
    )
```

```python
import functools

import jax
import jax.numpy as jnp
from jax import lax
from jax.experimental import pallas as pl
from jax.experimental.pallas import tpu as pltpu
from jax.sharding import PartitionSpec as P

MESH = pl.DeviceIdType.MESH
STEPS = 4
F32 = jnp.float32
X_CHIPS = 4

PAIRS = [(i, j) for j in range(STEPS) for i in range(j + 1)]
ROW = {pair: n for n, pair in enumerate(PAIRS)}
N_ROWS = 16


def kernel(
    dims,
    bits_hbm, kap_hbm, obs_hbm, out_ref,
    bits_v, kap_v, obs_v,
    s_m, s_h, d_m, d_h, o_m, o_h,
    m_m, m_h, hg_m, hg_h, al_m, be_m,
    v_m, v_h, u_m, u_h, r_m, r_h, f_m, f_h, y_f, ks,
    halo_out, halo_in, xs_out, xs_in,
    first_out, first_in, side_out, side_in, pl_out, pl_in, ed_out, ed_in,
    gram, red_out, red_a, red_b, t_out, t_in, kap_q, sub_q, data,
    in_sem, send_sem, recv_sem,
):
    probes, tiles, levels, x_chips, L, Y = dims
    z_chips = tiles // x_chips
    H = L // 2
    probe = lax.axis_index("probe")
    tile = lax.axis_index("tile")
    half = lax.axis_index("level")
    zc = tile // x_chips
    xc = tile - zc * x_chips
    nxt = lax.rem(tile + 1, tiles)
    prv = lax.rem(tile + tiles - 1, tiles)
    other = 1 - half
    n_a = probes * levels * x_chips
    spot = (probe * levels + half) * x_chips + xc

    loads = [
        pltpu.make_async_copy(kap_hbm, kap_v, in_sem.at[0]),
        pltpu.make_async_copy(bits_hbm.at[0], bits_v, in_sem.at[1]),
        pltpu.make_async_copy(obs_hbm, obs_v, in_sem.at[2]),
    ]
    for copy in loads:
        copy.start()

    near_p = [probe] + [lax.rem(probe + k, probes) for k in range(1, probes)]
    near_x = [tile] + [tile - xc + lax.rem(xc + k, x_chips) for k in range(1, x_chips)]
    near_h = [half, other]
    a_peers = [{"probe": p, "tile": t, "level": h} for t in near_x for h in near_h for p in near_p][1:]
    b_peers = [{"tile": lax.rem(tile + k * x_chips, tiles)} for k in range(1, z_chips)]
    p_peers = near_p[1:]

    barrier = pltpu.get_barrier_semaphore()
    greet = [{"tile": nxt}, {"tile": prv}, {"tile": nxt, "level": other}, {"tile": prv, "level": other}]
    greet += a_peers + b_peers
    for dev in greet:
        pl.semaphore_signal(barrier, inc=1, device_id=dev, device_id_type=MESH)

    sub = lax.broadcasted_iota(jnp.int32, (8, Y), 0)
    lane_h = lax.broadcasted_iota(jnp.int32, (8, 128), 1)
    sub_h = lax.broadcasted_iota(jnp.int32, (8, 128), 0)
    has_next = (tile < tiles - 1).astype(F32)
    has_prev = (tile > 0).astype(F32)
    mask_h = jnp.where(sub < 2, has_next, jnp.where(sub >= 6, has_prev, 0.0))
    zero = jnp.zeros((8, Y), F32)

    def src(l):
        return half * (L - 1) + (1 - 2 * half) * l

    def send(src_ref, dst_ref, ssem, rsem, dev):
        copy = pltpu.make_async_remote_copy(
            src_ref=src_ref, dst_ref=dst_ref, send_sem=ssem, recv_sem=rsem,
            device_id=dev, device_id_type=MESH)
        copy.start()
        return copy

    started = []
    counter = [0]

    def post(src_ref, dst_ref, dev):
        n = counter[0]
        counter[0] += 1
        copy = send(src_ref, dst_ref, send_sem.at[n], recv_sem.at[n], dev)
        started.append(copy)
        return copy

    def loop(n, chunk, body, init=0):
        chunk = min(chunk, n)

        def step(b, carry):
            for k in range(chunk):
                carry = body(b * chunk + k, carry)
            return carry

        return lax.fori_loop(0, n // chunk, step, init)

    def each(n, chunk, body):
        def step(l, carry):
            body(l)
            return carry
        loop(n, chunk, step)

    def pack_rows(rows, g, up_ref, dn_ref):
        up = rows[3]
        dn = pltpu.roll(rows[3], 6, 0)
        for k in (2, 1, 0):
            up = jnp.where(sub < 2 * k + 2, pltpu.roll(rows[k], 2 * k + 2, 0), up)
            dn = jnp.where(sub < 2 * k + 2, pltpu.roll(rows[k], 2 * k, 0) if k else rows[k], dn)
        up_ref[g] = up
        dn_ref[g] = dn

    def pack(put, up_ref, dn_ref):
        each(L // 4, 2, lambda g: pack_rows([put(4 * g + k) for k in range(4)], g, up_ref, dn_ref))

    def unpack(a_ref, b_ref, write):
        def body(g):
            a = a_ref[g]
            b = b_ref[g]
            for k in range(4):
                ra = pltpu.roll(a, 6 - 2 * k, 0) if k < 3 else a
                rb = pltpu.roll(b, 8 - 2 * k, 0) if k else b
                write(4 * g + k, jnp.where(sub >= 4, ra, rb))
        each(L // 4, 2, body)

    first_lane = lane_h == 0
    last_lane = lane_h == 127

    def sides(a):
        parts = [a[:, n * 128:(n + 1) * 128] for n in range(Y // 128)]
        right = [pltpu.roll(x, 1, 1) for x in parts]
        left = [pltpu.roll(x, 127, 1) for x in parts]
        out = []
        for n in range(len(parts)):
            before = jnp.where(first_lane, right[n - 1] if n else 0.0, right[n])
            after = jnp.where(last_lane, left[n + 1] if n + 1 < len(parts) else 0.0, left[n])
            out.append(before + after)
        return jnp.concatenate(out, axis=1)

    def beside(a, b):
        up = jnp.where(sub == 0, pltpu.roll(b, 1, 0), pltpu.roll(a, 1, 0))
        dn = jnp.where(sub == 7, pltpu.roll(b, 7, 0), pltpu.roll(a, 7, 0))
        return (up + dn) + sides(a)

    def factor(d_ref, m_ref, hg_ref):
        m_ref[0] = zero

        def up(l, m):
            m = 2.0 / (d_ref[l] - 2.0 * m)
            m_ref[l + 1] = m
            return m
        last = loop(L, 8, up, zero)

        def down(k, h):
            l = L - 1 - k
            h = m_ref[l + 1] * h
            hg_ref[l] = h
            return h
        loop(L, 8, down, zero + 1.0)

        def again(l, g):
            g = 0.5 * hg_ref[l] + m_ref[l] * g
            hg_ref[l] = g
            return g
        return last, loop(L, 8, again, zero)

    def solve(read, m_ref, f_ref, y_ref):
        def fwd(l, f):
            f = 0.5 * read(l) + m_ref[l] * f
            f_ref[l] = f
            return f
        first = loop(L, 16, fwd, zero)

        def back(k, y):
            l = L - 1 - k
            y = m_ref[l + 1] * (f_ref[l] + y)
            y_ref[l] = y
            return y
        loop(L, 16, back, zero)
        return first

    def passes(read, m_ref, f_ref):
        first = solve(read, m_ref, f_ref, y_f)

        def again(l, g):
            g = 0.5 * y_f[l] + m_ref[l] * g
            f_ref[l] = g
            return g
        return first, loop(L, 16, again, zero)

    def edges(a, b):
        inside = jnp.where(sub < 4, pltpu.roll(b, 2, 0), pltpu.roll(b, 6, 0))
        return jnp.where((sub >= 2) & (sub < 6), inside, a)

    def beyond(a, b):
        return jnp.where(sub >= 4, a, b), jnp.where(sub >= 4, pltpu.roll(a, 2, 0), pltpu.roll(b, 6, 0))

    def join(const, own, far):
        mo, ho, mp, hp, inv = const
        (fo, go), (fp, gp) = own, far
        x = mo * (fo + mp * fp) * inv
        xi = mp * (fp + mo * fo) * inv
        g = go + xi * ho
        gf = gp + x * hp
        w = mo * (g + mp * gf) * inv
        eta = mp * (gf + mo * g) * inv
        return xi, w, eta

    def finish_m(j, const, own, far, dp):
        xi, w, eta = join(const, own, far)
        next_one = 0.5 * (dp * eta - xi) - w
        v_m[j, L + 1] = eta if j == 0 else eta - v_m[j - 1, L + 1]
        v_m[j, L + 2] = next_one if j == 0 else next_one - v_m[j - 1, L + 2]

        def down(k, w):
            l = L - 1 - k
            w = m_m[l + 1] * ((f_m[l] + xi * hg_m[l]) + w)
            v_m[j, l + 1] = w if j == 0 else w - v_m[j - 1, l + 1]
            return w
        loop(L, 16, down, eta)

    def finish_h(j, const, own, far):
        xi, w, eta = join(const, own, far)
        v_h[L + 1] = eta if j == 0 else eta - v_h[L + 1]

        def down(k, w):
            l = L - 1 - k
            w = m_h[l + 1] * ((f_h[l] + xi * hg_h[l]) + w)
            v_h[l + 1] = w if j == 0 else w - v_h[l + 1]
            return w
        loop(L, 16, down, eta)

    def inner_k(j):
        def body(l):
            a = v_m[j, l + 1]
            rows = jnp.where(sub == 0, 0.0, pltpu.roll(a, 1, 0)) + jnp.where(sub == 7, 0.0, pltpu.roll(a, 7, 0))
            u_m[j, l + 1] = (d_m[l] * a - (rows + sides(a))) - 2.0 * (v_m[j, l] + v_m[j, l + 2])
        each(L, 8, body)
        if j < STEPS - 1:
            body(L)

    def outer_k(j):
        def fix(l, b):
            add = jnp.where(sub == 0, pltpu.roll(b, 1, 0), jnp.where(sub == 7, pltpu.roll(b, 7, 0), 0.0))
            u_m[j, l + 1] = u_m[j, l + 1] - add

        def body(l):
            b = v_h[l + 1]
            fix(l, b)
            if j < STEPS - 1:
                u = (d_h[l] * b - beside(b, v_m[j, l + 1])) - 2.0 * (v_h[l] + v_h[l + 2])
                u_h[l] = mask_h * u
        each(L, 8, body)
        if j < STEPS - 1:
            fix(L, v_h[L + 1])

    def again_k(j, l):
        a = u_m[j, l + 1]
        r = (d_m[l] * a - beside(a, u_h[l])) - 2.0 * (u_m[j, l] + u_m[j, l + 2])
        r_m[l] = r
        return r

    def fold(acc):
        row = jnp.sum(acc, axis=0, keepdims=True)
        total = row[:, :128]
        for n in range(1, Y // 128):
            total = total + row[:, n * 128:(n + 1) * 128]
        return total

    def dots(j):
        def body(l, carry):
            u = u_m[j, l + 1]
            out = [carry[0] + v_m[j, l + 1] * s_m[l + 1]]
            for i in range(j + 1):
                out.append(carry[i + 1] + u * u_m[i, l + 1])
            return tuple(out)
        sums = loop(L, 8, body, (zero,) * (j + 2))
        gram[len(PAIRS) + j:len(PAIRS) + j + 1] = fold(sums[0])
        for i in range(j + 1):
            n = ROW[i, j]
            gram[n:n + 1] = fold(sums[i + 1])

    low = lane_h < 64

    def quarter(q, top, bot):
        n = q // 2
        p, b = top[:, n * 128:(n + 1) * 128], bot[:, n * 128:(n + 1) * 128]
        if q % 2 == 0:
            return jnp.where(low, p, pltpu.roll(b, 64, 1))
        return jnp.where(low, pltpu.roll(p, 64, 1), b)

    def fill_t(j):
        def body(l):
            top = v_m[j, l + 1] * ks[l] + u_m[j, l + 1] * s_m[l + 1]
            k = l + H
            bot = v_m[j, k + 1] * ks[k] + u_m[j, k + 1] * s_m[k + 1]
            for q in range(probes):
                t_out[j, q, l] = quarter(q, top, bot)
            t_in[j, probe, l] = t_out[j, probe, l]
        each(H, 2, body)

    trace_parts = []

    def send_t(j):
        for g in p_peers:
            trace_parts.append(post(t_out.at[j, g], t_in.at[j, probe], {"probe": g}))

    loads[0].wait()

    def put_d(l):
        d = kap_v[src(l)] + 8.0
        d_m[l] = d
        return d
    pack(put_d, halo_out.at[0, 0], halo_out.at[0, 1])
    pl.semaphore_wait(barrier, len(greet))
    halo_d = [
        post(halo_out.at[0, 0], halo_in.at[0, 0], {"tile": nxt}),
        post(halo_out.at[0, 1], halo_in.at[0, 1], {"tile": prv}),
    ]
    mo_m, ho_m = factor(d_m, m_m, hg_m)
    loads[1].wait()

    def put_s(l):
        s = (2 * bits_v[src(l)] - 1).astype(F32)
        s_m[l + 1] = s
        return s
    pack(put_s, halo_out.at[1, 0], halo_out.at[1, 1])
    own_m = passes(lambda l: s_m[l + 1], m_m, f_m)
    loads[2].wait()
    side_out[0] = edges(mo_m, ho_m)
    side_out[1] = edges(own_m[0], own_m[1])
    for n, plane in enumerate((mo_m, ho_m, own_m[0], own_m[1], d_m[L - 1], s_m[L], obs_v[src(L - 1)])):
        first_out[n] = plane
    far = [
        post(side_out, side_in.at[0], {"tile": nxt, "level": other}),
        post(side_out, side_in.at[1], {"tile": prv, "level": other}),
        post(first_out, first_in, {"level": other}),
    ]
    halo_s = [
        post(halo_out.at[1, 0], halo_in.at[1, 0], {"tile": nxt}),
        post(halo_out.at[1, 1], halo_in.at[1, 1], {"tile": prv}),
    ]
    s_m[0] = zero
    o_m[0] = zero
    for j in range(STEPS):
        v_m[j, 0] = zero
        u_m[j, 0] = zero
    v_h[0] = zero

    def put_o(l):
        o = obs_v[src(l)]
        o_m[l + 1] = o
        return o
    pack(put_o, halo_out.at[2, 0], halo_out.at[2, 1])
    halo_o = [
        post(halo_out.at[2, 0], halo_in.at[2, 0], {"tile": nxt}),
        post(halo_out.at[2, 1], halo_in.at[2, 1], {"tile": prv}),
    ]

    def weigh(k, x):
        l = L - 1 - k
        al_m[l] = x
        return m_m[l] * x
    loop(L, 16, weigh, zero + 0.5)
    solve(lambda l: al_m[l], m_m, r_m, be_m)

    for copy in halo_d:
        copy.wait_recv()

    def put_dh(l, x):
        d_h[l] = jnp.where(mask_h > 0.0, x, 8.0)
    unpack(halo_in.at[0, 0], halo_in.at[0, 1], put_dh)
    mo_h, ho_h = factor(d_h, m_h, hg_h)

    far[2].wait_recv()
    mp_m, hp_m, fp_m, gp_m, dp_m = (first_in[n] for n in range(5))
    d_m[L] = dp_m
    s_m[L + 1] = first_in[5]
    o_m[L + 1] = first_in[6]
    const_m = (mo_m, ho_m, mp_m, hp_m, 1.0 / (1.0 - mo_m * mp_m))
    finish_m(0, const_m, own_m, (fp_m, gp_m), dp_m)
    inner_k(0)

    for copy in halo_s:
        copy.wait_recv()

    def put_sh(l, x):
        s_h[l] = x * mask_h
    unpack(halo_in.at[1, 0], halo_in.at[1, 1], put_sh)
    own_h = passes(lambda l: s_h[l], m_h, f_h)
    for copy in far[:2]:
        copy.wait_recv()

    mp_h, hp_h = beyond(side_in[0, 0], side_in[1, 0])
    fp_h, gp_h = beyond(side_in[0, 1], side_in[1, 1])
    const_h = (mo_h, ho_h, mp_h, hp_h, 1.0 / (1.0 - mo_h * mp_h))
    finish_h(0, const_h, own_h, (mask_h * fp_h, mask_h * gp_h))
    outer_k(0)

    odd = lax.rem(probe, 2) == 1
    upper = probe // 2 == 1

    def mine(top, bot):
        out = [jnp.where(odd, quarter(2 * n + 1, top, bot), quarter(2 * n, top, bot)) for n in range(Y // 128)]
        return jnp.where(upper, out[1], out[0])

    def side_terms():
        for copy in halo_o:
            copy.wait_recv()

        def put_oh(l, x):
            o_h[l] = x * mask_h
        unpack(halo_in.at[2, 0], halo_in.at[2, 1], put_oh)

        def body(l):
            a = s_m[l + 1]
            ks[l] = (d_m[l] * a - beside(a, s_h[l])) - 2.0 * (s_m[l] + s_m[l + 2])
            b = o_m[l + 1]
            ko = (d_m[l] * b - beside(b, o_h[l])) - 2.0 * (o_m[l] + o_m[l + 2])
            data[l] = kap_v[src(l)] * (2.0 * b * ko)
        each(L, 4, body)

    def quarters():
        def body(l):
            kap_q[l] = mine(kap_v[src(l)], kap_v[src(l + H)]) * (1.0 / probes)
            sub_q[l] = mine(data[l], data[l + H])
        each(H, 2, body)

    for j in range(1, STEPS):
        n = j - 1

        def form(g, carry):
            fo, go = carry
            tiles_r = []
            for k in range(4):
                l = 4 * g + k
                r = again_k(j - 1, l)
                fo = fo + al_m[l] * r
                go = go + be_m[l] * r
                tiles_r.append(r)
            pack_rows(tiles_r, g, xs_out.at[n, 0], xs_out.at[n, 1])
            return fo, go
        own_m = loop(L // 4, 2, form, (zero, zero))
        ed_out[n] = edges(own_m[0], own_m[1])
        pl_out[n, 0] = own_m[0]
        pl_out[n, 1] = own_m[1]
        planes = [
            post(ed_out.at[n], ed_in.at[n, 0], {"tile": nxt, "level": other}),
            post(ed_out.at[n], ed_in.at[n, 1], {"tile": prv, "level": other}),
            post(pl_out.at[n], pl_in.at[n], {"level": other}),
        ]
        rows = [
            post(xs_out.at[n, 0], xs_in.at[n, 0], {"tile": nxt}),
            post(xs_out.at[n, 1], xs_in.at[n, 1], {"tile": prv}),
        ]
        passes(lambda l: r_m[l], m_m, f_m)
        dots(j - 1)
        if j == 1:
            side_terms()
        if j == 2:
            quarters()
        fill_t(j - 1)
        planes[2].wait_recv()
        finish_m(j, const_m, own_m, (pl_in[n, 0], pl_in[n, 1]), dp_m)
        inner_k(j)
        for copy in rows:
            copy.wait_recv()

        def put_rh(l, x):
            r_h[l] = x * mask_h
        unpack(xs_in.at[n, 0], xs_in.at[n, 1], put_rh)
        own_h = passes(lambda l: r_h[l], m_h, f_h)
        for copy in planes[:2]:
            copy.wait_recv()
        send_t(j - 1)
        fp_h, gp_h = beyond(ed_in[n, 0], ed_in[n, 1])
        finish_h(j, const_h, own_h, (mask_h * fp_h, mask_h * gp_h))
        outer_k(j)
    for n in range(len(PAIRS) + STEPS, N_ROWS):
        gram[n:n + 1] = jnp.zeros((1, 128), F32)
    dots(STEPS - 1)

    wide = lax.broadcasted_iota(jnp.int32, (N_ROWS, 128), 1) == lax.broadcasted_iota(jnp.int32, (N_ROWS, 128), 0)
    each_sum = jnp.sum(gram[...], axis=1, keepdims=True)
    packed = jnp.sum(jnp.where(wide, each_sum, 0.0), axis=0, keepdims=True)
    red_out[...] = packed
    red_a[spot] = packed
    plane = [post(red_out, red_a.at[spot], dev) for dev in a_peers]
    fill_t(STEPS - 1)
    send_t(STEPS - 1)
    for copy in plane:
        copy.wait_recv()
    for p in range(probes):
        base = p * levels * x_chips
        part = red_a[base]
        for k in range(1, levels * x_chips):
            part = part + red_a[base + k]
        red_b[zc, p] = part
    before = list(started)
    line = [post(red_b.at[zc], red_b.at[zc], dev) for dev in b_peers]
    for copy in before:
        copy.wait_send()
    for copy in line:
        copy.wait_recv()
    total = None
    for p in range(probes):
        part = red_b[0, p]
        for k in range(1, z_chips):
            part = part + red_b[k, p]
        part = jnp.broadcast_to(part, (8, 128))
        total = part if p == 0 else jnp.where(sub_h == p, part, total)

    def column(n):
        return jnp.broadcast_to(total[:, n:n + 1], (8, 128))
    a = {pair: column(n) for pair, n in ROW.items()}
    c = [column(len(PAIRS) + j) for j in range(STEPS)]
    pivot = []
    ratio = {}
    for j in range(STEPS):
        pivot.append(1.0 / a[j, j])
        for i in range(j + 1, STEPS):
            ratio[j, i] = a[j, i] * pivot[j]
        for i in range(j + 1, STEPS):
            c[i] = c[i] - ratio[j, i] * c[j]
            for k in range(i, STEPS):
                a[i, k] = a[i, k] - ratio[j, i] * a[j, k]
    for j in range(STEPS - 1, -1, -1):
        c[j] = c[j] * pivot[j]
        for i in range(j + 1, STEPS):
            c[j] = c[j] - ratio[j, i] * c[i]
    weight = {(p, j): jnp.broadcast_to(c[j][p:p + 1], (8, 128)) for p in range(probes) for j in range(STEPS)}

    for copy in trace_parts:
        copy.wait_recv()

    def write(l):
        acc = None
        for j in range(STEPS):
            for p in range(probes):
                part = weight[p, j] * t_in[j, p, l]
                acc = part if acc is None else acc + part
        res = kap_q[l] * acc - sub_q[l]
        out_ref[src(l)] = res[:, :64]
        out_ref[src(l + H)] = pltpu.roll(res, 64, 1)[:, :64]
    each(H, 4, write)
    for copy in line:
        copy.wait_send()


def solution(mesh):
    probes, tiles, levels = (mesh.shape[a] for a in ("probe", "tile", "level"))
    x_chips = min(X_CHIPS, tiles)
    z_chips = tiles // x_chips

    def step(bits, kap, obs):
        _, L, rows, Y = bits.shape
        dims = (probes, tiles, levels, x_chips, L, Y)
        vm = lambda *lead: pltpu.VMEM((*lead, 8, Y), F32)
        dma = lambda n: pltpu.SemaphoreType.DMA((n,))
        G = L // 4
        n_sems = 9 + 5 * (STEPS - 1) + (probes * levels * x_chips - 1) + (z_chips - 1) + STEPS * (probes - 1)
        part = lambda *lead: pltpu.VMEM((*lead, L // 2, 8, 128), F32)
        scratch = [
            pltpu.VMEM((L, 8, Y), jnp.int32), vm(L), vm(L),
            vm(L + 2), vm(L), vm(L + 1), vm(L), vm(L + 2), vm(L),
            vm(L + 1), vm(L + 1), vm(L), vm(L), vm(L), vm(L),
            vm(STEPS, L + 3), vm(L + 2), vm(STEPS, L + 2), vm(L), vm(L), vm(L), vm(L), vm(L), vm(L), vm(L),
            vm(3, 2, G), vm(3, 2, G), vm(STEPS - 1, 2, G), vm(STEPS - 1, 2, G),
            vm(7), vm(7), vm(2), vm(2, 2),
            vm(STEPS - 1, 2), vm(STEPS - 1, 2), vm(STEPS - 1), vm(STEPS - 1, 2),
            pltpu.VMEM((N_ROWS, 128), F32),
            pltpu.VMEM((1, 128), F32),
            pltpu.VMEM((probes * levels * x_chips, 1, 128), F32),
            pltpu.VMEM((z_chips, probes, 1, 128), F32),
            part(STEPS, probes), part(STEPS, probes), part(), part(), vm(L),
            dma(3), dma(n_sems), dma(n_sems),
        ]
        return pl.pallas_call(
            functools.partial(kernel, dims),
            out_shape=jax.ShapeDtypeStruct((L, rows, Y // probes), F32),
            in_specs=[pl.BlockSpec(memory_space=pl.ANY)] * 3,
            out_specs=pl.BlockSpec(memory_space=pltpu.VMEM),
            scratch_shapes=scratch,
            compiler_params=pltpu.CompilerParams(collective_id=0, has_side_effects=True),
        )(bits, kap, obs)

    return jax.shard_map(
        step,
        mesh=mesh,
        in_specs=(P("probe", "level", "tile", None), P("level", "tile", None), P("level", "tile", None)),
        out_specs=P("level", "tile", "probe"),
        check_vma=False,
    )
```

```python
import functools

import jax
import jax.numpy as jnp
from jax import lax
from jax.experimental import pallas as pl
from jax.experimental.pallas import tpu as pltpu
from jax.sharding import PartitionSpec as P

MESH = pl.DeviceIdType.MESH
STEPS = 4
F32 = jnp.float32
X_CHIPS = 4

PAIRS = [(i, j) for j in range(STEPS) for i in range(j + 1)]
ROW = {pair: n for n, pair in enumerate(PAIRS)}
N_ROWS = 16


def kernel(
    dims,
    bits_hbm, kap_hbm, obs_hbm, out_ref,
    bits_v, kap_v, obs_v,
    s_m, s_h, d_m, d_h, o_m, o_h,
    m_m, m_h, hg_m, hg_h, al_m, be_m,
    v_m, v_h, u_m, u_h, r_m, r_h, f_m, f_h, y_f, ks,
    halo_out, halo_in, xs_out, xs_in,
    first_out, first_in, side_out, side_in, pl_out, pl_in, ed_out, ed_in,
    gram, red_out, red_a, red_b, t_out, t_in, kap_q, sub_q, data,
    in_sem, send_sem, recv_sem, here_sem,
):
    probes, tiles, levels, x_chips, L, Y = dims
    z_chips = tiles // x_chips
    H = L // 2
    probe = lax.axis_index("probe")
    tile = lax.axis_index("tile")
    half = lax.axis_index("level")
    zc = tile // x_chips
    xc = tile - zc * x_chips
    nxt = lax.rem(tile + 1, tiles)
    prv = lax.rem(tile + tiles - 1, tiles)
    other = 1 - half
    n_a = probes * levels * x_chips
    spot = (probe * levels + half) * x_chips + xc

    loads = [
        pltpu.make_async_copy(kap_hbm, kap_v, in_sem.at[0]),
        pltpu.make_async_copy(bits_hbm.at[0], bits_v, in_sem.at[1]),
        pltpu.make_async_copy(obs_hbm, obs_v, in_sem.at[2]),
    ]
    for copy in loads:
        copy.start()

    def around(n):
        return sorted(range(1, n), key=lambda k: (-min(k, n - k), k))

    near_p = [lax.rem(probe + k, probes) for k in around(probes)]
    near_x = [tile - xc + lax.rem(xc + k, x_chips) for k in around(x_chips)]
    a_peers = [{"probe": p, "tile": t, "level": h}
               for t in near_x + [tile] for h in (other, half) for p in near_p + [probe]][:-1]
    b_peers = [{"tile": lax.rem(tile + k * x_chips, tiles)} for k in around(z_chips)]
    p_peers = near_p
    z_beside = [{"tile": lax.rem(tile + x_chips, tiles)}, {"tile": lax.rem(tile + tiles - x_chips, tiles)}]
    if z_chips == 1:
        z_beside = []

    barrier = pltpu.get_barrier_semaphore()
    greet = [{"tile": nxt}, {"tile": prv}, {"level": other},
             {"tile": nxt, "level": other}, {"tile": prv, "level": other}]
    greet += [{"probe": p} for p in p_peers] + z_beside
    for dev in greet:
        pl.semaphore_signal(barrier, inc=1, device_id=dev, device_id_type=MESH)

    sub = lax.broadcasted_iota(jnp.int32, (8, Y), 0)
    lane_h = lax.broadcasted_iota(jnp.int32, (8, 128), 1)
    sub_h = lax.broadcasted_iota(jnp.int32, (8, 128), 0)
    has_next = (tile < tiles - 1).astype(F32)
    has_prev = (tile > 0).astype(F32)
    mask_h = jnp.where(sub < 2, has_next, jnp.where(sub >= 6, has_prev, 0.0))
    zero = jnp.zeros((8, Y), F32)

    def src(l):
        return half * (L - 1) + (1 - 2 * half) * l

    def send(src_ref, dst_ref, ssem, rsem, dev):
        copy = pltpu.make_async_remote_copy(
            src_ref=src_ref, dst_ref=dst_ref, send_sem=ssem, recv_sem=rsem,
            device_id=dev, device_id_type=MESH)
        copy.start()
        return copy

    started = []
    counter = [0]

    def post(src_ref, dst_ref, dev):
        n = counter[0]
        counter[0] += 1
        copy = send(src_ref, dst_ref, send_sem.at[n], recv_sem.at[n], dev)
        started.append(copy)
        return copy

    def loop(n, chunk, body, init=0):
        chunk = min(chunk, n)

        def step(b, carry):
            for k in range(chunk):
                carry = body(b * chunk + k, carry)
            return carry

        return lax.fori_loop(0, n // chunk, step, init)

    def each(n, chunk, body):
        def step(l, carry):
            body(l)
            return carry
        loop(n, chunk, step)

    def pack_rows(rows, g, up_ref, dn_ref):
        up = rows[3]
        dn = pltpu.roll(rows[3], 6, 0)
        for k in (2, 1, 0):
            up = jnp.where(sub < 2 * k + 2, pltpu.roll(rows[k], 2 * k + 2, 0), up)
            dn = jnp.where(sub < 2 * k + 2, pltpu.roll(rows[k], 2 * k, 0) if k else rows[k], dn)
        up_ref[g] = up
        dn_ref[g] = dn

    def pack(put, up_ref, dn_ref):
        each(L // 4, 2, lambda g: pack_rows([put(4 * g + k) for k in range(4)], g, up_ref, dn_ref))

    def unpack(a_ref, b_ref, write):
        def body(g):
            a = a_ref[g]
            b = b_ref[g]
            for k in range(4):
                ra = pltpu.roll(a, 6 - 2 * k, 0) if k < 3 else a
                rb = pltpu.roll(b, 8 - 2 * k, 0) if k else b
                write(4 * g + k, jnp.where(sub >= 4, ra, rb))
        each(L // 4, 2, body)

    first_lane = lane_h == 0
    last_lane = lane_h == 127

    def sides(a):
        parts = [a[:, n * 128:(n + 1) * 128] for n in range(Y // 128)]
        right = [pltpu.roll(x, 1, 1) for x in parts]
        left = [pltpu.roll(x, 127, 1) for x in parts]
        out = []
        for n in range(len(parts)):
            before = jnp.where(first_lane, right[n - 1] if n else 0.0, right[n])
            after = jnp.where(last_lane, left[n + 1] if n + 1 < len(parts) else 0.0, left[n])
            out.append(before + after)
        return jnp.concatenate(out, axis=1)

    def beside(a, b):
        up = jnp.where(sub == 0, pltpu.roll(b, 1, 0), pltpu.roll(a, 1, 0))
        dn = jnp.where(sub == 7, pltpu.roll(b, 7, 0), pltpu.roll(a, 7, 0))
        return (up + dn) + sides(a)

    def factor(d_ref, m_ref, hg_ref):
        m_ref[0] = zero

        def up(l, m):
            m = 2.0 / (d_ref[l] - 2.0 * m)
            m_ref[l + 1] = m
            return m
        last = loop(L, 8, up, zero)

        def down(k, h):
            l = L - 1 - k
            h = m_ref[l + 1] * h
            hg_ref[l] = h
            return h
        loop(L, 8, down, zero + 1.0)

        def again(l, g):
            g = 0.5 * hg_ref[l] + m_ref[l] * g
            hg_ref[l] = g
            return g
        return last, loop(L, 8, again, zero)

    def solve(read, m_ref, f_ref, y_ref):
        def fwd(l, f):
            f = 0.5 * read(l) + m_ref[l] * f
            f_ref[l] = f
            return f
        first = loop(L, 16, fwd, zero)

        def back(k, y):
            l = L - 1 - k
            y = m_ref[l + 1] * (f_ref[l] + y)
            y_ref[l] = y
            return y
        loop(L, 16, back, zero)
        return first

    def passes(read, m_ref, f_ref):
        first = solve(read, m_ref, f_ref, y_f)

        def again(l, g):
            g = 0.5 * y_f[l] + m_ref[l] * g
            f_ref[l] = g
            return g
        return first, loop(L, 16, again, zero)

    def edges(a, b):
        inside = jnp.where(sub < 4, pltpu.roll(b, 2, 0), pltpu.roll(b, 6, 0))
        return jnp.where((sub >= 2) & (sub < 6), inside, a)

    def beyond(a, b):
        return jnp.where(sub >= 4, a, b), jnp.where(sub >= 4, pltpu.roll(a, 2, 0), pltpu.roll(b, 6, 0))

    def join(const, own, far):
        mo, ho, mp, hp, inv = const
        (fo, go), (fp, gp) = own, far
        x = mo * (fo + mp * fp) * inv
        xi = mp * (fp + mo * fo) * inv
        g = go + xi * ho
        gf = gp + x * hp
        w = mo * (g + mp * gf) * inv
        eta = mp * (gf + mo * g) * inv
        return xi, w, eta

    def finish_m(j, const, own, far, dp):
        xi, w, eta = join(const, own, far)
        next_one = 0.5 * (dp * eta - xi) - w
        v_m[j, L + 1] = eta if j == 0 else eta - v_m[j - 1, L + 1]
        v_m[j, L + 2] = next_one if j == 0 else next_one - v_m[j - 1, L + 2]

        def down(k, w):
            l = L - 1 - k
            w = m_m[l + 1] * ((f_m[l] + xi * hg_m[l]) + w)
            v_m[j, l + 1] = w if j == 0 else w - v_m[j - 1, l + 1]
            return w
        loop(L, 16, down, eta)

    def finish_h(j, const, own, far):
        xi, w, eta = join(const, own, far)
        v_h[L + 1] = eta if j == 0 else eta - v_h[L + 1]

        def down(k, w):
            l = L - 1 - k
            w = m_h[l + 1] * ((f_h[l] + xi * hg_h[l]) + w)
            v_h[l + 1] = w if j == 0 else w - v_h[l + 1]
            return w
        loop(L, 16, down, eta)

    def inner_k(j):
        def body(l):
            a = v_m[j, l + 1]
            rows = jnp.where(sub == 0, 0.0, pltpu.roll(a, 1, 0)) + jnp.where(sub == 7, 0.0, pltpu.roll(a, 7, 0))
            u_m[j, l + 1] = (d_m[l] * a - (rows + sides(a))) - 2.0 * (v_m[j, l] + v_m[j, l + 2])
        each(L, 8, body)
        if j < STEPS - 1:
            body(L)

    def outer_k(j):
        def fix(l, b):
            add = jnp.where(sub == 0, pltpu.roll(b, 1, 0), jnp.where(sub == 7, pltpu.roll(b, 7, 0), 0.0))
            u_m[j, l + 1] = u_m[j, l + 1] - add

        def body(l):
            b = v_h[l + 1]
            fix(l, b)
            if j < STEPS - 1:
                u = (d_h[l] * b - beside(b, v_m[j, l + 1])) - 2.0 * (v_h[l] + v_h[l + 2])
                u_h[l] = mask_h * u
        each(L, 8, body)
        if j < STEPS - 1:
            fix(L, v_h[L + 1])

    def again_k(j, l):
        a = u_m[j, l + 1]
        r = (d_m[l] * a - beside(a, u_h[l])) - 2.0 * (u_m[j, l] + u_m[j, l + 2])
        r_m[l] = r
        return r

    def fold(acc):
        row = jnp.sum(acc, axis=0, keepdims=True)
        total = row[:, :128]
        for n in range(1, Y // 128):
            total = total + row[:, n * 128:(n + 1) * 128]
        return total

    def dots(j):
        def body(l, carry):
            u = u_m[j, l + 1]
            out = [carry[0] + v_m[j, l + 1] * s_m[l + 1]]
            for i in range(j + 1):
                out.append(carry[i + 1] + u * u_m[i, l + 1])
            return tuple(out)
        sums = loop(L, 8, body, (zero,) * (j + 2))
        gram[len(PAIRS) + j:len(PAIRS) + j + 1] = fold(sums[0])
        for i in range(j + 1):
            n = ROW[i, j]
            gram[n:n + 1] = fold(sums[i + 1])

    low = lane_h < 64

    def quarter(q, top, bot):
        n = q // 2
        p, b = top[:, n * 128:(n + 1) * 128], bot[:, n * 128:(n + 1) * 128]
        if q % 2 == 0:
            return jnp.where(low, p, pltpu.roll(b, 64, 1))
        return jnp.where(low, pltpu.roll(p, 64, 1), b)

    def fill_t(j):
        def body(l):
            top = v_m[j, l + 1] * ks[l] + u_m[j, l + 1] * s_m[l + 1]
            k = l + H
            bot = v_m[j, k + 1] * ks[k] + u_m[j, k + 1] * s_m[k + 1]
            for q in range(probes):
                t_out[j, q, l] = quarter(q, top, bot)
            t_in[j, probe, l] = t_out[j, probe, l]
        each(H, 2, body)

    trace_parts = []

    def send_t(j):
        for g in p_peers:
            trace_parts.append(post(t_out.at[j, g], t_in.at[j, probe], {"probe": g}))

    loads[0].wait()

    def put_d(l):
        d = kap_v[src(l)] + 8.0
        d_m[l] = d
        return d
    pack(put_d, halo_out.at[0, 0], halo_out.at[0, 1])
    pl.semaphore_wait(barrier, len(greet))
    halo_d = [
        post(halo_out.at[0, 0], halo_in.at[0, 0], {"tile": nxt}),
        post(halo_out.at[0, 1], halo_in.at[0, 1], {"tile": prv}),
    ]
    mo_m, ho_m = factor(d_m, m_m, hg_m)
    loads[1].wait()

    def put_s(l):
        s = (2 * bits_v[src(l)] - 1).astype(F32)
        s_m[l + 1] = s
        return s
    pack(put_s, halo_out.at[1, 0], halo_out.at[1, 1])
    own_m = passes(lambda l: s_m[l + 1], m_m, f_m)
    loads[2].wait()
    side_out[0] = edges(mo_m, ho_m)
    side_out[1] = edges(own_m[0], own_m[1])
    for n, plane in enumerate((mo_m, ho_m, own_m[0], own_m[1], d_m[L - 1], s_m[L], obs_v[src(L - 1)])):
        first_out[n] = plane
    far = [
        post(side_out, side_in.at[0], {"tile": nxt, "level": other}),
        post(side_out, side_in.at[1], {"tile": prv, "level": other}),
        post(first_out, first_in, {"level": other}),
    ]
    halo_s = [
        post(halo_out.at[1, 0], halo_in.at[1, 0], {"tile": nxt}),
        post(halo_out.at[1, 1], halo_in.at[1, 1], {"tile": prv}),
    ]
    s_m[0] = zero
    o_m[0] = zero
    for j in range(STEPS):
        v_m[j, 0] = zero
        u_m[j, 0] = zero
    v_h[0] = zero

    def put_o(l):
        o = obs_v[src(l)]
        o_m[l + 1] = o
        return o
    pack(put_o, halo_out.at[2, 0], halo_out.at[2, 1])
    halo_o = [
        post(halo_out.at[2, 0], halo_in.at[2, 0], {"tile": nxt}),
        post(halo_out.at[2, 1], halo_in.at[2, 1], {"tile": prv}),
    ]

    def weigh(k, x):
        l = L - 1 - k
        al_m[l] = x
        return m_m[l] * x
    loop(L, 16, weigh, zero + 0.5)
    solve(lambda l: al_m[l], m_m, r_m, be_m)

    for copy in halo_d:
        copy.wait_recv()

    def put_dh(l, x):
        d_h[l] = jnp.where(mask_h > 0.0, x, 8.0)
    unpack(halo_in.at[0, 0], halo_in.at[0, 1], put_dh)
    mo_h, ho_h = factor(d_h, m_h, hg_h)

    far[2].wait_recv()
    mp_m, hp_m, fp_m, gp_m, dp_m = (first_in[n] for n in range(5))
    d_m[L] = dp_m
    s_m[L + 1] = first_in[5]
    o_m[L + 1] = first_in[6]
    const_m = (mo_m, ho_m, mp_m, hp_m, 1.0 / (1.0 - mo_m * mp_m))
    finish_m(0, const_m, own_m, (fp_m, gp_m), dp_m)
    inner_k(0)

    for copy in halo_s:
        copy.wait_recv()

    def put_sh(l, x):
        s_h[l] = x * mask_h
    unpack(halo_in.at[1, 0], halo_in.at[1, 1], put_sh)
    own_h = passes(lambda l: s_h[l], m_h, f_h)
    for copy in far[:2]:
        copy.wait_recv()

    mp_h, hp_h = beyond(side_in[0, 0], side_in[1, 0])
    fp_h, gp_h = beyond(side_in[0, 1], side_in[1, 1])
    const_h = (mo_h, ho_h, mp_h, hp_h, 1.0 / (1.0 - mo_h * mp_h))
    finish_h(0, const_h, own_h, (mask_h * fp_h, mask_h * gp_h))
    outer_k(0)

    odd = lax.rem(probe, 2) == 1
    upper = probe // 2 == 1

    def mine(top, bot):
        out = [jnp.where(odd, quarter(2 * n + 1, top, bot), quarter(2 * n, top, bot)) for n in range(Y // 128)]
        return jnp.where(upper, out[1], out[0])

    def side_terms():
        for copy in halo_o:
            copy.wait_recv()

        def put_oh(l, x):
            o_h[l] = x * mask_h
        unpack(halo_in.at[2, 0], halo_in.at[2, 1], put_oh)

        def body(l):
            a = s_m[l + 1]
            ks[l] = (d_m[l] * a - beside(a, s_h[l])) - 2.0 * (s_m[l] + s_m[l + 2])
            b = o_m[l + 1]
            ko = (d_m[l] * b - beside(b, o_h[l])) - 2.0 * (o_m[l] + o_m[l + 2])
            data[l] = kap_v[src(l)] * (2.0 * b * ko)
        each(L, 4, body)

    def quarters():
        def body(l):
            kap_q[l] = mine(kap_v[src(l)], kap_v[src(l + H)]) * (1.0 / probes)
            sub_q[l] = mine(data[l], data[l + H])
        each(H, 2, body)

    for j in range(1, STEPS):
        n = j - 1

        def form(g, carry):
            fo, go = carry
            tiles_r = []
            for k in range(4):
                l = 4 * g + k
                r = again_k(j - 1, l)
                fo = fo + al_m[l] * r
                go = go + be_m[l] * r
                tiles_r.append(r)
            pack_rows(tiles_r, g, xs_out.at[n, 0], xs_out.at[n, 1])
            return fo, go
        own_m = loop(L // 4, 2, form, (zero, zero))
        ed_out[n] = edges(own_m[0], own_m[1])
        pl_out[n, 0] = own_m[0]
        pl_out[n, 1] = own_m[1]
        planes = [
            post(ed_out.at[n], ed_in.at[n, 0], {"tile": nxt, "level": other}),
            post(ed_out.at[n], ed_in.at[n, 1], {"tile": prv, "level": other}),
            post(pl_out.at[n], pl_in.at[n], {"level": other}),
        ]
        rows = [
            post(xs_out.at[n, 0], xs_in.at[n, 0], {"tile": nxt}),
            post(xs_out.at[n, 1], xs_in.at[n, 1], {"tile": prv}),
        ]
        for dev in z_beside:
            pl.semaphore_signal(here_sem.at[n], inc=1, device_id=dev, device_id_type=MESH)
        passes(lambda l: r_m[l], m_m, f_m)
        dots(j - 1)
        if j == 1:
            side_terms()
        if j == 2:
            quarters()
        fill_t(j - 1)
        planes[2].wait_recv()
        finish_m(j, const_m, own_m, (pl_in[n, 0], pl_in[n, 1]), dp_m)
        inner_k(j)
        for copy in rows:
            copy.wait_recv()

        def put_rh(l, x):
            r_h[l] = x * mask_h
        unpack(xs_in.at[n, 0], xs_in.at[n, 1], put_rh)
        own_h = passes(lambda l: r_h[l], m_h, f_h)
        for copy in planes[:2]:
            copy.wait_recv()
        if z_beside:
            pl.semaphore_wait(here_sem.at[n], len(z_beside))
        send_t(j - 1)
        fp_h, gp_h = beyond(ed_in[n, 0], ed_in[n, 1])
        finish_h(j, const_h, own_h, (mask_h * fp_h, mask_h * gp_h))
        outer_k(j)
    for n in range(len(PAIRS) + STEPS, N_ROWS):
        gram[n:n + 1] = jnp.zeros((1, 128), F32)
    dots(STEPS - 1)

    wide = lax.broadcasted_iota(jnp.int32, (N_ROWS, 128), 1) == lax.broadcasted_iota(jnp.int32, (N_ROWS, 128), 0)
    each_sum = jnp.sum(gram[...], axis=1, keepdims=True)
    packed = jnp.sum(jnp.where(wide, each_sum, 0.0), axis=0, keepdims=True)
    for copy in trace_parts[:probes - 1]:
        copy.wait_recv()
    red_out[...] = packed
    red_a[spot] = packed
    plane = [post(red_out, red_a.at[spot], dev) for dev in a_peers]
    fill_t(STEPS - 1)
    send_t(STEPS - 1)
    for copy in plane:
        copy.wait_recv()
    for p in range(probes):
        base = p * levels * x_chips
        part = red_a[base]
        for k in range(1, levels * x_chips):
            part = part + red_a[base + k]
        red_b[zc, p] = part
    before = list(started)
    line = [post(red_b.at[zc], red_b.at[zc], dev) for dev in b_peers]
    for copy in before:
        copy.wait_send()
    for copy in line:
        copy.wait_recv()
    total = None
    for p in range(probes):
        part = red_b[0, p]
        for k in range(1, z_chips):
            part = part + red_b[k, p]
        part = jnp.broadcast_to(part, (8, 128))
        total = part if p == 0 else jnp.where(sub_h == p, part, total)

    def column(n):
        return jnp.broadcast_to(total[:, n:n + 1], (8, 128))
    a = {pair: column(n) for pair, n in ROW.items()}
    c = [column(len(PAIRS) + j) for j in range(STEPS)]
    pivot = []
    ratio = {}
    for j in range(STEPS):
        pivot.append(1.0 / a[j, j])
        for i in range(j + 1, STEPS):
            ratio[j, i] = a[j, i] * pivot[j]
        for i in range(j + 1, STEPS):
            c[i] = c[i] - ratio[j, i] * c[j]
            for k in range(i, STEPS):
                a[i, k] = a[i, k] - ratio[j, i] * a[j, k]
    for j in range(STEPS - 1, -1, -1):
        c[j] = c[j] * pivot[j]
        for i in range(j + 1, STEPS):
            c[j] = c[j] - ratio[j, i] * c[i]
    weight = {(p, j): jnp.broadcast_to(c[j][p:p + 1], (8, 128)) for p in range(probes) for j in range(STEPS)}

    for copy in trace_parts[probes - 1:]:
        copy.wait_recv()

    def write(l):
        acc = None
        for j in range(STEPS):
            for p in range(probes):
                part = weight[p, j] * t_in[j, p, l]
                acc = part if acc is None else acc + part
        res = kap_q[l] * acc - sub_q[l]
        out_ref[src(l)] = res[:, :64]
        out_ref[src(l + H)] = pltpu.roll(res, 64, 1)[:, :64]
    each(H, 4, write)
    for copy in line:
        copy.wait_send()


def solution(mesh):
    probes, tiles, levels = (mesh.shape[a] for a in ("probe", "tile", "level"))
    x_chips = min(X_CHIPS, tiles)
    z_chips = tiles // x_chips

    def step(bits, kap, obs):
        _, L, rows, Y = bits.shape
        dims = (probes, tiles, levels, x_chips, L, Y)
        vm = lambda *lead: pltpu.VMEM((*lead, 8, Y), F32)
        dma = lambda n: pltpu.SemaphoreType.DMA((n,))
        G = L // 4
        n_sems = 9 + 5 * (STEPS - 1) + (probes * levels * x_chips - 1) + (z_chips - 1) + STEPS * (probes - 1)
        part = lambda *lead: pltpu.VMEM((*lead, L // 2, 8, 128), F32)
        scratch = [
            pltpu.VMEM((L, 8, Y), jnp.int32), vm(L), vm(L),
            vm(L + 2), vm(L), vm(L + 1), vm(L), vm(L + 2), vm(L),
            vm(L + 1), vm(L + 1), vm(L), vm(L), vm(L), vm(L),
            vm(STEPS, L + 3), vm(L + 2), vm(STEPS, L + 2), vm(L), vm(L), vm(L), vm(L), vm(L), vm(L), vm(L),
            vm(3, 2, G), vm(3, 2, G), vm(STEPS - 1, 2, G), vm(STEPS - 1, 2, G),
            vm(7), vm(7), vm(2), vm(2, 2),
            vm(STEPS - 1, 2), vm(STEPS - 1, 2), vm(STEPS - 1), vm(STEPS - 1, 2),
            pltpu.VMEM((N_ROWS, 128), F32),
            pltpu.VMEM((1, 128), F32),
            pltpu.VMEM((probes * levels * x_chips, 1, 128), F32),
            pltpu.VMEM((z_chips, probes, 1, 128), F32),
            part(STEPS, probes), part(STEPS, probes), part(), part(), vm(L),
            dma(3), dma(n_sems), dma(n_sems), pltpu.SemaphoreType.REGULAR((STEPS - 1,)),
        ]
        return pl.pallas_call(
            functools.partial(kernel, dims),
            out_shape=pltpu.VMEM((L, rows, Y // probes), F32),
            in_specs=[pl.BlockSpec(memory_space=pl.ANY)] * 3,
            out_specs=pl.BlockSpec(memory_space=pltpu.VMEM),
            scratch_shapes=scratch,
            compiler_params=pltpu.CompilerParams(collective_id=0, has_side_effects=True),
        )(bits, kap, obs)

    return jax.shard_map(
        step,
        mesh=mesh,
        in_specs=(P("probe", "level", "tile", None), P("level", "tile", None), P("level", "tile", None)),
        out_specs=P("level", "tile", "probe"),
        check_vma=False,
    )
```

```python
import functools

import jax
import jax.numpy as jnp
from jax import lax
from jax.experimental import pallas as pl
from jax.experimental.pallas import tpu as pltpu
from jax.sharding import PartitionSpec as P

MESH = pl.DeviceIdType.MESH
STEPS = 4
F32 = jnp.float32
X_CHIPS = 4

PAIRS = [(i, j) for j in range(STEPS) for i in range(j + 1)]
ROW = {pair: n for n, pair in enumerate(PAIRS)}
N_ROWS = 16


def kernel(
    dims,
    bits_hbm, kap_hbm, obs_hbm, out_ref,
    bits_v, kap_v, obs_v,
    s_m, s_h, d_m, d_h, o_m, o_h,
    m_m, m_h, hg_m, hg_h, al_m, be_m,
    v_m, v_h, u_m, u_h, r_m, f_m, f_h, y_f, ks,
    halo_out, halo_in, xs_out, xs_in,
    first_out, first_in, side_out, side_in, pl_out, pl_in, ed_out, ed_in,
    gram, red_out, red_a, red_b, t_out, t_in, kap_q, sub_q, data,
    in_sem, send_sem, recv_sem, here_sem,
):
    probes, tiles, levels, x_chips, L, Y = dims
    z_chips = tiles // x_chips
    H = L // 2
    probe = lax.axis_index("probe")
    tile = lax.axis_index("tile")
    half = lax.axis_index("level")
    zc = tile // x_chips
    xc = tile - zc * x_chips
    nxt = lax.rem(tile + 1, tiles)
    prv = lax.rem(tile + tiles - 1, tiles)
    other = 1 - half
    n_a = probes * levels * x_chips
    spot = (probe * levels + half) * x_chips + xc

    loads = [
        pltpu.make_async_copy(kap_hbm, kap_v, in_sem.at[0]),
        pltpu.make_async_copy(bits_hbm.at[0], bits_v, in_sem.at[1]),
        pltpu.make_async_copy(obs_hbm, obs_v, in_sem.at[2]),
    ]
    for copy in loads:
        copy.start()

    def around(n):
        return sorted(range(1, n), key=lambda k: (-min(k, n - k), k))

    near_p = [lax.rem(probe + k, probes) for k in around(probes)]
    near_x = [tile - xc + lax.rem(xc + k, x_chips) for k in around(x_chips)]
    a_peers = [{"probe": p, "tile": t, "level": h}
               for t in near_x + [tile] for h in (other, half) for p in near_p + [probe]][:-1]
    b_peers = [{"tile": lax.rem(tile + k * x_chips, tiles)} for k in around(z_chips)]
    p_peers = near_p
    z_beside = [{"tile": lax.rem(tile + x_chips, tiles)}, {"tile": lax.rem(tile + tiles - x_chips, tiles)}]
    if z_chips == 1:
        z_beside = []

    barrier = pltpu.get_barrier_semaphore()
    greet = [{"tile": nxt}, {"tile": prv}, {"level": other},
             {"tile": nxt, "level": other}, {"tile": prv, "level": other}]
    greet += [{"probe": p} for p in p_peers] + z_beside
    for dev in greet:
        pl.semaphore_signal(barrier, inc=1, device_id=dev, device_id_type=MESH)

    sub = lax.broadcasted_iota(jnp.int32, (8, Y), 0)
    lane_h = lax.broadcasted_iota(jnp.int32, (8, 128), 1)
    sub_h = lax.broadcasted_iota(jnp.int32, (8, 128), 0)
    has_next = (tile < tiles - 1).astype(F32)
    has_prev = (tile > 0).astype(F32)
    mask_h = jnp.where(sub < 2, has_next, jnp.where(sub >= 6, has_prev, 0.0))
    zero = jnp.zeros((8, Y), F32)

    def src(l):
        return half * (L - 1) + (1 - 2 * half) * l

    def send(src_ref, dst_ref, ssem, rsem, dev):
        copy = pltpu.make_async_remote_copy(
            src_ref=src_ref, dst_ref=dst_ref, send_sem=ssem, recv_sem=rsem,
            device_id=dev, device_id_type=MESH)
        copy.start()
        return copy

    started = []
    counter = [0]

    def post(src_ref, dst_ref, dev):
        n = counter[0]
        counter[0] += 1
        copy = send(src_ref, dst_ref, send_sem.at[n], recv_sem.at[n], dev)
        started.append(copy)
        return copy

    def loop(n, chunk, body, init=0):
        chunk = min(chunk, n)

        def step(b, carry):
            for k in range(chunk):
                carry = body(b * chunk + k, carry)
            return carry

        return lax.fori_loop(0, n // chunk, step, init)

    def each(n, chunk, body):
        def step(l, carry):
            body(l)
            return carry
        loop(n, chunk, step)

    def pack_rows(rows, g, up_ref, dn_ref):
        up = rows[3]
        dn = pltpu.roll(rows[3], 6, 0)
        for k in (2, 1, 0):
            up = jnp.where(sub < 2 * k + 2, pltpu.roll(rows[k], 2 * k + 2, 0), up)
            dn = jnp.where(sub < 2 * k + 2, pltpu.roll(rows[k], 2 * k, 0) if k else rows[k], dn)
        up_ref[g] = up
        dn_ref[g] = dn

    def pack(put, up_ref, dn_ref):
        each(L // 4, 2, lambda g: pack_rows([put(4 * g + k) for k in range(4)], g, up_ref, dn_ref))

    def beside_rows(a_ref, b_ref, g):
        a = a_ref[g]
        b = b_ref[g]
        out = []
        for k in range(4):
            ra = pltpu.roll(a, 6 - 2 * k, 0) if k < 3 else a
            rb = pltpu.roll(b, 8 - 2 * k, 0) if k else b
            out.append(jnp.where(sub >= 4, ra, rb))
        return out

    def unpack(a_ref, b_ref, write):
        def body(g):
            for k, x in enumerate(beside_rows(a_ref, b_ref, g)):
                write(4 * g + k, x)
        each(L // 4, 2, body)

    def pack_outer(rows, g, up_ref, dn_ref):
        up = rows[7]
        dn = pltpu.roll(rows[7], 7, 0)
        for k in range(6, -1, -1):
            up = jnp.where(sub <= k, pltpu.roll(rows[k], k + 1, 0), up)
            dn = jnp.where(sub <= k, pltpu.roll(rows[k], k, 0) if k else rows[k], dn)
        up_ref[g] = up
        dn_ref[g] = dn

    def beside_outer(a_ref, b_ref, g):
        a = a_ref[g]
        b = b_ref[g]
        out = []
        for k in range(8):
            ra = pltpu.roll(a, 7 - k, 0) if k < 7 else a
            rb = pltpu.roll(b, 8 - k, 0) if k else b
            out.append(jnp.where(sub >= 4, ra, rb))
        return out

    first_lane = lane_h == 0
    last_lane = lane_h == 127

    def sides(a):
        parts = [a[:, n * 128:(n + 1) * 128] for n in range(Y // 128)]
        right = [pltpu.roll(x, 1, 1) for x in parts]
        left = [pltpu.roll(x, 127, 1) for x in parts]
        out = []
        for n in range(len(parts)):
            before = jnp.where(first_lane, right[n - 1] if n else 0.0, right[n])
            after = jnp.where(last_lane, left[n + 1] if n + 1 < len(parts) else 0.0, left[n])
            out.append(before + after)
        return jnp.concatenate(out, axis=1)

    def beside(a, b):
        up = jnp.where(sub == 0, pltpu.roll(b, 1, 0), pltpu.roll(a, 1, 0))
        dn = jnp.where(sub == 7, pltpu.roll(b, 7, 0), pltpu.roll(a, 7, 0))
        return (up + dn) + sides(a)

    def factor(d_ref, m_ref, hg_ref):
        m_ref[0] = zero

        def up(l, m):
            m = 2.0 / (d_ref[l] - 2.0 * m)
            m_ref[l + 1] = m
            return m
        last = loop(L, 8, up, zero)

        def down(k, h):
            l = L - 1 - k
            h = m_ref[l + 1] * h
            hg_ref[l] = h
            return h
        loop(L, 8, down, zero + 1.0)

        def again(l, g):
            g = 0.5 * hg_ref[l] + m_ref[l] * g
            hg_ref[l] = g
            return g
        return last, loop(L, 8, again, zero)

    def solve(read, size, m_ref, f_ref, y_ref):
        def fwd(g, f):
            for k, r in enumerate(read(g)):
                l = g * size + k
                f = 0.5 * r + m_ref[l] * f
                f_ref[l] = f
            return f
        first = loop(L // size, 16 // size, fwd, zero)

        def back(k, y):
            l = L - 1 - k
            y = m_ref[l + 1] * (f_ref[l] + y)
            y_ref[l] = y
            return y
        loop(L, 16, back, zero)
        return first

    def passes(read, size, m_ref, f_ref):
        first = solve(read, size, m_ref, f_ref, y_f)

        def again(l, g):
            g = 0.5 * y_f[l] + m_ref[l] * g
            f_ref[l] = g
            return g
        return first, loop(L, 16, again, zero)

    def edges(a, b):
        inside = jnp.where(sub < 4, pltpu.roll(b, 2, 0), pltpu.roll(b, 6, 0))
        return jnp.where((sub >= 2) & (sub < 6), inside, a)

    def beyond(a, b):
        return jnp.where(sub >= 4, a, b), jnp.where(sub >= 4, pltpu.roll(a, 2, 0), pltpu.roll(b, 6, 0))

    def join(const, own, far):
        mo, ho, mp, hp, inv = const
        (fo, go), (fp, gp) = own, far
        x = mo * (fo + mp * fp) * inv
        xi = mp * (fp + mo * fo) * inv
        g = go + xi * ho
        gf = gp + x * hp
        w = mo * (g + mp * gf) * inv
        eta = mp * (gf + mo * g) * inv
        return xi, w, eta

    def finish_m(j, const, own, far, dp):
        xi, w, eta = join(const, own, far)
        next_one = 0.5 * (dp * eta - xi) - w
        v_m[j, L + 1] = eta if j == 0 else eta - v_m[j - 1, L + 1]
        v_m[j, L + 2] = next_one if j == 0 else next_one - v_m[j - 1, L + 2]

        def down(k, w):
            l = L - 1 - k
            w = m_m[l + 1] * ((f_m[l] + xi * hg_m[l]) + w)
            v_m[j, l + 1] = w if j == 0 else w - v_m[j - 1, l + 1]
            return w
        loop(L, 16, down, eta)

    def finish_h(j, const, own, far):
        xi, w, eta = join(const, own, far)
        v_h[L + 1] = eta if j == 0 else eta - v_h[L + 1]

        def down(k, w):
            l = L - 1 - k
            w = m_h[l + 1] * ((f_h[l] + xi * hg_h[l]) + w)
            v_h[l + 1] = w if j == 0 else w - v_h[l + 1]
            return w
        loop(L, 16, down, eta)

    def inner_k(j):
        def body(l):
            a = v_m[j, l + 1]
            rows = jnp.where(sub == 0, 0.0, pltpu.roll(a, 1, 0)) + jnp.where(sub == 7, 0.0, pltpu.roll(a, 7, 0))
            u_m[j, l + 1] = (d_m[l] * a - (rows + sides(a))) - 2.0 * (v_m[j, l] + v_m[j, l + 2])
        each(L, 8, body)
        if j < STEPS - 1:
            body(L)

    def outer_dots(j):
        def body(l, carry):
            b = v_h[l + 1]
            add = jnp.where(sub == 0, pltpu.roll(b, 1, 0), jnp.where(sub == 7, pltpu.roll(b, 7, 0), 0.0))
            u = u_m[j, l + 1] - add
            u_m[j, l + 1] = u
            out = [carry[i] + u * u_m[i, l + 1] for i in range(j)]
            return tuple(out + [carry[j] + u * u])
        sums = loop(L, 8, body, (zero,) * (j + 1))
        for i in range(j + 1):
            n = ROW[i, j]
            gram[n:n + 1] = fold(sums[i])

    def outer_k(j):
        def fix(l, b):
            add = jnp.where(sub == 0, pltpu.roll(b, 1, 0), jnp.where(sub == 7, pltpu.roll(b, 7, 0), 0.0))
            u_m[j, l + 1] = u_m[j, l + 1] - add

        def body(l):
            b = v_h[l + 1]
            fix(l, b)
            u = (d_h[l] * b - beside(b, v_m[j, l + 1])) - 2.0 * (v_h[l] + v_h[l + 2])
            u_h[l] = mask_h * u
        each(L, 8, body)
        fix(L, v_h[L + 1])

    def again_k(j, l):
        a = u_m[j, l + 1]
        r = (d_m[l] * a - beside(a, u_h[l])) - 2.0 * (u_m[j, l] + u_m[j, l + 2])
        r_m[l] = r
        return r

    def fold(acc):
        row = jnp.sum(acc, axis=0, keepdims=True)
        total = row[:, :128]
        for n in range(1, Y // 128):
            total = total + row[:, n * 128:(n + 1) * 128]
        return total

    def side_dot(j):
        n = len(PAIRS) + j
        gram[n:n + 1] = fold(loop(L, 8, lambda l, acc: acc + v_m[j, l + 1] * s_m[l + 1], zero))

    def dots(j):
        def body(l, carry):
            u = u_m[j, l + 1]
            return tuple(carry[i] + u * u_m[i, l + 1] for i in range(j + 1))
        sums = loop(L, 8, body, (zero,) * (j + 1))
        for i in range(j + 1):
            n = ROW[i, j]
            gram[n:n + 1] = fold(sums[i])

    low = lane_h < 64

    def quarter(q, top, bot):
        n = q // 2
        p, b = top[:, n * 128:(n + 1) * 128], bot[:, n * 128:(n + 1) * 128]
        if q % 2 == 0:
            return jnp.where(low, p, pltpu.roll(b, 64, 1))
        return jnp.where(low, pltpu.roll(p, 64, 1), b)

    def fill_t(j):
        def body(l):
            top = v_m[j, l + 1] * ks[l] + u_m[j, l + 1] * s_m[l + 1]
            k = l + H
            bot = v_m[j, k + 1] * ks[k] + u_m[j, k + 1] * s_m[k + 1]
            for q in range(probes):
                t_out[j, q, l] = quarter(q, top, bot)
            t_in[j, probe, l] = t_out[j, probe, l]
        each(H, 2, body)

    trace_parts = []

    def send_t(j):
        for g in p_peers:
            trace_parts.append(post(t_out.at[j, g], t_in.at[j, probe], {"probe": g}))

    loads[0].wait()

    def put_d(l):
        d = kap_v[src(l)] + 8.0
        d_m[l] = d
        return d
    pack(put_d, halo_out.at[0, 0], halo_out.at[0, 1])
    pl.semaphore_wait(barrier, len(greet))
    G2 = L // 8
    in_pair = lax.rem(probe, 2)
    part = pl.ds(in_pair * G2, G2)
    pair = {"probe": probe + 1 - 2 * in_pair}
    halo_d = [
        post(halo_out.at[0, 0, part], halo_in.at[0, 0, part], {"tile": nxt}),
        post(halo_out.at[0, 1, part], halo_in.at[0, 1, part], {"tile": prv}),
    ]
    mo_m, ho_m = factor(d_m, m_m, hg_m)
    loads[1].wait()

    def put_s(l):
        s = (2 * bits_v[src(l)] - 1).astype(F32)
        s_m[l + 1] = s
        return s
    pack(put_s, halo_out.at[1, 0], halo_out.at[1, 1])
    own_m = passes(lambda l: [s_m[l + 1]], 1, m_m, f_m)
    loads[2].wait()
    side_out[0] = edges(mo_m, ho_m)
    side_out[1] = edges(own_m[0], own_m[1])
    for n, plane in enumerate((mo_m, ho_m, own_m[0], own_m[1], d_m[L - 1], s_m[L], obs_v[src(L - 1)])):
        first_out[n] = plane
    far = [
        post(side_out, side_in.at[0], {"tile": nxt, "level": other}),
        post(side_out, side_in.at[1], {"tile": prv, "level": other}),
        post(first_out, first_in, {"level": other}),
    ]
    halo_s = [
        post(halo_out.at[1, 0], halo_in.at[1, 0], {"tile": nxt}),
        post(halo_out.at[1, 1], halo_in.at[1, 1], {"tile": prv}),
    ]
    s_m[0] = zero
    o_m[0] = zero
    for j in range(STEPS):
        v_m[j, 0] = zero
        u_m[j, 0] = zero
    v_h[0] = zero

    def put_o(l):
        o = obs_v[src(l)]
        o_m[l + 1] = o
        return o
    pack(put_o, halo_out.at[2, 0], halo_out.at[2, 1])
    halo_o = [
        post(halo_out.at[2, 0], halo_in.at[2, 0], {"tile": nxt}),
        post(halo_out.at[2, 1], halo_in.at[2, 1], {"tile": prv}),
    ]

    def weigh(k, x):
        l = L - 1 - k
        al_m[l] = x
        return m_m[l] * x
    loop(L, 16, weigh, zero + 0.5)
    solve(lambda l: [al_m[l]], 1, m_m, r_m, be_m)

    shared = []
    for side, copy in enumerate(halo_d):
        copy.wait_recv()
        shared.append(post(halo_in.at[0, side, part], halo_in.at[0, side, part], pair))
    for copy in shared:
        copy.wait_recv()

    def put_dh(l, x):
        d_h[l] = jnp.where(mask_h > 0.0, x, 8.0)
    unpack(halo_in.at[0, 0], halo_in.at[0, 1], put_dh)
    mo_h, ho_h = factor(d_h, m_h, hg_h)

    far[2].wait_recv()
    mp_m, hp_m, fp_m, gp_m, dp_m = (first_in[n] for n in range(5))
    d_m[L] = dp_m
    s_m[L + 1] = first_in[5]
    o_m[L + 1] = first_in[6]
    const_m = (mo_m, ho_m, mp_m, hp_m, 1.0 / (1.0 - mo_m * mp_m))
    finish_m(0, const_m, own_m, (fp_m, gp_m), dp_m)
    inner_k(0)

    for copy in halo_s:
        copy.wait_recv()

    def read_sh(g):
        rows = [x * mask_h for x in beside_rows(halo_in.at[1, 0], halo_in.at[1, 1], g)]
        for k, x in enumerate(rows):
            s_h[4 * g + k] = x
        return rows
    own_h = passes(read_sh, 4, m_h, f_h)
    for copy in far[:2]:
        copy.wait_recv()

    mp_h, hp_h = beyond(side_in[0, 0], side_in[1, 0])
    fp_h, gp_h = beyond(side_in[0, 1], side_in[1, 1])
    const_h = (mo_h, ho_h, mp_h, hp_h, 1.0 / (1.0 - mo_h * mp_h))
    finish_h(0, const_h, own_h, (mask_h * fp_h, mask_h * gp_h))
    outer_k(0)

    odd = lax.rem(probe, 2) == 1
    upper = probe // 2 == 1

    def mine(top, bot):
        out = [jnp.where(odd, quarter(2 * n + 1, top, bot), quarter(2 * n, top, bot)) for n in range(Y // 128)]
        return jnp.where(upper, out[1], out[0])

    def side_terms():
        for copy in halo_o:
            copy.wait_recv()

        def put_oh(l, x):
            o_h[l] = x * mask_h
        unpack(halo_in.at[2, 0], halo_in.at[2, 1], put_oh)

        def body(l):
            a = s_m[l + 1]
            ks[l] = (d_m[l] * a - beside(a, s_h[l])) - 2.0 * (s_m[l] + s_m[l + 2])
            b = o_m[l + 1]
            ko = (d_m[l] * b - beside(b, o_h[l])) - 2.0 * (o_m[l] + o_m[l + 2])
            data[l] = kap_v[src(l)] * (2.0 * b * ko)
        each(L, 4, body)

    def quarters():
        def body(l):
            kap_q[l] = mine(kap_v[src(l)], kap_v[src(l + H)]) * (1.0 / probes)
            sub_q[l] = mine(data[l], data[l + H])
        each(H, 2, body)

    for j in range(1, STEPS):
        n = j - 1
        one_row = j == STEPS - 1 and L % 8 == 0
        size = 8 if one_row else 4
        used = pl.ds(0, L // size)

        def form(g, carry):
            fo, go = carry
            tiles_r = []
            for k in range(size):
                l = size * g + k
                r = again_k(j - 1, l)
                fo = fo + al_m[l] * r
                go = go + be_m[l] * r
                tiles_r.append(r)
            (pack_outer if one_row else pack_rows)(tiles_r, g, xs_out.at[n, 0], xs_out.at[n, 1])
            return fo, go
        own_m = loop(L // size, 8 // size, form, (zero, zero))
        ed_out[n] = edges(own_m[0], own_m[1])
        pl_out[n, 0] = own_m[0]
        pl_out[n, 1] = own_m[1]
        planes = [
            post(ed_out.at[n], ed_in.at[n, 0], {"tile": nxt, "level": other}),
            post(ed_out.at[n], ed_in.at[n, 1], {"tile": prv, "level": other}),
            post(pl_out.at[n], pl_in.at[n], {"level": other}),
        ]
        rows = [
            post(xs_out.at[n, 0, used], xs_in.at[n, 0, used], {"tile": nxt}),
            post(xs_out.at[n, 1, used], xs_in.at[n, 1, used], {"tile": prv}),
        ]
        for dev in z_beside:
            pl.semaphore_signal(here_sem.at[n], inc=1, device_id=dev, device_id_type=MESH)
        passes(lambda l: [r_m[l]], 1, m_m, f_m)
        dots(j - 1)
        side_dot(j - 1)
        if j == 1:
            side_terms()
        if j == 2:
            quarters()
        fill_t(j - 1)
        planes[2].wait_recv()
        finish_m(j, const_m, own_m, (pl_in[n, 0], pl_in[n, 1]), dp_m)
        inner_k(j)
        if j == STEPS - 1:
            side_dot(j)
            for i in range(len(PAIRS) + STEPS, N_ROWS):
                gram[i:i + 1] = jnp.zeros((1, 128), F32)
        for copy in rows:
            copy.wait_recv()

        beside_r = beside_outer if one_row else beside_rows

        def read_rh(g):
            return [x * mask_h for x in beside_r(xs_in.at[n, 0], xs_in.at[n, 1], g)]
        own_h = passes(read_rh, size, m_h, f_h)
        for copy in planes[:2]:
            copy.wait_recv()
        if z_beside:
            pl.semaphore_wait(here_sem.at[n], len(z_beside))
        send_t(j - 1)
        fp_h, gp_h = beyond(ed_in[n, 0], ed_in[n, 1])
        finish_h(j, const_h, own_h, (mask_h * fp_h, mask_h * gp_h))
        if j < STEPS - 1:
            outer_k(j)
        else:
            outer_dots(j)

    wide = lax.broadcasted_iota(jnp.int32, (N_ROWS, 128), 1) == lax.broadcasted_iota(jnp.int32, (N_ROWS, 128), 0)
    each_sum = jnp.sum(gram[...], axis=1, keepdims=True)
    packed = jnp.sum(jnp.where(wide, each_sum, 0.0), axis=0, keepdims=True)
    for copy in trace_parts[:probes - 1]:
        copy.wait_recv()
    red_out[...] = packed
    red_a[spot] = packed
    plane = [post(red_out, red_a.at[spot], dev) for dev in a_peers]
    fill_t(STEPS - 1)
    send_t(STEPS - 1)
    for copy in plane:
        copy.wait_recv()
    for p in range(probes):
        base = p * levels * x_chips
        part = red_a[base]
        for k in range(1, levels * x_chips):
            part = part + red_a[base + k]
        red_b[zc, p] = part
    before = list(started)
    line = [post(red_b.at[zc], red_b.at[zc], dev) for dev in b_peers]
    for copy in before:
        copy.wait_send()
    for copy in line:
        copy.wait_recv()
    total = None
    for p in range(probes):
        part = red_b[0, p]
        for k in range(1, z_chips):
            part = part + red_b[k, p]
        part = jnp.broadcast_to(part, (8, 128))
        total = part if p == 0 else jnp.where(sub_h == p, part, total)

    def column(n):
        return jnp.broadcast_to(total[:, n:n + 1], (8, 128))
    a = {pair: column(n) for pair, n in ROW.items()}
    c = [column(len(PAIRS) + j) for j in range(STEPS)]
    pivot = []
    ratio = {}
    for j in range(STEPS):
        pivot.append(1.0 / a[j, j])
        for i in range(j + 1, STEPS):
            ratio[j, i] = a[j, i] * pivot[j]
        for i in range(j + 1, STEPS):
            c[i] = c[i] - ratio[j, i] * c[j]
            for k in range(i, STEPS):
                a[i, k] = a[i, k] - ratio[j, i] * a[j, k]
    for j in range(STEPS - 1, -1, -1):
        c[j] = c[j] * pivot[j]
        for i in range(j + 1, STEPS):
            c[j] = c[j] - ratio[j, i] * c[i]
    weight = {(p, j): jnp.broadcast_to(c[j][p:p + 1], (8, 128)) for p in range(probes) for j in range(STEPS)}

    for copy in trace_parts[probes - 1:]:
        copy.wait_recv()

    def write(l):
        acc = None
        for j in range(STEPS):
            for p in range(probes):
                part = weight[p, j] * t_in[j, p, l]
                acc = part if acc is None else acc + part
        res = kap_q[l] * acc - sub_q[l]
        out_ref[src(l)] = res[:, :64]
        out_ref[src(l + H)] = pltpu.roll(res, 64, 1)[:, :64]
    each(H, 4, write)
    for copy in line:
        copy.wait_send()


def solution(mesh):
    probes, tiles, levels = (mesh.shape[a] for a in ("probe", "tile", "level"))
    x_chips = min(X_CHIPS, tiles)
    z_chips = tiles // x_chips

    def step(bits, kap, obs):
        _, L, rows, Y = bits.shape
        dims = (probes, tiles, levels, x_chips, L, Y)
        vm = lambda *lead: pltpu.VMEM((*lead, 8, Y), F32)
        dma = lambda n: pltpu.SemaphoreType.DMA((n,))
        G = L // 4
        n_sems = 11 + 5 * (STEPS - 1) + (probes * levels * x_chips - 1) + (z_chips - 1) + STEPS * (probes - 1)
        part = lambda *lead: pltpu.VMEM((*lead, L // 2, 8, 128), F32)
        scratch = [
            pltpu.VMEM((L, 8, Y), jnp.int32), vm(L), vm(L),
            vm(L + 2), vm(L), vm(L + 1), vm(L), vm(L + 2), vm(L),
            vm(L + 1), vm(L + 1), vm(L), vm(L), vm(L), vm(L),
            vm(STEPS, L + 3), vm(L + 2), vm(STEPS, L + 2), vm(L), vm(L), vm(L), vm(L), vm(L), vm(L),
            vm(3, 2, G), vm(3, 2, G), vm(STEPS - 1, 2, G), vm(STEPS - 1, 2, G),
            vm(7), vm(7), vm(2), vm(2, 2),
            vm(STEPS - 1, 2), vm(STEPS - 1, 2), vm(STEPS - 1), vm(STEPS - 1, 2),
            pltpu.VMEM((N_ROWS, 128), F32),
            pltpu.VMEM((1, 128), F32),
            pltpu.VMEM((probes * levels * x_chips, 1, 128), F32),
            pltpu.VMEM((z_chips, probes, 1, 128), F32),
            part(STEPS, probes), part(STEPS, probes), part(), part(), vm(L),
            dma(3), dma(n_sems), dma(n_sems), pltpu.SemaphoreType.REGULAR((STEPS - 1,)),
        ]
        return pl.pallas_call(
            functools.partial(kernel, dims),
            out_shape=pltpu.VMEM((L, rows, Y // probes), F32),
            in_specs=[pl.BlockSpec(memory_space=pl.ANY)] * 3,
            out_specs=pl.BlockSpec(memory_space=pltpu.VMEM),
            scratch_shapes=scratch,
            compiler_params=pltpu.CompilerParams(collective_id=0, has_side_effects=True),
        )(bits, kap, obs)

    return jax.shard_map(
        step,
        mesh=mesh,
        in_specs=(P("probe", "level", "tile", None), P("level", "tile", None), P("level", "tile", None)),
        out_specs=P("level", "tile", "probe"),
        check_vma=False,
    )
```

```python
import functools

import jax
import jax.numpy as jnp
from jax import lax
from jax.experimental import pallas as pl
from jax.experimental.pallas import tpu as pltpu
from jax.sharding import PartitionSpec as P

MESH = pl.DeviceIdType.MESH
STEPS = 4
F32 = jnp.float32
X_CHIPS = 4

PAIRS = [(i, j) for j in range(STEPS) for i in range(j + 1)]
ROW = {pair: n for n, pair in enumerate(PAIRS)}
N_ROWS = 16


def kernel(
    dims,
    bits_hbm, kap_hbm, obs_hbm, out_ref,
    bits_v, kap_v, obs_v,
    s_m, s_h, d_m, d_h, o_m, o_h,
    m_m, m_h, hg_m, hg_h, al_m, be_m,
    v_m, v_h, u_m, u_h, r_m, f_m, f_h, y_f, ks,
    halo_out, halo_in, xs_out, xs_in,
    first_out, first_in, side_out, side_in, pl_out, pl_in, ed_out, ed_in,
    gram, red_out, red_a, red_b, t_out, t_in, kap_q, sub_q, data,
    in_sem, send_sem, recv_sem, here_sem,
):
    probes, tiles, levels, x_chips, L, Y = dims
    z_chips = tiles // x_chips
    H = L // 2
    probe = lax.axis_index("probe")
    tile = lax.axis_index("tile")
    half = lax.axis_index("level")
    zc = tile // x_chips
    xc = tile - zc * x_chips
    nxt = lax.rem(tile + 1, tiles)
    prv = lax.rem(tile + tiles - 1, tiles)
    other = 1 - half
    n_a = probes * levels * x_chips
    spot = (probe * levels + half) * x_chips + xc

    loads = [
        pltpu.make_async_copy(kap_hbm, kap_v, in_sem.at[0]),
        pltpu.make_async_copy(bits_hbm.at[0], bits_v, in_sem.at[1]),
        pltpu.make_async_copy(obs_hbm, obs_v, in_sem.at[2]),
    ]
    for copy in loads:
        copy.start()

    def around(n):
        return sorted(range(1, n), key=lambda k: (-min(k, n - k), k))

    near_p = [lax.rem(probe + k, probes) for k in around(probes)]
    near_x = [tile - xc + lax.rem(xc + k, x_chips) for k in around(x_chips)]
    a_peers = [{"probe": p, "tile": t, "level": h}
               for t in near_x + [tile] for h in (other, half) for p in near_p + [probe]][:-1]
    b_peers = [{"tile": lax.rem(tile + k * x_chips, tiles)} for k in around(z_chips)]
    p_peers = near_p
    not_end = [tile < tiles - 1, tile > 0]

    def along_z(d):
        return [(zc + d < z_chips, {"tile": lax.rem(tile + d * x_chips, tiles)}),
                (zc >= d, {"tile": lax.rem(tile + tiles - d * x_chips, tiles)})]

    def signal_if(sem, pairs):
        for there, dev in pairs:
            pl.when(there)(functools.partial(
                pl.semaphore_signal, sem, inc=1, device_id=dev, device_id_type=MESH))

    def count(pairs):
        return sum(there.astype(jnp.int32) for there, _ in pairs)

    barrier = pltpu.get_barrier_semaphore()
    ends = [(not_end[0], {"tile": nxt}), (not_end[1], {"tile": prv}),
            (not_end[0], {"tile": nxt, "level": other}), (not_end[1], {"tile": prv, "level": other})]
    ends += along_z(1)
    greet = [{"level": other}] + [{"probe": p} for p in p_peers]
    signal_if(barrier, ends)
    for dev in greet:
        pl.semaphore_signal(barrier, inc=1, device_id=dev, device_id_type=MESH)

    sub = lax.broadcasted_iota(jnp.int32, (8, Y), 0)
    lane_h = lax.broadcasted_iota(jnp.int32, (8, 128), 1)
    sub_h = lax.broadcasted_iota(jnp.int32, (8, 128), 0)
    has_next = (tile < tiles - 1).astype(F32)
    has_prev = (tile > 0).astype(F32)
    mask_h = jnp.where(sub < 2, has_next, jnp.where(sub >= 6, has_prev, 0.0))
    zero = jnp.zeros((8, Y), F32)

    def src(l):
        return half * (L - 1) + (1 - 2 * half) * l

    def send(src_ref, dst_ref, ssem, rsem, dev):
        copy = pltpu.make_async_remote_copy(
            src_ref=src_ref, dst_ref=dst_ref, send_sem=ssem, recv_sem=rsem,
            device_id=dev, device_id_type=MESH)
        copy.start()
        return copy

    started = []
    counter = [0]

    def post(src_ref, dst_ref, dev):
        n = counter[0]
        counter[0] += 1
        copy = send(src_ref, dst_ref, send_sem.at[n], recv_sem.at[n], dev)
        started.append(copy)
        return copy

    class Ended:
        def __init__(self, copy, goes, comes):
            self.copy, self.goes, self.comes = copy, goes, comes
            pl.when(goes)(copy.start)

        def wait_send(self):
            pl.when(self.goes)(self.copy.wait_send)

        def wait_recv(self):
            pl.when(self.comes)(self.copy.wait_recv)

    def post_to(side, src_ref, dst_ref, dev):
        n = counter[0]
        counter[0] += 1
        copy = pltpu.make_async_remote_copy(
            src_ref=src_ref, dst_ref=dst_ref, send_sem=send_sem.at[n], recv_sem=recv_sem.at[n],
            device_id=dev, device_id_type=MESH)
        copy = Ended(copy, not_end[side], not_end[1 - side])
        started.append(copy)
        return copy

    def loop(n, chunk, body, init=0):
        chunk = min(chunk, n)

        def step(b, carry):
            for k in range(chunk):
                carry = body(b * chunk + k, carry)
            return carry

        return lax.fori_loop(0, n // chunk, step, init)

    def each(n, chunk, body):
        def step(l, carry):
            body(l)
            return carry
        loop(n, chunk, step)

    def pack_rows(rows, g, up_ref, dn_ref):
        up = rows[3]
        dn = pltpu.roll(rows[3], 6, 0)
        for k in (2, 1, 0):
            up = jnp.where(sub < 2 * k + 2, pltpu.roll(rows[k], 2 * k + 2, 0), up)
            dn = jnp.where(sub < 2 * k + 2, pltpu.roll(rows[k], 2 * k, 0) if k else rows[k], dn)
        up_ref[g] = up
        dn_ref[g] = dn

    def pack(put, up_ref, dn_ref):
        each(L // 4, 2, lambda g: pack_rows([put(4 * g + k) for k in range(4)], g, up_ref, dn_ref))

    def beside_rows(a_ref, b_ref, g):
        a = a_ref[g]
        b = b_ref[g]
        out = []
        for k in range(4):
            ra = pltpu.roll(a, 6 - 2 * k, 0) if k < 3 else a
            rb = pltpu.roll(b, 8 - 2 * k, 0) if k else b
            out.append(jnp.where(sub >= 4, ra, rb))
        return out

    def unpack(a_ref, b_ref, write):
        def body(g):
            for k, x in enumerate(beside_rows(a_ref, b_ref, g)):
                write(4 * g + k, x)
        each(L // 4, 2, body)

    def pack_outer(rows, g, up_ref, dn_ref):
        up = rows[7]
        dn = pltpu.roll(rows[7], 7, 0)
        for k in range(6, -1, -1):
            up = jnp.where(sub <= k, pltpu.roll(rows[k], k + 1, 0), up)
            dn = jnp.where(sub <= k, pltpu.roll(rows[k], k, 0) if k else rows[k], dn)
        up_ref[g] = up
        dn_ref[g] = dn

    def beside_outer(a_ref, b_ref, g):
        a = a_ref[g]
        b = b_ref[g]
        out = []
        for k in range(8):
            ra = pltpu.roll(a, 7 - k, 0) if k < 7 else a
            rb = pltpu.roll(b, 8 - k, 0) if k else b
            out.append(jnp.where(sub >= 4, ra, rb))
        return out

    first_lane = lane_h == 0
    last_lane = lane_h == 127

    def sides(a):
        parts = [a[:, n * 128:(n + 1) * 128] for n in range(Y // 128)]
        right = [pltpu.roll(x, 1, 1) for x in parts]
        left = [pltpu.roll(x, 127, 1) for x in parts]
        out = []
        for n in range(len(parts)):
            before = jnp.where(first_lane, right[n - 1] if n else 0.0, right[n])
            after = jnp.where(last_lane, left[n + 1] if n + 1 < len(parts) else 0.0, left[n])
            out.append(before + after)
        return jnp.concatenate(out, axis=1)

    def beside(a, b):
        up = jnp.where(sub == 0, pltpu.roll(b, 1, 0), pltpu.roll(a, 1, 0))
        dn = jnp.where(sub == 7, pltpu.roll(b, 7, 0), pltpu.roll(a, 7, 0))
        return (up + dn) + sides(a)

    def factor(d_ref, m_ref, hg_ref):
        m_ref[0] = zero

        def up(l, m):
            m = 2.0 / (d_ref[l] - 2.0 * m)
            m_ref[l + 1] = m
            return m
        last = loop(L, 8, up, zero)

        def down(k, h):
            l = L - 1 - k
            h = m_ref[l + 1] * h
            hg_ref[l] = h
            return h
        loop(L, 8, down, zero + 1.0)

        def again(l, g):
            g = 0.5 * hg_ref[l] + m_ref[l] * g
            hg_ref[l] = g
            return g
        return last, loop(L, 8, again, zero)

    def solve(read, size, m_ref, f_ref, y_ref):
        def fwd(g, f):
            for k, r in enumerate(read(g)):
                l = g * size + k
                f = 0.5 * r + m_ref[l] * f
                f_ref[l] = f
            return f
        first = loop(L // size, 16 // size, fwd, zero)

        def back(k, y):
            l = L - 1 - k
            y = m_ref[l + 1] * (f_ref[l] + y)
            y_ref[l] = y
            return y
        loop(L, 16, back, zero)
        return first

    def passes(read, size, m_ref, f_ref):
        first = solve(read, size, m_ref, f_ref, y_f)

        def again(l, g):
            g = 0.5 * y_f[l] + m_ref[l] * g
            f_ref[l] = g
            return g
        return first, loop(L, 16, again, zero)

    def edges(a, b):
        inside = jnp.where(sub < 4, pltpu.roll(b, 2, 0), pltpu.roll(b, 6, 0))
        return jnp.where((sub >= 2) & (sub < 6), inside, a)

    def beyond(a, b):
        return jnp.where(sub >= 4, a, b), jnp.where(sub >= 4, pltpu.roll(a, 2, 0), pltpu.roll(b, 6, 0))

    def join(const, own, far):
        mo, ho, mp, hp, inv = const
        (fo, go), (fp, gp) = own, far
        x = mo * (fo + mp * fp) * inv
        xi = mp * (fp + mo * fo) * inv
        g = go + xi * ho
        gf = gp + x * hp
        w = mo * (g + mp * gf) * inv
        eta = mp * (gf + mo * g) * inv
        return xi, w, eta

    def finish_m(j, const, own, far, dp):
        xi, w, eta = join(const, own, far)
        next_one = 0.5 * (dp * eta - xi) - w
        v_m[j, L + 1] = eta if j == 0 else eta - v_m[j - 1, L + 1]
        v_m[j, L + 2] = next_one if j == 0 else next_one - v_m[j - 1, L + 2]

        def down(k, w):
            l = L - 1 - k
            w = m_m[l + 1] * ((f_m[l] + xi * hg_m[l]) + w)
            v_m[j, l + 1] = w if j == 0 else w - v_m[j - 1, l + 1]
            return w
        loop(L, 16, down, eta)

    def finish_h(j, const, own, far):
        xi, w, eta = join(const, own, far)
        v_h[L + 1] = eta if j == 0 else eta - v_h[L + 1]

        def down(k, w):
            l = L - 1 - k
            w = m_h[l + 1] * ((f_h[l] + xi * hg_h[l]) + w)
            v_h[l + 1] = w if j == 0 else w - v_h[l + 1]
            return w
        loop(L, 16, down, eta)

    def inner_k(j):
        def body(l):
            a = v_m[j, l + 1]
            rows = jnp.where(sub == 0, 0.0, pltpu.roll(a, 1, 0)) + jnp.where(sub == 7, 0.0, pltpu.roll(a, 7, 0))
            u_m[j, l + 1] = (d_m[l] * a - (rows + sides(a))) - 2.0 * (v_m[j, l] + v_m[j, l + 2])
        each(L, 8, body)
        if j < STEPS - 1:
            body(L)

    def outer_dots(j):
        def body(l, carry):
            b = v_h[l + 1]
            add = jnp.where(sub == 0, pltpu.roll(b, 1, 0), jnp.where(sub == 7, pltpu.roll(b, 7, 0), 0.0))
            u = u_m[j, l + 1] - add
            u_m[j, l + 1] = u
            out = [carry[i] + u * u_m[i, l + 1] for i in range(j)]
            return tuple(out + [carry[j] + u * u])
        sums = loop(L, 8, body, (zero,) * (j + 1))
        for i in range(j + 1):
            n = ROW[i, j]
            gram[n:n + 1] = fold(sums[i])

    def outer_k(j):
        def fix(l, b):
            add = jnp.where(sub == 0, pltpu.roll(b, 1, 0), jnp.where(sub == 7, pltpu.roll(b, 7, 0), 0.0))
            u_m[j, l + 1] = u_m[j, l + 1] - add

        def body(l):
            b = v_h[l + 1]
            fix(l, b)
            u = (d_h[l] * b - beside(b, v_m[j, l + 1])) - 2.0 * (v_h[l] + v_h[l + 2])
            u_h[l] = mask_h * u
        each(L, 8, body)
        fix(L, v_h[L + 1])

    def again_k(j, l):
        a = u_m[j, l + 1]
        r = (d_m[l] * a - beside(a, u_h[l])) - 2.0 * (u_m[j, l] + u_m[j, l + 2])
        r_m[l] = r
        return r

    def fold(acc):
        row = jnp.sum(acc, axis=0, keepdims=True)
        total = row[:, :128]
        for n in range(1, Y // 128):
            total = total + row[:, n * 128:(n + 1) * 128]
        return total

    def side_dot(j):
        n = len(PAIRS) + j
        gram[n:n + 1] = fold(loop(L, 8, lambda l, acc: acc + v_m[j, l + 1] * s_m[l + 1], zero))

    def dots(j):
        def body(l, carry):
            u = u_m[j, l + 1]
            return tuple(carry[i] + u * u_m[i, l + 1] for i in range(j + 1))
        sums = loop(L, 8, body, (zero,) * (j + 1))
        for i in range(j + 1):
            n = ROW[i, j]
            gram[n:n + 1] = fold(sums[i])

    low = lane_h < 64

    def quarter(q, top, bot):
        n = q // 2
        p, b = top[:, n * 128:(n + 1) * 128], bot[:, n * 128:(n + 1) * 128]
        if q % 2 == 0:
            return jnp.where(low, p, pltpu.roll(b, 64, 1))
        return jnp.where(low, pltpu.roll(p, 64, 1), b)

    def fill_t(j):
        def body(l):
            top = v_m[j, l + 1] * ks[l] + u_m[j, l + 1] * s_m[l + 1]
            k = l + H
            bot = v_m[j, k + 1] * ks[k] + u_m[j, k + 1] * s_m[k + 1]
            for q in range(probes):
                t_out[j, q, l] = quarter(q, top, bot)
            t_in[j, probe, l] = t_out[j, probe, l]
        each(H, 2, body)

    trace_parts = []

    def send_t(j):
        for g in p_peers:
            trace_parts.append(post(t_out.at[j, g], t_in.at[j, probe], {"probe": g}))

    loads[0].wait()

    for side in range(2):
        @pl.when(jnp.logical_not(not_end[1 - side]))
        def _():
            def clear(g):
                for k in range(3):
                    halo_in[k, side, g] = zero
                for k in range(STEPS - 1):
                    xs_in[k, side, g] = zero
            each(L // 4, 1, clear)
            for k in range(2):
                side_in[side, k] = zero
            for k in range(STEPS - 1):
                ed_in[k, side] = zero

    def put_d(l):
        d = kap_v[src(l)] + 8.0
        d_m[l] = d
        return d
    pack(put_d, halo_out.at[0, 0], halo_out.at[0, 1])
    pl.semaphore_wait(barrier, len(greet) + count(ends))
    halo_d = [
        post_to(0, halo_out.at[0, 0], halo_in.at[0, 0], {"tile": nxt}),
        post_to(1, halo_out.at[0, 1], halo_in.at[0, 1], {"tile": prv}),
    ]
    mo_m, ho_m = factor(d_m, m_m, hg_m)
    loads[1].wait()

    def put_s(l):
        s = (2 * bits_v[src(l)] - 1).astype(F32)
        s_m[l + 1] = s
        return s
    pack(put_s, halo_out.at[1, 0], halo_out.at[1, 1])
    own_m = passes(lambda l: [s_m[l + 1]], 1, m_m, f_m)
    loads[2].wait()
    side_out[0] = edges(mo_m, ho_m)
    side_out[1] = edges(own_m[0], own_m[1])
    for n, plane in enumerate((mo_m, ho_m, own_m[0], own_m[1], d_m[L - 1], s_m[L], obs_v[src(L - 1)])):
        first_out[n] = plane
    far = [
        post_to(0, side_out, side_in.at[0], {"tile": nxt, "level": other}),
        post_to(1, side_out, side_in.at[1], {"tile": prv, "level": other}),
        post(first_out, first_in, {"level": other}),
    ]
    halo_s = [
        post_to(0, halo_out.at[1, 0], halo_in.at[1, 0], {"tile": nxt}),
        post_to(1, halo_out.at[1, 1], halo_in.at[1, 1], {"tile": prv}),
    ]
    s_m[0] = zero
    o_m[0] = zero
    for j in range(STEPS):
        v_m[j, 0] = zero
        u_m[j, 0] = zero
    v_h[0] = zero

    def put_o(l):
        o = obs_v[src(l)]
        o_m[l + 1] = o
        return o
    pack(put_o, halo_out.at[2, 0], halo_out.at[2, 1])
    halo_o = [
        post_to(0, halo_out.at[2, 0], halo_in.at[2, 0], {"tile": nxt}),
        post_to(1, halo_out.at[2, 1], halo_in.at[2, 1], {"tile": prv}),
    ]

    def weigh(k, x):
        l = L - 1 - k
        al_m[l] = x
        return m_m[l] * x
    loop(L, 16, weigh, zero + 0.5)
    solve(lambda l: [al_m[l]], 1, m_m, r_m, be_m)

    for copy in halo_d:
        copy.wait_recv()

    def put_dh(l, x):
        d_h[l] = jnp.where(mask_h > 0.0, x, 8.0)
    unpack(halo_in.at[0, 0], halo_in.at[0, 1], put_dh)
    mo_h, ho_h = factor(d_h, m_h, hg_h)

    far[2].wait_recv()
    mp_m, hp_m, fp_m, gp_m, dp_m = (first_in[n] for n in range(5))
    d_m[L] = dp_m
    s_m[L + 1] = first_in[5]
    o_m[L + 1] = first_in[6]
    const_m = (mo_m, ho_m, mp_m, hp_m, 1.0 / (1.0 - mo_m * mp_m))
    finish_m(0, const_m, own_m, (fp_m, gp_m), dp_m)
    inner_k(0)

    for copy in halo_s:
        copy.wait_recv()

    def read_sh(g):
        rows = [x * mask_h for x in beside_rows(halo_in.at[1, 0], halo_in.at[1, 1], g)]
        for k, x in enumerate(rows):
            s_h[4 * g + k] = x
        return rows
    own_h = passes(read_sh, 4, m_h, f_h)
    for copy in far[:2]:
        copy.wait_recv()

    mp_h, hp_h = beyond(side_in[0, 0], side_in[1, 0])
    fp_h, gp_h = beyond(side_in[0, 1], side_in[1, 1])
    const_h = (mo_h, ho_h, mp_h, hp_h, 1.0 / (1.0 - mo_h * mp_h))
    finish_h(0, const_h, own_h, (mask_h * fp_h, mask_h * gp_h))
    outer_k(0)

    odd = lax.rem(probe, 2) == 1
    upper = probe // 2 == 1

    def mine(top, bot):
        out = [jnp.where(odd, quarter(2 * n + 1, top, bot), quarter(2 * n, top, bot)) for n in range(Y // 128)]
        return jnp.where(upper, out[1], out[0])

    def side_terms():
        for copy in halo_o:
            copy.wait_recv()

        def put_oh(l, x):
            o_h[l] = x * mask_h
        unpack(halo_in.at[2, 0], halo_in.at[2, 1], put_oh)

        def body(l):
            a = s_m[l + 1]
            ks[l] = (d_m[l] * a - beside(a, s_h[l])) - 2.0 * (s_m[l] + s_m[l + 2])
            b = o_m[l + 1]
            ko = (d_m[l] * b - beside(b, o_h[l])) - 2.0 * (o_m[l] + o_m[l + 2])
            data[l] = kap_v[src(l)] * (2.0 * b * ko)
        each(L, 4, body)

    def quarters():
        def body(l):
            kap_q[l] = mine(kap_v[src(l)], kap_v[src(l + H)]) * (1.0 / probes)
            sub_q[l] = mine(data[l], data[l + H])
        each(H, 2, body)

    for j in range(1, STEPS):
        n = j - 1
        one_row = j == STEPS - 1 and L % 8 == 0
        size = 8 if one_row else 4
        used = pl.ds(0, L // size)

        def form(g, carry):
            fo, go = carry
            tiles_r = []
            for k in range(size):
                l = size * g + k
                r = again_k(j - 1, l)
                fo = fo + al_m[l] * r
                go = go + be_m[l] * r
                tiles_r.append(r)
            (pack_outer if one_row else pack_rows)(tiles_r, g, xs_out.at[n, 0], xs_out.at[n, 1])
            return fo, go
        own_m = loop(L // size, 8 // size, form, (zero, zero))
        ed_out[n] = edges(own_m[0], own_m[1])
        pl_out[n, 0] = own_m[0]
        pl_out[n, 1] = own_m[1]
        planes = [
            post_to(0, ed_out.at[n], ed_in.at[n, 0], {"tile": nxt, "level": other}),
            post_to(1, ed_out.at[n], ed_in.at[n, 1], {"tile": prv, "level": other}),
            post(pl_out.at[n], pl_in.at[n], {"level": other}),
        ]
        rows = [
            post_to(0, xs_out.at[n, 0, used], xs_in.at[n, 0, used], {"tile": nxt}),
            post_to(1, xs_out.at[n, 1, used], xs_in.at[n, 1, used], {"tile": prv}),
        ]
        signal_if(here_sem.at[n], along_z(2 ** n))
        passes(lambda l: [r_m[l]], 1, m_m, f_m)
        dots(j - 1)
        side_dot(j - 1)
        if j == 1:
            side_terms()
        if j == 2:
            quarters()
        fill_t(j - 1)
        planes[2].wait_recv()
        finish_m(j, const_m, own_m, (pl_in[n, 0], pl_in[n, 1]), dp_m)
        inner_k(j)
        if j == STEPS - 1:
            side_dot(j)
            for i in range(len(PAIRS) + STEPS, N_ROWS):
                gram[i:i + 1] = jnp.zeros((1, 128), F32)
        for copy in rows:
            copy.wait_recv()

        beside_r = beside_outer if one_row else beside_rows

        def read_rh(g):
            return [x * mask_h for x in beside_r(xs_in.at[n, 0], xs_in.at[n, 1], g)]
        own_h = passes(read_rh, size, m_h, f_h)
        for copy in planes[:2]:
            copy.wait_recv()
        pl.semaphore_wait(here_sem.at[n], count(along_z(2 ** n)))
        send_t(j - 1)
        fp_h, gp_h = beyond(ed_in[n, 0], ed_in[n, 1])
        finish_h(j, const_h, own_h, (mask_h * fp_h, mask_h * gp_h))
        if j < STEPS - 1:
            outer_k(j)
        else:
            outer_dots(j)

    wide = lax.broadcasted_iota(jnp.int32, (N_ROWS, 128), 1) == lax.broadcasted_iota(jnp.int32, (N_ROWS, 128), 0)
    each_sum = jnp.sum(gram[...], axis=1, keepdims=True)
    packed = jnp.sum(jnp.where(wide, each_sum, 0.0), axis=0, keepdims=True)
    for copy in trace_parts[:probes - 1]:
        copy.wait_recv()
    red_out[...] = packed
    red_a[spot] = packed
    plane = [post(red_out, red_a.at[spot], dev) for dev in a_peers]
    fill_t(STEPS - 1)
    send_t(STEPS - 1)
    for copy in plane:
        copy.wait_recv()
    for p in range(probes):
        base = p * levels * x_chips
        part = red_a[base]
        for k in range(1, levels * x_chips):
            part = part + red_a[base + k]
        red_b[zc, p] = part
    before = list(started)
    line = [post(red_b.at[zc], red_b.at[zc], dev) for dev in b_peers]
    for copy in before:
        copy.wait_send()
    for copy in line:
        copy.wait_recv()
    total = None
    for p in range(probes):
        part = red_b[0, p]
        for k in range(1, z_chips):
            part = part + red_b[k, p]
        part = jnp.broadcast_to(part, (8, 128))
        total = part if p == 0 else jnp.where(sub_h == p, part, total)

    def column(n):
        return jnp.broadcast_to(total[:, n:n + 1], (8, 128))
    a = {pair: column(n) for pair, n in ROW.items()}
    c = [column(len(PAIRS) + j) for j in range(STEPS)]
    pivot = []
    ratio = {}
    for j in range(STEPS):
        pivot.append(1.0 / a[j, j])
        for i in range(j + 1, STEPS):
            ratio[j, i] = a[j, i] * pivot[j]
        for i in range(j + 1, STEPS):
            c[i] = c[i] - ratio[j, i] * c[j]
            for k in range(i, STEPS):
                a[i, k] = a[i, k] - ratio[j, i] * a[j, k]
    for j in range(STEPS - 1, -1, -1):
        c[j] = c[j] * pivot[j]
        for i in range(j + 1, STEPS):
            c[j] = c[j] - ratio[j, i] * c[i]
    weight = {(p, j): jnp.broadcast_to(c[j][p:p + 1], (8, 128)) for p in range(probes) for j in range(STEPS)}

    for copy in trace_parts[probes - 1:]:
        copy.wait_recv()

    def write(l):
        acc = None
        for j in range(STEPS):
            for p in range(probes):
                part = weight[p, j] * t_in[j, p, l]
                acc = part if acc is None else acc + part
        res = kap_q[l] * acc - sub_q[l]
        out_ref[src(l)] = res[:, :64]
        out_ref[src(l + H)] = pltpu.roll(res, 64, 1)[:, :64]
    each(H, 4, write)
    for copy in line:
        copy.wait_send()


def solution(mesh):
    probes, tiles, levels = (mesh.shape[a] for a in ("probe", "tile", "level"))
    x_chips = min(X_CHIPS, tiles)
    z_chips = tiles // x_chips

    def step(bits, kap, obs):
        _, L, rows, Y = bits.shape
        dims = (probes, tiles, levels, x_chips, L, Y)
        vm = lambda *lead: pltpu.VMEM((*lead, 8, Y), F32)
        dma = lambda n: pltpu.SemaphoreType.DMA((n,))
        G = L // 4
        n_sems = 9 + 5 * (STEPS - 1) + (probes * levels * x_chips - 1) + (z_chips - 1) + STEPS * (probes - 1)
        part = lambda *lead: pltpu.VMEM((*lead, L // 2, 8, 128), F32)
        scratch = [
            pltpu.VMEM((L, 8, Y), jnp.int32), vm(L), vm(L),
            vm(L + 2), vm(L), vm(L + 1), vm(L), vm(L + 2), vm(L),
            vm(L + 1), vm(L + 1), vm(L), vm(L), vm(L), vm(L),
            vm(STEPS, L + 3), vm(L + 2), vm(STEPS, L + 2), vm(L), vm(L), vm(L), vm(L), vm(L), vm(L),
            vm(3, 2, G), vm(3, 2, G), vm(STEPS - 1, 2, G), vm(STEPS - 1, 2, G),
            vm(7), vm(7), vm(2), vm(2, 2),
            vm(STEPS - 1, 2), vm(STEPS - 1, 2), vm(STEPS - 1), vm(STEPS - 1, 2),
            pltpu.VMEM((N_ROWS, 128), F32),
            pltpu.VMEM((1, 128), F32),
            pltpu.VMEM((probes * levels * x_chips, 1, 128), F32),
            pltpu.VMEM((z_chips, probes, 1, 128), F32),
            part(STEPS, probes), part(STEPS, probes), part(), part(), vm(L),
            dma(3), dma(n_sems), dma(n_sems), pltpu.SemaphoreType.REGULAR((STEPS - 1,)),
        ]
        return pl.pallas_call(
            functools.partial(kernel, dims),
            out_shape=pltpu.VMEM((L, rows, Y // probes), F32),
            in_specs=[pl.BlockSpec(memory_space=pl.ANY)] * 3,
            out_specs=pl.BlockSpec(memory_space=pltpu.VMEM),
            scratch_shapes=scratch,
            compiler_params=pltpu.CompilerParams(collective_id=0, has_side_effects=True),
        )(bits, kap, obs)

    return jax.shard_map(
        step,
        mesh=mesh,
        in_specs=(P("probe", "level", "tile", None), P("level", "tile", None), P("level", "tile", None)),
        out_specs=P("level", "tile", "probe"),
        check_vma=False,
    )
```

```python
import functools

import jax
import jax.numpy as jnp
from jax import lax
from jax.experimental import pallas as pl
from jax.experimental.pallas import tpu as pltpu
from jax.sharding import PartitionSpec as P

MESH = pl.DeviceIdType.MESH
STEPS = 4
F32 = jnp.float32
X_CHIPS = 4

PAIRS = [(i, j) for j in range(STEPS) for i in range(j + 1)]
ROW = {pair: n for n, pair in enumerate(PAIRS)}
N_ROWS = 16


def kernel(
    dims,
    bits_hbm, kap_hbm, obs_hbm, out_ref,
    bits_v, kap_v, obs_v,
    s_m, s_h, d_m, d_h, o_m, o_h,
    m_m, m_h, hg_m, hg_h, al_m, be_m,
    v_m, v_h, u_m, r_m, f_m, f_h, y_f, ks,
    halo_out, halo_in, xs_out, xs_in,
    first_out, first_in, side_out, side_in, pl_out, pl_in, ed_out, ed_in,
    gram, red_out, red_a, red_b, t_out, t_in, kap_q, sub_q, data,
    in_sem, send_sem, recv_sem, here_sem,
):
    probes, tiles, levels, x_chips, L, Y = dims
    z_chips = tiles // x_chips
    H = L // 2
    probe = lax.axis_index("probe")
    tile = lax.axis_index("tile")
    half = lax.axis_index("level")
    zc = tile // x_chips
    xc = tile - zc * x_chips
    nxt = lax.rem(tile + 1, tiles)
    prv = lax.rem(tile + tiles - 1, tiles)
    other = 1 - half
    n_a = probes * levels * x_chips
    spot = (probe * levels + half) * x_chips + xc

    loads = [
        pltpu.make_async_copy(kap_hbm, kap_v, in_sem.at[0]),
        pltpu.make_async_copy(bits_hbm.at[0], bits_v, in_sem.at[1]),
        pltpu.make_async_copy(obs_hbm, obs_v, in_sem.at[2]),
    ]
    for copy in loads:
        copy.start()

    def around(n):
        return sorted(range(1, n), key=lambda k: (-min(k, n - k), k))

    near_p = [lax.rem(probe + k, probes) for k in around(probes)]
    near_x = [tile - xc + lax.rem(xc + k, x_chips) for k in around(x_chips)]
    a_peers = [{"probe": p, "tile": t, "level": h}
               for t in near_x + [tile] for h in (other, half) for p in near_p + [probe]][:-1]
    b_peers = [{"tile": lax.rem(tile + k * x_chips, tiles)} for k in around(z_chips)]
    p_peers = near_p
    not_end = [tile < tiles - 1, tile > 0]

    def along_z(d):
        return [(zc + d < z_chips, {"tile": lax.rem(tile + d * x_chips, tiles)}),
                (zc >= d, {"tile": lax.rem(tile + tiles - d * x_chips, tiles)})]

    def signal_if(sem, pairs):
        for there, dev in pairs:
            pl.when(there)(functools.partial(
                pl.semaphore_signal, sem, inc=1, device_id=dev, device_id_type=MESH))

    def count(pairs):
        return sum(there.astype(jnp.int32) for there, _ in pairs)

    barrier = pltpu.get_barrier_semaphore()
    ends = [(not_end[0], {"tile": nxt}), (not_end[1], {"tile": prv}),
            (not_end[0], {"tile": nxt, "level": other}), (not_end[1], {"tile": prv, "level": other})]
    ends += along_z(1)
    greet = [{"level": other}] + [{"probe": p} for p in p_peers]
    signal_if(barrier, ends)
    for dev in greet:
        pl.semaphore_signal(barrier, inc=1, device_id=dev, device_id_type=MESH)

    sub = lax.broadcasted_iota(jnp.int32, (8, Y), 0)
    lane_h = lax.broadcasted_iota(jnp.int32, (8, 128), 1)
    sub_h = lax.broadcasted_iota(jnp.int32, (8, 128), 0)
    has_next = (tile < tiles - 1).astype(F32)
    has_prev = (tile > 0).astype(F32)
    mask_h = jnp.where(sub < 2, has_next, jnp.where(sub >= 6, has_prev, 0.0))
    zero = jnp.zeros((8, Y), F32)

    def src(l):
        return half * (L - 1) + (1 - 2 * half) * l

    def send(src_ref, dst_ref, ssem, rsem, dev):
        copy = pltpu.make_async_remote_copy(
            src_ref=src_ref, dst_ref=dst_ref, send_sem=ssem, recv_sem=rsem,
            device_id=dev, device_id_type=MESH)
        copy.start()
        return copy

    started = []
    counter = [0]

    def post(src_ref, dst_ref, dev):
        n = counter[0]
        counter[0] += 1
        copy = send(src_ref, dst_ref, send_sem.at[n], recv_sem.at[n], dev)
        started.append(copy)
        return copy

    class Ended:
        def __init__(self, copy, goes, comes):
            self.copy, self.goes, self.comes = copy, goes, comes
            pl.when(goes)(copy.start)

        def wait_send(self):
            pl.when(self.goes)(self.copy.wait_send)

        def wait_recv(self):
            pl.when(self.comes)(self.copy.wait_recv)

    def post_to(side, src_ref, dst_ref, dev):
        n = counter[0]
        counter[0] += 1
        copy = pltpu.make_async_remote_copy(
            src_ref=src_ref, dst_ref=dst_ref, send_sem=send_sem.at[n], recv_sem=recv_sem.at[n],
            device_id=dev, device_id_type=MESH)
        copy = Ended(copy, not_end[side], not_end[1 - side])
        started.append(copy)
        return copy

    def loop(n, chunk, body, init=0):
        chunk = min(chunk, n)

        def step(b, carry):
            for k in range(chunk):
                carry = body(b * chunk + k, carry)
            return carry

        return lax.fori_loop(0, n // chunk, step, init)

    def each(n, chunk, body):
        def step(l, carry):
            body(l)
            return carry
        loop(n, chunk, step)

    def pack_rows(rows, g, up_ref, dn_ref):
        up = rows[3]
        dn = pltpu.roll(rows[3], 6, 0)
        for k in (2, 1, 0):
            up = jnp.where(sub < 2 * k + 2, pltpu.roll(rows[k], 2 * k + 2, 0), up)
            dn = jnp.where(sub < 2 * k + 2, pltpu.roll(rows[k], 2 * k, 0) if k else rows[k], dn)
        up_ref[g] = up
        dn_ref[g] = dn

    def pack(put, up_ref, dn_ref):
        each(L // 4, 2, lambda g: pack_rows([put(4 * g + k) for k in range(4)], g, up_ref, dn_ref))

    def beside_rows(a_ref, b_ref, g):
        a = a_ref[g]
        b = b_ref[g]
        out = []
        for k in range(4):
            ra = pltpu.roll(a, 6 - 2 * k, 0) if k < 3 else a
            rb = pltpu.roll(b, 8 - 2 * k, 0) if k else b
            out.append(jnp.where(sub >= 4, ra, rb))
        return out

    def unpack(a_ref, b_ref, write):
        def body(g):
            for k, x in enumerate(beside_rows(a_ref, b_ref, g)):
                write(4 * g + k, x)
        each(L // 4, 2, body)

    def pack_outer(rows, g, up_ref, dn_ref):
        up = rows[7]
        dn = pltpu.roll(rows[7], 7, 0)
        for k in range(6, -1, -1):
            up = jnp.where(sub <= k, pltpu.roll(rows[k], k + 1, 0), up)
            dn = jnp.where(sub <= k, pltpu.roll(rows[k], k, 0) if k else rows[k], dn)
        up_ref[g] = up
        dn_ref[g] = dn

    def beside_outer(a_ref, b_ref, g):
        a = a_ref[g]
        b = b_ref[g]
        out = []
        for k in range(8):
            ra = pltpu.roll(a, 7 - k, 0) if k < 7 else a
            rb = pltpu.roll(b, 8 - k, 0) if k else b
            out.append(jnp.where(sub >= 4, ra, rb))
        return out

    first_lane = lane_h == 0
    last_lane = lane_h == 127

    def sides(a):
        parts = [a[:, n * 128:(n + 1) * 128] for n in range(Y // 128)]
        right = [pltpu.roll(x, 1, 1) for x in parts]
        left = [pltpu.roll(x, 127, 1) for x in parts]
        out = []
        for n in range(len(parts)):
            before = jnp.where(first_lane, right[n - 1] if n else 0.0, right[n])
            after = jnp.where(last_lane, left[n + 1] if n + 1 < len(parts) else 0.0, left[n])
            out.append(before + after)
        return jnp.concatenate(out, axis=1)

    def beside(a, b):
        up = jnp.where(sub == 0, pltpu.roll(b, 1, 0), pltpu.roll(a, 1, 0))
        dn = jnp.where(sub == 7, pltpu.roll(b, 7, 0), pltpu.roll(a, 7, 0))
        return (up + dn) + sides(a)

    def factor(d_ref, m_ref, hg_ref):
        m_ref[0] = zero

        def up(l, m):
            m = 2.0 / (d_ref[l] - 2.0 * m)
            m_ref[l + 1] = m
            return m
        last = loop(L, 8, up, zero)

        def down(k, h):
            l = L - 1 - k
            h = m_ref[l + 1] * h
            hg_ref[l] = h
            return h
        loop(L, 8, down, zero + 1.0)

        def again(l, g):
            g = 0.5 * hg_ref[l] + m_ref[l] * g
            hg_ref[l] = g
            return g
        return last, loop(L, 8, again, zero)

    def solve(read, size, m_ref, f_ref, y_ref, waits=()):
        def fwd(g, f):
            for k, r in enumerate(read(g)):
                l = g * size + k
                f = 0.5 * r + m_ref[l] * f
                f_ref[l] = f
            return f
        pieces = max(len(waits), 1)
        per = L // size // pieces
        first = zero
        for p in range(pieces):
            for copy in waits[p] if waits else ():
                copy.wait_recv()
            first = loop(per, max(16 // size, 1), functools.partial(lambda at, g, f: fwd(at + g, f), p * per), first)

        def back(k, y):
            l = L - 1 - k
            y = m_ref[l + 1] * (f_ref[l] + y)
            y_ref[l] = y
            return y
        loop(L, 16, back, zero)
        return first

    def passes(read, size, m_ref, f_ref, waits=()):
        first = solve(read, size, m_ref, f_ref, y_f, waits)

        def again(l, g):
            g = 0.5 * y_f[l] + m_ref[l] * g
            f_ref[l] = g
            return g
        return first, loop(L, 16, again, zero)

    def edges(a, b):
        inside = jnp.where(sub < 4, pltpu.roll(b, 2, 0), pltpu.roll(b, 6, 0))
        return jnp.where((sub >= 2) & (sub < 6), inside, a)

    def beyond(a, b):
        return jnp.where(sub >= 4, a, b), jnp.where(sub >= 4, pltpu.roll(a, 2, 0), pltpu.roll(b, 6, 0))

    def join(const, own, far):
        mo, ho, mp, hp, inv = const
        (fo, go), (fp, gp) = own, far
        x = mo * (fo + mp * fp) * inv
        xi = mp * (fp + mo * fo) * inv
        g = go + xi * ho
        gf = gp + x * hp
        w = mo * (g + mp * gf) * inv
        eta = mp * (gf + mo * g) * inv
        return xi, w, eta

    def finish_m(j, const, own, far, dp):
        xi, w, eta = join(const, own, far)
        next_one = 0.5 * (dp * eta - xi) - w
        v_m[j, L + 1] = eta if j == 0 else eta - v_m[j - 1, L + 1]
        v_m[j, L + 2] = next_one if j == 0 else next_one - v_m[j - 1, L + 2]

        def down(k, w):
            l = L - 1 - k
            w = m_m[l + 1] * ((f_m[l] + xi * hg_m[l]) + w)
            v_m[j, l + 1] = w if j == 0 else w - v_m[j - 1, l + 1]
            return w
        loop(L, 16, down, eta)

    def finish_h(j, const, own, far):
        xi, w, eta = join(const, own, far)
        v_h[L + 1] = eta if j == 0 else eta - v_h[L + 1]

        def down(k, w):
            l = L - 1 - k
            w = m_h[l + 1] * ((f_h[l] + xi * hg_h[l]) + w)
            v_h[l + 1] = w if j == 0 else w - v_h[l + 1]
            return w
        loop(L, 16, down, eta)

    def inner_k(j):
        def body(l):
            a = v_m[j, l + 1]
            rows = jnp.where(sub == 0, 0.0, pltpu.roll(a, 1, 0)) + jnp.where(sub == 7, 0.0, pltpu.roll(a, 7, 0))
            u_m[j, l + 1] = (d_m[l] * a - (rows + sides(a))) - 2.0 * (v_m[j, l] + v_m[j, l + 2])
        each(L, 8, body)
        if j < STEPS - 1:
            body(L)

    def outer_dots(j):
        def body(l, carry):
            b = v_h[l + 1]
            add = jnp.where(sub == 0, pltpu.roll(b, 1, 0), jnp.where(sub == 7, pltpu.roll(b, 7, 0), 0.0))
            u = u_m[j, l + 1] - add
            u_m[j, l + 1] = u
            out = [carry[i] + u * u_m[i, l + 1] for i in range(j)]
            return tuple(out + [carry[j] + u * u])
        sums = loop(L, 8, body, (zero,) * (j + 1))
        for i in range(j + 1):
            n = ROW[i, j]
            gram[n:n + 1] = fold(sums[i])

    def one_row(j):
        return j == STEPS - 2 and L % 16 == 0

    def advance(j):
        size = 8 if one_row(j) else 4
        per = L // size // 2
        wrap = pack_outer if one_row(j) else pack_rows

        def settle(l):
            b = v_h[l + 1]
            a = v_m[j, l + 1]
            from_up, from_dn = pltpu.roll(b, 1, 0), pltpu.roll(b, 7, 0)
            u = u_m[j, l + 1] - jnp.where(sub == 0, from_up, jnp.where(sub == 7, from_dn, 0.0))
            u_m[j, l + 1] = u
            up = jnp.where(sub == 0, pltpu.roll(a, 1, 0), from_up)
            dn = jnp.where(sub == 7, pltpu.roll(a, 7, 0), from_dn)
            outer = (d_h[l] * b - ((up + dn) + sides(b))) - 2.0 * (v_h[l] + v_h[l + 2])
            return u, mask_h * outer

        def form(g, carry):
            before, here, outer, fo, go = carry
            tiles_r = []
            for k in range(size):
                l = size * g + k
                after, next_outer = settle(l + 1)
                r = (d_m[l] * here - beside(here, outer)) - 2.0 * (before + after)
                r_m[l] = r
                fo = fo + al_m[l] * r
                go = go + be_m[l] * r
                tiles_r.append(r)
                before, here, outer = here, after, next_outer
            wrap(tiles_r, g, xs_out.at[j, 0], xs_out.at[j, 1])
            return before, here, outer, fo, go

        state = (zero,) + settle(0) + (zero, zero)
        rows = []
        for p in range(2):
            state = loop(per, 8 // size, functools.partial(lambda at, g, c: form(at + g, c), p * per), state)
            if p == 1:
                own = state[3:]
                ed_out[j] = edges(own[0], own[1])
                pl_out[j, 0] = own[0]
                pl_out[j, 1] = own[1]
                planes = [
                    post_to(0, ed_out.at[j], ed_in.at[j, 0], {"tile": nxt, "level": other}),
                    post_to(1, ed_out.at[j], ed_in.at[j, 1], {"tile": prv, "level": other}),
                    post(pl_out.at[j], pl_in.at[j], {"level": other}),
                ]
            cut = pl.ds(p * per, per)
            rows.append([
                post_to(0, xs_out.at[j, 0, cut], xs_in.at[j, 0, cut], {"tile": nxt}),
                post_to(1, xs_out.at[j, 1, cut], xs_in.at[j, 1, cut], {"tile": prv}),
            ])
        return own, planes, rows

    def fold(acc):
        row = jnp.sum(acc, axis=0, keepdims=True)
        total = row[:, :128]
        for n in range(1, Y // 128):
            total = total + row[:, n * 128:(n + 1) * 128]
        return total

    def side_dot(j):
        n = len(PAIRS) + j
        gram[n:n + 1] = fold(loop(L, 8, lambda l, acc: acc + v_m[j, l + 1] * s_m[l + 1], zero))

    def dots(j):
        def body(l, carry):
            u = u_m[j, l + 1]
            return tuple(carry[i] + u * u_m[i, l + 1] for i in range(j + 1))
        sums = loop(L, 8, body, (zero,) * (j + 1))
        for i in range(j + 1):
            n = ROW[i, j]
            gram[n:n + 1] = fold(sums[i])

    low = lane_h < 64

    def quarter(q, top, bot):
        n = q // 2
        p, b = top[:, n * 128:(n + 1) * 128], bot[:, n * 128:(n + 1) * 128]
        if q % 2 == 0:
            return jnp.where(low, p, pltpu.roll(b, 64, 1))
        return jnp.where(low, pltpu.roll(p, 64, 1), b)

    def fill_t(j):
        def body(l):
            top = v_m[j, l + 1] * ks[l] + u_m[j, l + 1] * s_m[l + 1]
            k = l + H
            bot = v_m[j, k + 1] * ks[k] + u_m[j, k + 1] * s_m[k + 1]
            for q in range(probes):
                t_out[j, q, l] = quarter(q, top, bot)
            t_in[j, probe, l] = t_out[j, probe, l]
        each(H, 2, body)

    trace_parts = []

    def send_t(j):
        for g in p_peers:
            trace_parts.append(post(t_out.at[j, g], t_in.at[j, probe], {"probe": g}))

    loads[0].wait()

    for side in range(2):
        @pl.when(jnp.logical_not(not_end[1 - side]))
        def _():
            def clear(g):
                for k in range(3):
                    halo_in[k, side, g] = zero
                for k in range(STEPS - 1):
                    xs_in[k, side, g] = zero
            each(L // 4, 1, clear)
            for k in range(2):
                side_in[side, k] = zero
            for k in range(STEPS - 1):
                ed_in[k, side] = zero

    def put_d(l):
        d = kap_v[src(l)] + 8.0
        d_m[l] = d
        return d
    pack(put_d, halo_out.at[0, 0], halo_out.at[0, 1])
    pl.semaphore_wait(barrier, len(greet) + count(ends))
    halo_d = [
        post_to(0, halo_out.at[0, 0], halo_in.at[0, 0], {"tile": nxt}),
        post_to(1, halo_out.at[0, 1], halo_in.at[0, 1], {"tile": prv}),
    ]
    mo_m, ho_m = factor(d_m, m_m, hg_m)
    loads[1].wait()

    def put_s(l):
        s = (2 * bits_v[src(l)] - 1).astype(F32)
        s_m[l + 1] = s
        return s
    pack(put_s, halo_out.at[1, 0], halo_out.at[1, 1])
    own_m = passes(lambda l: [s_m[l + 1]], 1, m_m, f_m)
    loads[2].wait()
    side_out[0] = edges(mo_m, ho_m)
    side_out[1] = edges(own_m[0], own_m[1])
    for n, plane in enumerate((mo_m, ho_m, own_m[0], own_m[1], d_m[L - 1], s_m[L], obs_v[src(L - 1)])):
        first_out[n] = plane
    far = [
        post_to(0, side_out, side_in.at[0], {"tile": nxt, "level": other}),
        post_to(1, side_out, side_in.at[1], {"tile": prv, "level": other}),
        post(first_out, first_in, {"level": other}),
    ]
    halo_s = [
        post_to(0, halo_out.at[1, 0], halo_in.at[1, 0], {"tile": nxt}),
        post_to(1, halo_out.at[1, 1], halo_in.at[1, 1], {"tile": prv}),
    ]
    s_m[0] = zero
    o_m[0] = zero
    for j in range(STEPS):
        v_m[j, 0] = zero
        u_m[j, 0] = zero
    v_h[0] = zero
    v_h[L + 2] = zero
    d_h[L] = zero

    def put_o(l):
        o = obs_v[src(l)]
        o_m[l + 1] = o
        return o
    pack(put_o, halo_out.at[2, 0], halo_out.at[2, 1])
    halo_o = [
        post_to(0, halo_out.at[2, 0], halo_in.at[2, 0], {"tile": nxt}),
        post_to(1, halo_out.at[2, 1], halo_in.at[2, 1], {"tile": prv}),
    ]

    def weigh(k, x):
        l = L - 1 - k
        al_m[l] = x
        return m_m[l] * x
    loop(L, 16, weigh, zero + 0.5)
    solve(lambda l: [al_m[l]], 1, m_m, r_m, be_m)

    for copy in halo_d:
        copy.wait_recv()

    def put_dh(l, x):
        d_h[l] = jnp.where(mask_h > 0.0, x, 8.0)
    unpack(halo_in.at[0, 0], halo_in.at[0, 1], put_dh)
    mo_h, ho_h = factor(d_h, m_h, hg_h)

    far[2].wait_recv()
    mp_m, hp_m, fp_m, gp_m, dp_m = (first_in[n] for n in range(5))
    d_m[L] = dp_m
    s_m[L + 1] = first_in[5]
    o_m[L + 1] = first_in[6]
    const_m = (mo_m, ho_m, mp_m, hp_m, 1.0 / (1.0 - mo_m * mp_m))
    finish_m(0, const_m, own_m, (fp_m, gp_m), dp_m)
    inner_k(0)

    for copy in halo_s:
        copy.wait_recv()

    def read_sh(g):
        rows = [x * mask_h for x in beside_rows(halo_in.at[1, 0], halo_in.at[1, 1], g)]
        for k, x in enumerate(rows):
            s_h[4 * g + k] = x
        return rows
    own_h = passes(read_sh, 4, m_h, f_h)
    for copy in far[:2]:
        copy.wait_recv()

    mp_h, hp_h = beyond(side_in[0, 0], side_in[1, 0])
    fp_h, gp_h = beyond(side_in[0, 1], side_in[1, 1])
    const_h = (mo_h, ho_h, mp_h, hp_h, 1.0 / (1.0 - mo_h * mp_h))
    finish_h(0, const_h, own_h, (mask_h * fp_h, mask_h * gp_h))
    own_m, planes, rows = advance(0)

    odd = lax.rem(probe, 2) == 1
    upper = probe // 2 == 1

    def mine(top, bot):
        out = [jnp.where(odd, quarter(2 * n + 1, top, bot), quarter(2 * n, top, bot)) for n in range(Y // 128)]
        return jnp.where(upper, out[1], out[0])

    def side_terms():
        for copy in halo_o:
            copy.wait_recv()

        def put_oh(l, x):
            o_h[l] = x * mask_h
        unpack(halo_in.at[2, 0], halo_in.at[2, 1], put_oh)

        def body(l):
            a = s_m[l + 1]
            ks[l] = (d_m[l] * a - beside(a, s_h[l])) - 2.0 * (s_m[l] + s_m[l + 2])
            b = o_m[l + 1]
            ko = (d_m[l] * b - beside(b, o_h[l])) - 2.0 * (o_m[l] + o_m[l + 2])
            data[l] = kap_v[src(l)] * (2.0 * b * ko)
        each(L, 4, body)

    def quarters():
        def body(l):
            kap_q[l] = mine(kap_v[src(l)], kap_v[src(l + H)]) * (1.0 / probes)
            sub_q[l] = mine(data[l], data[l + H])
        each(H, 2, body)

    for j in range(1, STEPS):
        n = j - 1
        signal_if(here_sem.at[n], along_z(2 ** n))
        passes(lambda l: [r_m[l]], 1, m_m, f_m)
        dots(j - 1)
        side_dot(j - 1)
        if j == 1:
            side_terms()
        if j == 2:
            quarters()
        fill_t(j - 1)
        planes[2].wait_recv()
        finish_m(j, const_m, own_m, (pl_in[n, 0], pl_in[n, 1]), dp_m)
        inner_k(j)
        if j == STEPS - 1:
            side_dot(j)
            for i in range(len(PAIRS) + STEPS, N_ROWS):
                gram[i:i + 1] = jnp.zeros((1, 128), F32)
        beside_r = beside_outer if one_row(j - 1) else beside_rows

        def read_rh(g):
            return [x * mask_h for x in beside_r(xs_in.at[n, 0], xs_in.at[n, 1], g)]
        own_h = passes(read_rh, 8 if one_row(j - 1) else 4, m_h, f_h, rows)
        for copy in planes[:2]:
            copy.wait_recv()
        pl.semaphore_wait(here_sem.at[n], count(along_z(2 ** n)))
        send_t(j - 1)
        fp_h, gp_h = beyond(ed_in[n, 0], ed_in[n, 1])
        finish_h(j, const_h, own_h, (mask_h * fp_h, mask_h * gp_h))
        if j < STEPS - 1:
            own_m, planes, rows = advance(j)
        else:
            outer_dots(j)

    wide = lax.broadcasted_iota(jnp.int32, (N_ROWS, 128), 1) == lax.broadcasted_iota(jnp.int32, (N_ROWS, 128), 0)
    each_sum = jnp.sum(gram[...], axis=1, keepdims=True)
    packed = jnp.sum(jnp.where(wide, each_sum, 0.0), axis=0, keepdims=True)
    for copy in trace_parts[:probes - 1]:
        copy.wait_recv()
    red_out[...] = packed
    red_a[spot] = packed
    plane = [post(red_out, red_a.at[spot], dev) for dev in a_peers]
    fill_t(STEPS - 1)
    send_t(STEPS - 1)
    for copy in plane:
        copy.wait_recv()
    for p in range(probes):
        base = p * levels * x_chips
        part = red_a[base]
        for k in range(1, levels * x_chips):
            part = part + red_a[base + k]
        red_b[zc, p] = part
    before = list(started)
    line = [post(red_b.at[zc], red_b.at[zc], dev) for dev in b_peers]
    for copy in before:
        copy.wait_send()
    for copy in line:
        copy.wait_recv()
    total = None
    for p in range(probes):
        part = red_b[0, p]
        for k in range(1, z_chips):
            part = part + red_b[k, p]
        part = jnp.broadcast_to(part, (8, 128))
        total = part if p == 0 else jnp.where(sub_h == p, part, total)

    def column(n):
        return jnp.broadcast_to(total[:, n:n + 1], (8, 128))
    a = {pair: column(n) for pair, n in ROW.items()}
    c = [column(len(PAIRS) + j) for j in range(STEPS)]
    pivot = []
    ratio = {}
    for j in range(STEPS):
        pivot.append(1.0 / a[j, j])
        for i in range(j + 1, STEPS):
            ratio[j, i] = a[j, i] * pivot[j]
        for i in range(j + 1, STEPS):
            c[i] = c[i] - ratio[j, i] * c[j]
            for k in range(i, STEPS):
                a[i, k] = a[i, k] - ratio[j, i] * a[j, k]
    for j in range(STEPS - 1, -1, -1):
        c[j] = c[j] * pivot[j]
        for i in range(j + 1, STEPS):
            c[j] = c[j] - ratio[j, i] * c[i]
    weight = {(p, j): jnp.broadcast_to(c[j][p:p + 1], (8, 128)) for p in range(probes) for j in range(STEPS)}

    for copy in trace_parts[probes - 1:]:
        copy.wait_recv()

    def write(l):
        acc = None
        for j in range(STEPS):
            for p in range(probes):
                part = weight[p, j] * t_in[j, p, l]
                acc = part if acc is None else acc + part
        res = kap_q[l] * acc - sub_q[l]
        out_ref[src(l)] = res[:, :64]
        out_ref[src(l + H)] = pltpu.roll(res, 64, 1)[:, :64]
    each(H, 4, write)
    for copy in line:
        copy.wait_send()


def solution(mesh):
    probes, tiles, levels = (mesh.shape[a] for a in ("probe", "tile", "level"))
    x_chips = min(X_CHIPS, tiles)
    z_chips = tiles // x_chips

    def step(bits, kap, obs):
        _, L, rows, Y = bits.shape
        dims = (probes, tiles, levels, x_chips, L, Y)
        vm = lambda *lead: pltpu.VMEM((*lead, 8, Y), F32)
        dma = lambda n: pltpu.SemaphoreType.DMA((n,))
        G = L // 4
        n_sems = 9 + 7 * (STEPS - 1) + (probes * levels * x_chips - 1) + (z_chips - 1) + STEPS * (probes - 1)
        part = lambda *lead: pltpu.VMEM((*lead, L // 2, 8, 128), F32)
        scratch = [
            pltpu.VMEM((L, 8, Y), jnp.int32), vm(L), vm(L),
            vm(L + 2), vm(L), vm(L + 1), vm(L + 1), vm(L + 2), vm(L),
            vm(L + 1), vm(L + 1), vm(L), vm(L), vm(L), vm(L),
            vm(STEPS, L + 3), vm(L + 3), vm(STEPS, L + 2), vm(L), vm(L), vm(L), vm(L), vm(L),
            vm(3, 2, G), vm(3, 2, G), vm(STEPS - 1, 2, G), vm(STEPS - 1, 2, G),
            vm(7), vm(7), vm(2), vm(2, 2),
            vm(STEPS - 1, 2), vm(STEPS - 1, 2), vm(STEPS - 1), vm(STEPS - 1, 2),
            pltpu.VMEM((N_ROWS, 128), F32),
            pltpu.VMEM((1, 128), F32),
            pltpu.VMEM((probes * levels * x_chips, 1, 128), F32),
            pltpu.VMEM((z_chips, probes, 1, 128), F32),
            part(STEPS, probes), part(STEPS, probes), part(), part(), vm(L),
            dma(3), dma(n_sems), dma(n_sems), pltpu.SemaphoreType.REGULAR((STEPS - 1,)),
        ]
        return pl.pallas_call(
            functools.partial(kernel, dims),
            out_shape=pltpu.VMEM((L, rows, Y // probes), F32),
            in_specs=[pl.BlockSpec(memory_space=pl.ANY)] * 3,
            out_specs=pl.BlockSpec(memory_space=pltpu.VMEM),
            scratch_shapes=scratch,
            compiler_params=pltpu.CompilerParams(collective_id=0, has_side_effects=True),
        )(bits, kap, obs)

    return jax.shard_map(
        step,
        mesh=mesh,
        in_specs=(P("probe", "level", "tile", None), P("level", "tile", None), P("level", "tile", None)),
        out_specs=P("level", "tile", "probe"),
        check_vma=False,
    )
```

```python
import functools

import jax
import jax.numpy as jnp
from jax import lax
from jax.experimental import pallas as pl
from jax.experimental.pallas import tpu as pltpu
from jax.sharding import PartitionSpec as P

MESH = pl.DeviceIdType.MESH
STEPS = 4
F32 = jnp.float32
X_CHIPS = 4

PAIRS = [(i, j) for j in range(STEPS) for i in range(j + 1)]
ROW = {pair: n for n, pair in enumerate(PAIRS)}
N_ROWS = 16


def kernel(
    dims,
    bits_hbm, kap_hbm, obs_hbm, out_ref,
    bits_v, kap_v, obs_v,
    s_m, s_h, d_m, d_h, o_m, o_h,
    m_m, m_h, hg_m, hg_h, al_m, be_m,
    v_m, v_h, u_m, r_m, f_m, f_h, y_f, ks,
    halo_out, halo_in, xs_out, xs_in,
    first_out, first_in, side_out, side_in, pl_out, pl_in, ed_out, ed_in,
    gram, red_out, red_a, red_b, t_out, t_in, kap_q, sub_q, data,
    in_sem, send_sem, recv_sem, here_sem,
):
    probes, tiles, levels, x_chips, L, Y = dims
    z_chips = tiles // x_chips
    H = L // 2
    probe = lax.axis_index("probe")
    tile = lax.axis_index("tile")
    half = lax.axis_index("level")
    zc = tile // x_chips
    xc = tile - zc * x_chips
    nxt = lax.rem(tile + 1, tiles)
    prv = lax.rem(tile + tiles - 1, tiles)
    other = 1 - half
    n_a = probes * levels * x_chips
    spot = (probe * levels + half) * x_chips + xc

    loads = [
        pltpu.make_async_copy(kap_hbm, kap_v, in_sem.at[0]),
        pltpu.make_async_copy(bits_hbm.at[0], bits_v, in_sem.at[1]),
        pltpu.make_async_copy(obs_hbm, obs_v, in_sem.at[2]),
    ]
    for copy in loads:
        copy.start()

    def around(n):
        return sorted(range(1, n), key=lambda k: (-min(k, n - k), k))

    near_p = [lax.rem(probe + k, probes) for k in around(probes)]
    near_x = [tile - xc + lax.rem(xc + k, x_chips) for k in around(x_chips)]
    a_peers = [{"probe": p, "tile": t, "level": h}
               for t in near_x + [tile] for h in (other, half) for p in near_p + [probe]][:-1]
    b_peers = [{"tile": lax.rem(tile + k * x_chips, tiles)} for k in around(z_chips)]
    p_peers = near_p
    not_end = [tile < tiles - 1, tile > 0]

    def along_z(d):
        return [(zc + d < z_chips, {"tile": lax.rem(tile + d * x_chips, tiles)}),
                (zc >= d, {"tile": lax.rem(tile + tiles - d * x_chips, tiles)})]

    def signal_if(sem, pairs):
        for there, dev in pairs:
            pl.when(there)(functools.partial(
                pl.semaphore_signal, sem, inc=1, device_id=dev, device_id_type=MESH))

    def count(pairs):
        return sum(there.astype(jnp.int32) for there, _ in pairs)

    barrier = pltpu.get_barrier_semaphore()
    ends = [(not_end[0], {"tile": nxt}), (not_end[1], {"tile": prv}),
            (not_end[0], {"tile": nxt, "level": other}), (not_end[1], {"tile": prv, "level": other})]
    ends += along_z(1)
    greet = [{"level": other}] + [{"probe": p} for p in p_peers]
    signal_if(barrier, ends)
    for dev in greet:
        pl.semaphore_signal(barrier, inc=1, device_id=dev, device_id_type=MESH)

    sub = lax.broadcasted_iota(jnp.int32, (8, Y), 0)
    lane_h = lax.broadcasted_iota(jnp.int32, (8, 128), 1)
    sub_h = lax.broadcasted_iota(jnp.int32, (8, 128), 0)
    has_next = (tile < tiles - 1).astype(F32)
    has_prev = (tile > 0).astype(F32)
    mask_h = jnp.where(sub < 2, has_next, jnp.where(sub >= 6, has_prev, 0.0))
    zero = jnp.zeros((8, Y), F32)

    def src(l):
        return half * (L - 1) + (1 - 2 * half) * l

    def send(src_ref, dst_ref, ssem, rsem, dev):
        copy = pltpu.make_async_remote_copy(
            src_ref=src_ref, dst_ref=dst_ref, send_sem=ssem, recv_sem=rsem,
            device_id=dev, device_id_type=MESH)
        copy.start()
        return copy

    started = []
    counter = [0]

    def post(src_ref, dst_ref, dev):
        n = counter[0]
        counter[0] += 1
        copy = send(src_ref, dst_ref, send_sem.at[n], recv_sem.at[n], dev)
        started.append(copy)
        return copy

    class Ended:
        def __init__(self, copy, goes, comes):
            self.copy, self.goes, self.comes = copy, goes, comes
            pl.when(goes)(copy.start)

        def wait_send(self):
            pl.when(self.goes)(self.copy.wait_send)

        def wait_recv(self):
            pl.when(self.comes)(self.copy.wait_recv)

    def post_to(side, src_ref, dst_ref, dev):
        n = counter[0]
        counter[0] += 1
        copy = pltpu.make_async_remote_copy(
            src_ref=src_ref, dst_ref=dst_ref, send_sem=send_sem.at[n], recv_sem=recv_sem.at[n],
            device_id=dev, device_id_type=MESH)
        copy = Ended(copy, not_end[side], not_end[1 - side])
        started.append(copy)
        return copy

    def loop(n, chunk, body, init=0):
        chunk = min(chunk, n)

        def step(b, carry):
            for k in range(chunk):
                carry = body(b * chunk + k, carry)
            return carry

        return lax.fori_loop(0, n // chunk, step, init)

    def each(n, chunk, body):
        def step(l, carry):
            body(l)
            return carry
        loop(n, chunk, step)

    def pack_rows(rows, g, up_ref, dn_ref):
        up = rows[3]
        dn = pltpu.roll(rows[3], 6, 0)
        for k in (2, 1, 0):
            up = jnp.where(sub < 2 * k + 2, pltpu.roll(rows[k], 2 * k + 2, 0), up)
            dn = jnp.where(sub < 2 * k + 2, pltpu.roll(rows[k], 2 * k, 0) if k else rows[k], dn)
        up_ref[g] = up
        dn_ref[g] = dn

    def pack(put, up_ref, dn_ref):
        each(L // 4, 2, lambda g: pack_rows([put(4 * g + k) for k in range(4)], g, up_ref, dn_ref))

    def beside_rows(a_ref, b_ref, g):
        a = a_ref[g]
        b = b_ref[g]
        out = []
        for k in range(4):
            ra = pltpu.roll(a, 6 - 2 * k, 0) if k < 3 else a
            rb = pltpu.roll(b, 8 - 2 * k, 0) if k else b
            out.append(jnp.where(sub >= 4, ra, rb))
        return out

    def unpack(a_ref, b_ref, write):
        def body(g):
            for k, x in enumerate(beside_rows(a_ref, b_ref, g)):
                write(4 * g + k, x)
        each(L // 4, 2, body)

    def pack_outer(rows, g, up_ref, dn_ref):
        up = rows[7]
        dn = pltpu.roll(rows[7], 7, 0)
        for k in range(6, -1, -1):
            up = jnp.where(sub <= k, pltpu.roll(rows[k], k + 1, 0), up)
            dn = jnp.where(sub <= k, pltpu.roll(rows[k], k, 0) if k else rows[k], dn)
        up_ref[g] = up
        dn_ref[g] = dn

    def beside_outer(a_ref, b_ref, g):
        a = a_ref[g]
        b = b_ref[g]
        out = []
        for k in range(8):
            ra = pltpu.roll(a, 7 - k, 0) if k < 7 else a
            rb = pltpu.roll(b, 8 - k, 0) if k else b
            out.append(jnp.where(sub >= 4, ra, rb))
        return out

    first_lane = lane_h == 0
    last_lane = lane_h == 127

    def sides(a):
        parts = [a[:, n * 128:(n + 1) * 128] for n in range(Y // 128)]
        right = [pltpu.roll(x, 1, 1) for x in parts]
        left = [pltpu.roll(x, 127, 1) for x in parts]
        out = []
        for n in range(len(parts)):
            before = jnp.where(first_lane, right[n - 1] if n else 0.0, right[n])
            after = jnp.where(last_lane, left[n + 1] if n + 1 < len(parts) else 0.0, left[n])
            out.append(before + after)
        return jnp.concatenate(out, axis=1)

    def beside(a, b):
        up = jnp.where(sub == 0, pltpu.roll(b, 1, 0), pltpu.roll(a, 1, 0))
        dn = jnp.where(sub == 7, pltpu.roll(b, 7, 0), pltpu.roll(a, 7, 0))
        return (up + dn) + sides(a)

    def factor(d_ref, m_ref, hg_ref):
        m_ref[0] = zero

        def up(l, m):
            m = 2.0 / (d_ref[l] - 2.0 * m)
            m_ref[l + 1] = m
            return m
        last = loop(L, 8, up, zero)

        def down(k, h):
            l = L - 1 - k
            h = m_ref[l + 1] * h
            hg_ref[l] = h
            return h
        loop(L, 8, down, zero + 1.0)

        def again(l, g):
            g = 0.5 * hg_ref[l] + m_ref[l] * g
            hg_ref[l] = g
            return g
        return last, loop(L, 8, again, zero)

    def solve(read, size, m_ref, f_ref, y_ref, waits=()):
        def fwd(g, f):
            for k, r in enumerate(read(g)):
                l = g * size + k
                f = 0.5 * r + m_ref[l] * f
                f_ref[l] = f
            return f
        pieces = max(len(waits), 1)
        per = L // size // pieces
        first = zero
        for p in range(pieces):
            for copy in waits[p] if waits else ():
                copy.wait_recv()
            first = loop(per, max(16 // size, 1), functools.partial(lambda at, g, f: fwd(at + g, f), p * per), first)

        def back(k, y):
            l = L - 1 - k
            y = m_ref[l + 1] * (f_ref[l] + y)
            y_ref[l] = y
            return y
        loop(L, 16, back, zero)
        return first

    def passes(read, size, m_ref, f_ref, waits=()):
        first = solve(read, size, m_ref, f_ref, y_f, waits)

        def again(l, g):
            g = 0.5 * y_f[l] + m_ref[l] * g
            f_ref[l] = g
            return g
        return first, loop(L, 16, again, zero)

    def edges(a, b):
        inside = jnp.where(sub < 4, pltpu.roll(b, 2, 0), pltpu.roll(b, 6, 0))
        return jnp.where((sub >= 2) & (sub < 6), inside, a)

    def beyond(a, b):
        return jnp.where(sub >= 4, a, b), jnp.where(sub >= 4, pltpu.roll(a, 2, 0), pltpu.roll(b, 6, 0))

    def join(const, own, far):
        mo, ho, mp, hp, inv = const
        (fo, go), (fp, gp) = own, far
        x = mo * (fo + mp * fp) * inv
        xi = mp * (fp + mo * fo) * inv
        g = go + xi * ho
        gf = gp + x * hp
        w = mo * (g + mp * gf) * inv
        eta = mp * (gf + mo * g) * inv
        return xi, w, eta

    def finish_m(j, const, own, far, dp):
        xi, w, eta = join(const, own, far)
        next_one = 0.5 * (dp * eta - xi) - w
        v_m[j, L + 1] = eta if j == 0 else eta - v_m[j - 1, L + 1]
        v_m[j, L + 2] = next_one if j == 0 else next_one - v_m[j - 1, L + 2]

        def down(k, w):
            l = L - 1 - k
            w = m_m[l + 1] * ((f_m[l] + xi * hg_m[l]) + w)
            v_m[j, l + 1] = w if j == 0 else w - v_m[j - 1, l + 1]
            return w
        loop(L, 16, down, eta)

    def finish_h(j, const, own, far):
        xi, w, eta = join(const, own, far)
        v_h[L + 1] = eta if j == 0 else eta - v_h[L + 1]

        def down(k, w):
            l = L - 1 - k
            w = m_h[l + 1] * ((f_h[l] + xi * hg_h[l]) + w)
            v_h[l + 1] = w if j == 0 else w - v_h[l + 1]
            return w
        loop(L, 16, down, eta)

    def inner_k(j):
        def body(l):
            a = v_m[j, l + 1]
            rows = jnp.where(sub == 0, 0.0, pltpu.roll(a, 1, 0)) + jnp.where(sub == 7, 0.0, pltpu.roll(a, 7, 0))
            u_m[j, l + 1] = (d_m[l] * a - (rows + sides(a))) - 2.0 * (v_m[j, l] + v_m[j, l + 2])
        each(L, 8, body)
        if j < STEPS - 1:
            body(L)

    def outer_dots(j):
        def body(l, carry):
            b = v_h[l + 1]
            add = jnp.where(sub == 0, pltpu.roll(b, 1, 0), jnp.where(sub == 7, pltpu.roll(b, 7, 0), 0.0))
            u = u_m[j, l + 1] - add
            u_m[j, l + 1] = u
            out = [carry[i] + u * u_m[i, l + 1] for i in range(j)]
            return tuple(out + [carry[j] + u * u])
        sums = loop(L, 8, body, (zero,) * (j + 1))
        for i in range(j + 1):
            n = ROW[i, j]
            gram[n:n + 1] = fold(sums[i])

    def one_row(j):
        return j == STEPS - 2 and L % 16 == 0

    def advance(j):
        size = 8 if one_row(j) else 4
        per = L // size // 2
        wrap = pack_outer if one_row(j) else pack_rows

        def settle(l):
            b = v_h[l + 1]
            a = v_m[j, l + 1]
            from_up, from_dn = pltpu.roll(b, 1, 0), pltpu.roll(b, 7, 0)
            u = u_m[j, l + 1] - jnp.where(sub == 0, from_up, jnp.where(sub == 7, from_dn, 0.0))
            u_m[j, l + 1] = u
            up = jnp.where(sub == 0, pltpu.roll(a, 1, 0), from_up)
            dn = jnp.where(sub == 7, pltpu.roll(a, 7, 0), from_dn)
            outer = (d_h[l] * b - ((up + dn) + sides(b))) - 2.0 * (v_h[l] + v_h[l + 2])
            return u, mask_h * outer

        def form(g, carry):
            before, here, outer, fo, go = carry
            tiles_r = []
            for k in range(size):
                l = size * g + k
                after, next_outer = settle(l + 1)
                r = (d_m[l] * here - beside(here, outer)) - 2.0 * (before + after)
                r_m[l] = r
                fo = fo + al_m[l] * r
                go = go + be_m[l] * r
                tiles_r.append(r)
                before, here, outer = here, after, next_outer
            wrap(tiles_r, g, xs_out.at[j, 0], xs_out.at[j, 1])
            return before, here, outer, fo, go

        state = (zero,) + settle(0) + (zero, zero)
        rows = []
        for p in range(2):
            state = loop(per, 8 // size, functools.partial(lambda at, g, c: form(at + g, c), p * per), state)
            if p == 1:
                own = state[3:]
                ed_out[j] = edges(own[0], own[1])
                pl_out[j, 0] = own[0]
                pl_out[j, 1] = own[1]
                planes = [
                    post_to(0, ed_out.at[j], ed_in.at[j, 0], {"tile": nxt, "level": other}),
                    post_to(1, ed_out.at[j], ed_in.at[j, 1], {"tile": prv, "level": other}),
                    post(pl_out.at[j], pl_in.at[j], {"level": other}),
                ]
            cut = pl.ds(p * per, per)
            rows.append([
                post_to(0, xs_out.at[j, 0, cut], xs_in.at[j, 0, cut], {"tile": nxt}),
                post_to(1, xs_out.at[j, 1, cut], xs_in.at[j, 1, cut], {"tile": prv}),
            ])
        return own, planes, rows

    def fold(acc):
        row = jnp.sum(acc, axis=0, keepdims=True)
        total = row[:, :128]
        for n in range(1, Y // 128):
            total = total + row[:, n * 128:(n + 1) * 128]
        return total

    def side_dot(j):
        n = len(PAIRS) + j
        gram[n:n + 1] = fold(loop(L, 8, lambda l, acc: acc + v_m[j, l + 1] * s_m[l + 1], zero))

    def dots(j):
        def body(l, carry):
            u = u_m[j, l + 1]
            return tuple(carry[i] + u * u_m[i, l + 1] for i in range(j + 1))
        sums = loop(L, 8, body, (zero,) * (j + 1))
        for i in range(j + 1):
            n = ROW[i, j]
            gram[n:n + 1] = fold(sums[i])

    low = lane_h < 64

    def quarter(q, top, bot):
        n = q // 2
        p, b = top[:, n * 128:(n + 1) * 128], bot[:, n * 128:(n + 1) * 128]
        if q % 2 == 0:
            return jnp.where(low, p, pltpu.roll(b, 64, 1))
        return jnp.where(low, pltpu.roll(p, 64, 1), b)

    def fill_t(j):
        def body(l):
            top = v_m[j, l + 1] * ks[l] + u_m[j, l + 1] * s_m[l + 1]
            k = l + H
            bot = v_m[j, k + 1] * ks[k] + u_m[j, k + 1] * s_m[k + 1]
            for q in range(probes):
                t_out[j, q, l] = quarter(q, top, bot)
            t_in[j, probe, l] = t_out[j, probe, l]
        each(H, 2, body)

    trace_parts = []

    def send_t(j):
        for g in p_peers:
            trace_parts.append(post(t_out.at[j, g], t_in.at[j, probe], {"probe": g}))

    loads[0].wait()

    for side in range(2):
        @pl.when(jnp.logical_not(not_end[1 - side]))
        def _():
            def clear(g):
                for k in range(3):
                    halo_in[k, side, g] = zero
                for k in range(STEPS - 1):
                    xs_in[k, side, g] = zero
            each(L // 4, 1, clear)
            for k in range(2):
                side_in[side, k] = zero
            for k in range(STEPS - 1):
                ed_in[k, side] = zero

    def put_d(l):
        d = kap_v[src(l)] + 8.0
        d_m[l] = d
        return d
    pack(put_d, halo_out.at[0, 0], halo_out.at[0, 1])
    mo_m, ho_m = factor(d_m, m_m, hg_m)
    loads[1].wait()

    def put_s(l):
        s = (2 * bits_v[src(l)] - 1).astype(F32)
        s_m[l + 1] = s
        return s
    pack(put_s, halo_out.at[1, 0], halo_out.at[1, 1])
    own_m = passes(lambda l: [s_m[l + 1]], 1, m_m, f_m)
    loads[2].wait()
    side_out[0] = edges(mo_m, ho_m)
    side_out[1] = edges(own_m[0], own_m[1])
    for n, plane in enumerate((mo_m, ho_m, own_m[0], own_m[1], d_m[L - 1], s_m[L], obs_v[src(L - 1)])):
        first_out[n] = plane
    pl.semaphore_wait(barrier, len(greet) + count(ends))
    halo_d = [
        post_to(0, halo_out.at[0, 0], halo_in.at[0, 0], {"tile": nxt}),
        post_to(1, halo_out.at[0, 1], halo_in.at[0, 1], {"tile": prv}),
    ]
    far = [
        post_to(0, side_out, side_in.at[0], {"tile": nxt, "level": other}),
        post_to(1, side_out, side_in.at[1], {"tile": prv, "level": other}),
        post(first_out, first_in, {"level": other}),
    ]
    halo_s = [
        post_to(0, halo_out.at[1, 0], halo_in.at[1, 0], {"tile": nxt}),
        post_to(1, halo_out.at[1, 1], halo_in.at[1, 1], {"tile": prv}),
    ]
    s_m[0] = zero
    o_m[0] = zero
    for j in range(STEPS):
        v_m[j, 0] = zero
        u_m[j, 0] = zero
    v_h[0] = zero
    v_h[L + 2] = zero
    d_h[L] = zero

    def put_o(l):
        o = obs_v[src(l)]
        o_m[l + 1] = o
        return o
    pack(put_o, halo_out.at[2, 0], halo_out.at[2, 1])
    halo_o = [
        post_to(0, halo_out.at[2, 0], halo_in.at[2, 0], {"tile": nxt}),
        post_to(1, halo_out.at[2, 1], halo_in.at[2, 1], {"tile": prv}),
    ]

    def weigh(k, x):
        l = L - 1 - k
        al_m[l] = x
        return m_m[l] * x
    loop(L, 16, weigh, zero + 0.5)
    solve(lambda l: [al_m[l]], 1, m_m, r_m, be_m)

    for copy in halo_d:
        copy.wait_recv()

    def put_dh(l, x):
        d_h[l] = jnp.where(mask_h > 0.0, x, 8.0)
    unpack(halo_in.at[0, 0], halo_in.at[0, 1], put_dh)
    mo_h, ho_h = factor(d_h, m_h, hg_h)

    far[2].wait_recv()
    mp_m, hp_m, fp_m, gp_m, dp_m = (first_in[n] for n in range(5))
    d_m[L] = dp_m
    s_m[L + 1] = first_in[5]
    o_m[L + 1] = first_in[6]
    const_m = (mo_m, ho_m, mp_m, hp_m, 1.0 / (1.0 - mo_m * mp_m))
    finish_m(0, const_m, own_m, (fp_m, gp_m), dp_m)
    inner_k(0)

    for copy in halo_s:
        copy.wait_recv()

    def read_sh(g):
        rows = [x * mask_h for x in beside_rows(halo_in.at[1, 0], halo_in.at[1, 1], g)]
        for k, x in enumerate(rows):
            s_h[4 * g + k] = x
        return rows
    own_h = passes(read_sh, 4, m_h, f_h)
    for copy in far[:2]:
        copy.wait_recv()

    mp_h, hp_h = beyond(side_in[0, 0], side_in[1, 0])
    fp_h, gp_h = beyond(side_in[0, 1], side_in[1, 1])
    const_h = (mo_h, ho_h, mp_h, hp_h, 1.0 / (1.0 - mo_h * mp_h))
    finish_h(0, const_h, own_h, (mask_h * fp_h, mask_h * gp_h))
    own_m, planes, rows = advance(0)

    odd = lax.rem(probe, 2) == 1
    upper = probe // 2 == 1

    def mine(top, bot):
        out = [jnp.where(odd, quarter(2 * n + 1, top, bot), quarter(2 * n, top, bot)) for n in range(Y // 128)]
        return jnp.where(upper, out[1], out[0])

    def side_terms():
        for copy in halo_o:
            copy.wait_recv()

        def put_oh(l, x):
            o_h[l] = x * mask_h
        unpack(halo_in.at[2, 0], halo_in.at[2, 1], put_oh)

        def body(l):
            a = s_m[l + 1]
            ks[l] = (d_m[l] * a - beside(a, s_h[l])) - 2.0 * (s_m[l] + s_m[l + 2])
            b = o_m[l + 1]
            ko = (d_m[l] * b - beside(b, o_h[l])) - 2.0 * (o_m[l] + o_m[l + 2])
            data[l] = kap_v[src(l)] * (2.0 * b * ko)
        each(L, 4, body)

    def quarters():
        def body(l):
            kap_q[l] = mine(kap_v[src(l)], kap_v[src(l + H)]) * (1.0 / probes)
            sub_q[l] = mine(data[l], data[l + H])
        each(H, 2, body)

    for j in range(1, STEPS):
        n = j - 1
        signal_if(here_sem.at[n], along_z(2 ** n))
        passes(lambda l: [r_m[l]], 1, m_m, f_m)
        dots(j - 1)
        side_dot(j - 1)
        if j == 1:
            side_terms()
        if j == 2:
            quarters()
        fill_t(j - 1)
        planes[2].wait_recv()
        finish_m(j, const_m, own_m, (pl_in[n, 0], pl_in[n, 1]), dp_m)
        inner_k(j)
        if j == STEPS - 1:
            side_dot(j)
            for i in range(len(PAIRS) + STEPS, N_ROWS):
                gram[i:i + 1] = jnp.zeros((1, 128), F32)
        beside_r = beside_outer if one_row(j - 1) else beside_rows

        def read_rh(g):
            return [x * mask_h for x in beside_r(xs_in.at[n, 0], xs_in.at[n, 1], g)]
        own_h = passes(read_rh, 8 if one_row(j - 1) else 4, m_h, f_h, rows)
        for copy in planes[:2]:
            copy.wait_recv()
        pl.semaphore_wait(here_sem.at[n], count(along_z(2 ** n)))
        send_t(j - 1)
        fp_h, gp_h = beyond(ed_in[n, 0], ed_in[n, 1])
        finish_h(j, const_h, own_h, (mask_h * fp_h, mask_h * gp_h))
        if j < STEPS - 1:
            own_m, planes, rows = advance(j)
        else:
            outer_dots(j)

    wide = lax.broadcasted_iota(jnp.int32, (N_ROWS, 128), 1) == lax.broadcasted_iota(jnp.int32, (N_ROWS, 128), 0)
    each_sum = jnp.sum(gram[...], axis=1, keepdims=True)
    packed = jnp.sum(jnp.where(wide, each_sum, 0.0), axis=0, keepdims=True)
    for copy in trace_parts[:probes - 1]:
        copy.wait_recv()
    red_out[...] = packed
    red_a[spot] = packed
    plane = [post(red_out, red_a.at[spot], dev) for dev in a_peers]
    fill_t(STEPS - 1)
    send_t(STEPS - 1)
    for copy in plane:
        copy.wait_recv()
    for p in range(probes):
        base = p * levels * x_chips
        part = red_a[base]
        for k in range(1, levels * x_chips):
            part = part + red_a[base + k]
        red_b[zc, p] = part
    before = list(started)
    line = [post(red_b.at[zc], red_b.at[zc], dev) for dev in b_peers]
    for copy in before:
        copy.wait_send()
    for copy in line:
        copy.wait_recv()
    total = None
    for p in range(probes):
        part = red_b[0, p]
        for k in range(1, z_chips):
            part = part + red_b[k, p]
        part = jnp.broadcast_to(part, (8, 128))
        total = part if p == 0 else jnp.where(sub_h == p, part, total)

    def column(n):
        return jnp.broadcast_to(total[:, n:n + 1], (8, 128))
    a = {pair: column(n) for pair, n in ROW.items()}
    c = [column(len(PAIRS) + j) for j in range(STEPS)]
    pivot = []
    ratio = {}
    for j in range(STEPS):
        pivot.append(1.0 / a[j, j])
        for i in range(j + 1, STEPS):
            ratio[j, i] = a[j, i] * pivot[j]
        for i in range(j + 1, STEPS):
            c[i] = c[i] - ratio[j, i] * c[j]
            for k in range(i, STEPS):
                a[i, k] = a[i, k] - ratio[j, i] * a[j, k]
    for j in range(STEPS - 1, -1, -1):
        c[j] = c[j] * pivot[j]
        for i in range(j + 1, STEPS):
            c[j] = c[j] - ratio[j, i] * c[i]
    weight = {(p, j): jnp.broadcast_to(c[j][p:p + 1], (8, 128)) for p in range(probes) for j in range(STEPS)}

    for copy in trace_parts[probes - 1:]:
        copy.wait_recv()

    def write(l):
        acc = None
        for j in range(STEPS):
            for p in range(probes):
                part = weight[p, j] * t_in[j, p, l]
                acc = part if acc is None else acc + part
        res = kap_q[l] * acc - sub_q[l]
        out_ref[src(l)] = res[:, :64]
        out_ref[src(l + H)] = pltpu.roll(res, 64, 1)[:, :64]
    each(H, 4, write)
    for copy in line:
        copy.wait_send()


def solution(mesh):
    probes, tiles, levels = (mesh.shape[a] for a in ("probe", "tile", "level"))
    x_chips = min(X_CHIPS, tiles)
    z_chips = tiles // x_chips

    def step(bits, kap, obs):
        _, L, rows, Y = bits.shape
        dims = (probes, tiles, levels, x_chips, L, Y)
        vm = lambda *lead: pltpu.VMEM((*lead, 8, Y), F32)
        dma = lambda n: pltpu.SemaphoreType.DMA((n,))
        G = L // 4
        n_sems = 9 + 7 * (STEPS - 1) + (probes * levels * x_chips - 1) + (z_chips - 1) + STEPS * (probes - 1)
        part = lambda *lead: pltpu.VMEM((*lead, L // 2, 8, 128), F32)
        scratch = [
            pltpu.VMEM((L, 8, Y), jnp.int32), vm(L), vm(L),
            vm(L + 2), vm(L), vm(L + 1), vm(L + 1), vm(L + 2), vm(L),
            vm(L + 1), vm(L + 1), vm(L), vm(L), vm(L), vm(L),
            vm(STEPS, L + 3), vm(L + 3), vm(STEPS, L + 2), vm(L), vm(L), vm(L), vm(L), vm(L),
            vm(3, 2, G), vm(3, 2, G), vm(STEPS - 1, 2, G), vm(STEPS - 1, 2, G),
            vm(7), vm(7), vm(2), vm(2, 2),
            vm(STEPS - 1, 2), vm(STEPS - 1, 2), vm(STEPS - 1), vm(STEPS - 1, 2),
            pltpu.VMEM((N_ROWS, 128), F32),
            pltpu.VMEM((1, 128), F32),
            pltpu.VMEM((probes * levels * x_chips, 1, 128), F32),
            pltpu.VMEM((z_chips, probes, 1, 128), F32),
            part(STEPS, probes), part(STEPS, probes), part(), part(), vm(L),
            dma(3), dma(n_sems), dma(n_sems), pltpu.SemaphoreType.REGULAR((STEPS - 1,)),
        ]
        return pl.pallas_call(
            functools.partial(kernel, dims),
            out_shape=pltpu.VMEM((L, rows, Y // probes), F32),
            in_specs=[pl.BlockSpec(memory_space=pl.ANY)] * 3,
            out_specs=pl.BlockSpec(memory_space=pltpu.VMEM),
            scratch_shapes=scratch,
            compiler_params=pltpu.CompilerParams(collective_id=0, has_side_effects=True),
        )(bits, kap, obs)

    return jax.shard_map(
        step,
        mesh=mesh,
        in_specs=(P("probe", "level", "tile", None), P("level", "tile", None), P("level", "tile", None)),
        out_specs=P("level", "tile", "probe"),
        check_vma=False,
    )
```

```python
import functools

import jax
import jax.numpy as jnp
from jax import lax
from jax.experimental import pallas as pl
from jax.experimental.pallas import tpu as pltpu
from jax.sharding import PartitionSpec as P

MESH = pl.DeviceIdType.MESH
STEPS = 4
F32 = jnp.float32
X_CHIPS = 4

PAIRS = [(i, j) for j in range(STEPS) for i in range(j + 1)]
ROW = {pair: n for n, pair in enumerate(PAIRS)}
N_ROWS = 16


def kernel(
    dims,
    bits_hbm, kap_hbm, obs_hbm, out_ref,
    bits_v, kap_v, obs_v,
    s_m, s_h, d_m, d_h, o_m, o_h,
    m_m, m_h, hg_m, hg_h, al_m, be_m,
    v_m, v_h, u_m, r_m, f_m, f_h, y_f, ks,
    halo_out, halo_in, xs_out, xs_in,
    first_out, first_in, side_out, side_in, pl_out, pl_in, ed_out, ed_in,
    gram, red_out, red_a, red_b, t_out, t_in, kap_q, sub_q, data,
    in_sem, send_sem, recv_sem, here_sem,
):
    probes, tiles, levels, x_chips, L, Y = dims
    z_chips = tiles // x_chips
    H = L // 2
    probe = lax.axis_index("probe")
    tile = lax.axis_index("tile")
    half = lax.axis_index("level")
    zc = tile // x_chips
    xc = tile - zc * x_chips
    nxt = lax.rem(tile + 1, tiles)
    prv = lax.rem(tile + tiles - 1, tiles)
    other = 1 - half
    n_a = probes * levels * x_chips
    spot = (probe * levels + half) * x_chips + xc

    loads = [
        pltpu.make_async_copy(kap_hbm, kap_v, in_sem.at[0]),
        pltpu.make_async_copy(bits_hbm.at[0], bits_v, in_sem.at[1]),
        pltpu.make_async_copy(obs_hbm, obs_v, in_sem.at[2]),
    ]
    for copy in loads:
        copy.start()

    def around(n):
        return sorted(range(1, n), key=lambda k: (-min(k, n - k), k))

    near_p = [lax.rem(probe + k, probes) for k in around(probes)]
    near_x = [tile - xc + lax.rem(xc + k, x_chips) for k in around(x_chips)]
    a_peers = [{"probe": p, "tile": t, "level": h}
               for t in near_x + [tile] for h in (other, half) for p in near_p + [probe]][:-1]
    b_peers = [{"tile": lax.rem(tile + k * x_chips, tiles)} for k in around(z_chips)]
    p_peers = near_p
    not_end = [tile < tiles - 1, tile > 0]

    def along_z(d):
        return [(zc + d < z_chips, {"tile": lax.rem(tile + d * x_chips, tiles)}),
                (zc >= d, {"tile": lax.rem(tile + tiles - d * x_chips, tiles)})]

    def signal_if(sem, pairs):
        for there, dev in pairs:
            pl.when(there)(functools.partial(
                pl.semaphore_signal, sem, inc=1, device_id=dev, device_id_type=MESH))

    def count(pairs):
        return sum(there.astype(jnp.int32) for there, _ in pairs)

    barrier = pltpu.get_barrier_semaphore()
    ends = [(not_end[0], {"tile": nxt}), (not_end[1], {"tile": prv}),
            (not_end[0], {"tile": nxt, "level": other}), (not_end[1], {"tile": prv, "level": other})]
    ends += along_z(1)
    greet = [{"level": other}] + [{"probe": p} for p in p_peers]
    signal_if(barrier, ends)
    for dev in greet:
        pl.semaphore_signal(barrier, inc=1, device_id=dev, device_id_type=MESH)

    sub = lax.broadcasted_iota(jnp.int32, (8, Y), 0)
    lane_h = lax.broadcasted_iota(jnp.int32, (8, 128), 1)
    sub_h = lax.broadcasted_iota(jnp.int32, (8, 128), 0)
    has_next = (tile < tiles - 1).astype(F32)
    has_prev = (tile > 0).astype(F32)
    mask_h = jnp.where(sub < 2, has_next, jnp.where(sub >= 6, has_prev, 0.0))
    zero = jnp.zeros((8, Y), F32)

    def src(l):
        return half * (L - 1) + (1 - 2 * half) * l

    def send(src_ref, dst_ref, ssem, rsem, dev):
        copy = pltpu.make_async_remote_copy(
            src_ref=src_ref, dst_ref=dst_ref, send_sem=ssem, recv_sem=rsem,
            device_id=dev, device_id_type=MESH)
        copy.start()
        return copy

    started = []
    counter = [0]

    def post(src_ref, dst_ref, dev):
        n = counter[0]
        counter[0] += 1
        copy = send(src_ref, dst_ref, send_sem.at[n], recv_sem.at[n], dev)
        started.append(copy)
        return copy

    class Ended:
        def __init__(self, copy, goes, comes):
            self.copy, self.goes, self.comes = copy, goes, comes
            pl.when(goes)(copy.start)

        def wait_send(self):
            pl.when(self.goes)(self.copy.wait_send)

        def wait_recv(self):
            pl.when(self.comes)(self.copy.wait_recv)

    def post_to(side, src_ref, dst_ref, dev):
        n = counter[0]
        counter[0] += 1
        copy = pltpu.make_async_remote_copy(
            src_ref=src_ref, dst_ref=dst_ref, send_sem=send_sem.at[n], recv_sem=recv_sem.at[n],
            device_id=dev, device_id_type=MESH)
        copy = Ended(copy, not_end[side], not_end[1 - side])
        started.append(copy)
        return copy

    def loop(n, chunk, body, init=0):
        chunk = min(chunk, n)

        def step(b, carry):
            for k in range(chunk):
                carry = body(b * chunk + k, carry)
            return carry

        return lax.fori_loop(0, n // chunk, step, init)

    def each(n, chunk, body):
        def step(l, carry):
            body(l)
            return carry
        loop(n, chunk, step)

    def pack_rows(rows, g, up_ref, dn_ref):
        up = rows[3]
        dn = pltpu.roll(rows[3], 6, 0)
        for k in (2, 1, 0):
            up = jnp.where(sub < 2 * k + 2, pltpu.roll(rows[k], 2 * k + 2, 0), up)
            dn = jnp.where(sub < 2 * k + 2, pltpu.roll(rows[k], 2 * k, 0) if k else rows[k], dn)
        up_ref[g] = up
        dn_ref[g] = dn

    def pack(put, up_ref, dn_ref):
        each(L // 4, 2, lambda g: pack_rows([put(4 * g + k) for k in range(4)], g, up_ref, dn_ref))

    def beside_rows(a_ref, b_ref, g):
        a = a_ref[g]
        b = b_ref[g]
        out = []
        for k in range(4):
            ra = pltpu.roll(a, 6 - 2 * k, 0) if k < 3 else a
            rb = pltpu.roll(b, 8 - 2 * k, 0) if k else b
            out.append(jnp.where(sub >= 4, ra, rb))
        return out

    def unpack(a_ref, b_ref, write):
        def body(g):
            for k, x in enumerate(beside_rows(a_ref, b_ref, g)):
                write(4 * g + k, x)
        each(L // 4, 2, body)

    def pack_outer(rows, g, up_ref, dn_ref):
        up = rows[7]
        dn = pltpu.roll(rows[7], 7, 0)
        for k in range(6, -1, -1):
            up = jnp.where(sub <= k, pltpu.roll(rows[k], k + 1, 0), up)
            dn = jnp.where(sub <= k, pltpu.roll(rows[k], k, 0) if k else rows[k], dn)
        up_ref[g] = up
        dn_ref[g] = dn

    def beside_outer(a_ref, b_ref, g):
        a = a_ref[g]
        b = b_ref[g]
        out = []
        for k in range(8):
            ra = pltpu.roll(a, 7 - k, 0) if k < 7 else a
            rb = pltpu.roll(b, 8 - k, 0) if k else b
            out.append(jnp.where(sub >= 4, ra, rb))
        return out

    first_lane = lane_h == 0
    last_lane = lane_h == 127

    def sides(a):
        parts = [a[:, n * 128:(n + 1) * 128] for n in range(Y // 128)]
        right = [pltpu.roll(x, 1, 1) for x in parts]
        left = [pltpu.roll(x, 127, 1) for x in parts]
        out = []
        for n in range(len(parts)):
            before = jnp.where(first_lane, right[n - 1] if n else 0.0, right[n])
            after = jnp.where(last_lane, left[n + 1] if n + 1 < len(parts) else 0.0, left[n])
            out.append(before + after)
        return jnp.concatenate(out, axis=1)

    def beside(a, b):
        up = jnp.where(sub == 0, pltpu.roll(b, 1, 0), pltpu.roll(a, 1, 0))
        dn = jnp.where(sub == 7, pltpu.roll(b, 7, 0), pltpu.roll(a, 7, 0))
        return (up + dn) + sides(a)

    def factor(d_ref, m_ref, hg_ref):
        m_ref[0] = zero

        def up(l, m):
            m = 2.0 / (d_ref[l] - 2.0 * m)
            m_ref[l + 1] = m
            return m
        last = loop(L, 8, up, zero)

        def down(k, h):
            l = L - 1 - k
            h = m_ref[l + 1] * h
            hg_ref[l] = h
            return h
        loop(L, 8, down, zero + 1.0)

        def again(l, g):
            g = 0.5 * hg_ref[l] + m_ref[l] * g
            hg_ref[l] = g
            return g
        return last, loop(L, 8, again, zero)

    def solve(read, size, m_ref, f_ref, y_ref, waits=()):
        def fwd(g, f):
            for k, r in enumerate(read(g)):
                l = g * size + k
                f = 0.5 * r + m_ref[l] * f
                f_ref[l] = f
            return f
        pieces = max(len(waits), 1)
        per = L // size // pieces
        first = zero
        for p in range(pieces):
            for copy in waits[p] if waits else ():
                copy.wait_recv()
            first = loop(per, max(16 // size, 1), functools.partial(lambda at, g, f: fwd(at + g, f), p * per), first)

        def back(k, y):
            l = L - 1 - k
            y = m_ref[l + 1] * (f_ref[l] + y)
            y_ref[l] = y
            return y
        loop(L, 16, back, zero)
        return first

    def passes(read, size, m_ref, f_ref, waits=()):
        first = solve(read, size, m_ref, f_ref, y_f, waits)

        def again(l, g):
            g = 0.5 * y_f[l] + m_ref[l] * g
            f_ref[l] = g
            return g
        return first, loop(L, 16, again, zero)

    def edges(a, b):
        inside = jnp.where(sub < 4, pltpu.roll(b, 2, 0), pltpu.roll(b, 6, 0))
        return jnp.where((sub >= 2) & (sub < 6), inside, a)

    def beyond(a, b):
        return jnp.where(sub >= 4, a, b), jnp.where(sub >= 4, pltpu.roll(a, 2, 0), pltpu.roll(b, 6, 0))

    def join(const, own, far):
        mo, ho, mp, hp, inv = const
        (fo, go), (fp, gp) = own, far
        x = mo * (fo + mp * fp) * inv
        xi = mp * (fp + mo * fo) * inv
        g = go + xi * ho
        gf = gp + x * hp
        w = mo * (g + mp * gf) * inv
        eta = mp * (gf + mo * g) * inv
        return xi, w, eta

    def finish_m(j, const, own, far, dp):
        xi, w, eta = join(const, own, far)
        next_one = 0.5 * (dp * eta - xi) - w
        v_m[j, L + 1] = eta if j == 0 else eta - v_m[j - 1, L + 1]
        v_m[j, L + 2] = next_one if j == 0 else next_one - v_m[j - 1, L + 2]

        def down(k, w):
            l = L - 1 - k
            w = m_m[l + 1] * ((f_m[l] + xi * hg_m[l]) + w)
            v_m[j, l + 1] = w if j == 0 else w - v_m[j - 1, l + 1]
            return w
        loop(L, 16, down, eta)

    def finish_h(j, const, own, far):
        xi, w, eta = join(const, own, far)
        v_h[L + 1] = eta if j == 0 else eta - v_h[L + 1]

        def down(k, w):
            l = L - 1 - k
            w = m_h[l + 1] * ((f_h[l] + xi * hg_h[l]) + w)
            v_h[l + 1] = w if j == 0 else w - v_h[l + 1]
            return w
        loop(L, 16, down, eta)

    def inner_k(j):
        def body(l):
            a = v_m[j, l + 1]
            rows = jnp.where(sub == 0, 0.0, pltpu.roll(a, 1, 0)) + jnp.where(sub == 7, 0.0, pltpu.roll(a, 7, 0))
            u_m[j, l + 1] = (d_m[l] * a - (rows + sides(a))) - 2.0 * (v_m[j, l] + v_m[j, l + 2])
        each(L, 8, body)
        if j < STEPS - 1:
            body(L)

    def outer_dots(j):
        def body(l, carry):
            b = v_h[l + 1]
            add = jnp.where(sub == 0, pltpu.roll(b, 1, 0), jnp.where(sub == 7, pltpu.roll(b, 7, 0), 0.0))
            u = u_m[j, l + 1] - add
            u_m[j, l + 1] = u
            out = [carry[i] + u * u_m[i, l + 1] for i in range(j)]
            return tuple(out + [carry[j] + u * u])
        sums = loop(L, 8, body, (zero,) * (j + 1))
        for i in range(j + 1):
            n = ROW[i, j]
            gram[n:n + 1] = fold(sums[i])

    def one_row(j):
        return j == STEPS - 2 and L % 16 == 0

    def advance(j):
        size = 8 if one_row(j) else 4
        per = L // size // 2
        wrap = pack_outer if one_row(j) else pack_rows

        def settle(l):
            b = v_h[l + 1]
            a = v_m[j, l + 1]
            from_up, from_dn = pltpu.roll(b, 1, 0), pltpu.roll(b, 7, 0)
            u = u_m[j, l + 1] - jnp.where(sub == 0, from_up, jnp.where(sub == 7, from_dn, 0.0))
            u_m[j, l + 1] = u
            up = jnp.where(sub == 0, pltpu.roll(a, 1, 0), from_up)
            dn = jnp.where(sub == 7, pltpu.roll(a, 7, 0), from_dn)
            outer = (d_h[l] * b - ((up + dn) + sides(b))) - 2.0 * (v_h[l] + v_h[l + 2])
            return u, mask_h * outer

        def form(g, carry):
            before, here, outer, fo, go = carry
            tiles_r = []
            for k in range(size):
                l = size * g + k
                after, next_outer = settle(l + 1)
                r = (d_m[l] * here - beside(here, outer)) - 2.0 * (before + after)
                r_m[l] = r
                fo = fo + al_m[l] * r
                go = go + be_m[l] * r
                tiles_r.append(r)
                before, here, outer = here, after, next_outer
            wrap(tiles_r, g, xs_out.at[j, 0], xs_out.at[j, 1])
            return before, here, outer, fo, go

        state = (zero,) + settle(0) + (zero, zero)
        rows = []
        for p in range(2):
            state = loop(per, 8 // size, functools.partial(lambda at, g, c: form(at + g, c), p * per), state)
            if p == 1:
                own = state[3:]
                ed_out[j] = edges(own[0], own[1])
                pl_out[j, 0] = own[0]
                pl_out[j, 1] = own[1]
                planes = [
                    post_to(0, ed_out.at[j], ed_in.at[j, 0], {"tile": nxt, "level": other}),
                    post_to(1, ed_out.at[j], ed_in.at[j, 1], {"tile": prv, "level": other}),
                    post(pl_out.at[j], pl_in.at[j], {"level": other}),
                ]
            cut = pl.ds(p * per, per)
            rows.append([
                post_to(0, xs_out.at[j, 0, cut], xs_in.at[j, 0, cut], {"tile": nxt}),
                post_to(1, xs_out.at[j, 1, cut], xs_in.at[j, 1, cut], {"tile": prv}),
            ])
        return own, planes, rows

    def fold(acc):
        row = jnp.sum(acc, axis=0, keepdims=True)
        total = row[:, :128]
        for n in range(1, Y // 128):
            total = total + row[:, n * 128:(n + 1) * 128]
        return total

    def side_dot(j):
        n = len(PAIRS) + j
        gram[n:n + 1] = fold(loop(L, 8, lambda l, acc: acc + v_m[j, l + 1] * s_m[l + 1], zero))

    def dots(j):
        def body(l, carry):
            u = u_m[j, l + 1]
            return tuple(carry[i] + u * u_m[i, l + 1] for i in range(j + 1))
        sums = loop(L, 8, body, (zero,) * (j + 1))
        for i in range(j + 1):
            n = ROW[i, j]
            gram[n:n + 1] = fold(sums[i])

    low = lane_h < 64

    def quarter(q, top, bot):
        n = q // 2
        p, b = top[:, n * 128:(n + 1) * 128], bot[:, n * 128:(n + 1) * 128]
        if q % 2 == 0:
            return jnp.where(low, p, pltpu.roll(b, 64, 1))
        return jnp.where(low, pltpu.roll(p, 64, 1), b)

    def fill_t(j):
        def body(l):
            top = v_m[j, l + 1] * ks[l] + u_m[j, l + 1] * s_m[l + 1]
            k = l + H
            bot = v_m[j, k + 1] * ks[k] + u_m[j, k + 1] * s_m[k + 1]
            for q in range(probes):
                t_out[j, q, l] = quarter(q, top, bot)
            t_in[j, probe, l] = t_out[j, probe, l]
        each(H, 2, body)

    trace_parts = []

    def send_t(j):
        for g in p_peers:
            trace_parts.append(post(t_out.at[j, g], t_in.at[j, probe], {"probe": g}))

    loads[0].wait()

    for side in range(2):
        @pl.when(jnp.logical_not(not_end[1 - side]))
        def _():
            def clear(g):
                for k in range(3):
                    halo_in[k, side, g] = zero
                for k in range(STEPS - 1):
                    xs_in[k, side, g] = zero
            each(L // 4, 1, clear)
            for k in range(2):
                side_in[side, k] = zero
            for k in range(STEPS - 1):
                ed_in[k, side] = zero

    def put_d(l):
        d = kap_v[src(l)] + 8.0
        d_m[l] = d
        return d
    pack(put_d, halo_out.at[0, 0], halo_out.at[0, 1])
    mo_m, ho_m = factor(d_m, m_m, hg_m)
    loads[1].wait()

    def put_s(l):
        s = (2 * bits_v[src(l)] - 1).astype(F32)
        s_m[l + 1] = s
        return s
    pack(put_s, halo_out.at[1, 0], halo_out.at[1, 1])
    own_m = passes(lambda l: [s_m[l + 1]], 1, m_m, f_m)
    loads[2].wait()
    side_out[0] = edges(mo_m, ho_m)
    side_out[1] = edges(own_m[0], own_m[1])
    for n, plane in enumerate((mo_m, ho_m, own_m[0], own_m[1], d_m[L - 1], s_m[L], obs_v[src(L - 1)])):
        first_out[n] = plane
    pl.semaphore_wait(barrier, len(greet) + count(ends))
    far = [
        post_to(0, side_out, side_in.at[0], {"tile": nxt, "level": other}),
        post_to(1, side_out, side_in.at[1], {"tile": prv, "level": other}),
    ]
    halo_d = [
        post_to(0, halo_out.at[0, 0], halo_in.at[0, 0], {"tile": nxt}),
        post_to(1, halo_out.at[0, 1], halo_in.at[0, 1], {"tile": prv}),
    ]
    far.append(post(first_out, first_in, {"level": other}))
    halo_s = [
        post_to(0, halo_out.at[1, 0], halo_in.at[1, 0], {"tile": nxt}),
        post_to(1, halo_out.at[1, 1], halo_in.at[1, 1], {"tile": prv}),
    ]
    s_m[0] = zero
    o_m[0] = zero
    for j in range(STEPS):
        v_m[j, 0] = zero
        u_m[j, 0] = zero
    v_h[0] = zero
    v_h[L + 2] = zero
    d_h[L] = zero

    def put_o(l):
        o = obs_v[src(l)]
        o_m[l + 1] = o
        return o
    pack(put_o, halo_out.at[2, 0], halo_out.at[2, 1])
    halo_o = [
        post_to(0, halo_out.at[2, 0], halo_in.at[2, 0], {"tile": nxt}),
        post_to(1, halo_out.at[2, 1], halo_in.at[2, 1], {"tile": prv}),
    ]

    def weigh(k, x):
        l = L - 1 - k
        al_m[l] = x
        return m_m[l] * x
    loop(L, 16, weigh, zero + 0.5)
    solve(lambda l: [al_m[l]], 1, m_m, r_m, be_m)

    for copy in halo_d:
        copy.wait_recv()

    def put_dh(l, x):
        d_h[l] = jnp.where(mask_h > 0.0, x, 8.0)
    unpack(halo_in.at[0, 0], halo_in.at[0, 1], put_dh)
    mo_h, ho_h = factor(d_h, m_h, hg_h)

    far[2].wait_recv()
    mp_m, hp_m, fp_m, gp_m, dp_m = (first_in[n] for n in range(5))
    d_m[L] = dp_m
    s_m[L + 1] = first_in[5]
    o_m[L + 1] = first_in[6]
    const_m = (mo_m, ho_m, mp_m, hp_m, 1.0 / (1.0 - mo_m * mp_m))
    finish_m(0, const_m, own_m, (fp_m, gp_m), dp_m)
    inner_k(0)

    for copy in halo_s:
        copy.wait_recv()

    def read_sh(g):
        rows = [x * mask_h for x in beside_rows(halo_in.at[1, 0], halo_in.at[1, 1], g)]
        for k, x in enumerate(rows):
            s_h[4 * g + k] = x
        return rows
    own_h = passes(read_sh, 4, m_h, f_h)
    for copy in far[:2]:
        copy.wait_recv()

    mp_h, hp_h = beyond(side_in[0, 0], side_in[1, 0])
    fp_h, gp_h = beyond(side_in[0, 1], side_in[1, 1])
    const_h = (mo_h, ho_h, mp_h, hp_h, 1.0 / (1.0 - mo_h * mp_h))
    finish_h(0, const_h, own_h, (mask_h * fp_h, mask_h * gp_h))
    own_m, planes, rows = advance(0)

    odd = lax.rem(probe, 2) == 1
    upper = probe // 2 == 1

    def mine(top, bot):
        out = [jnp.where(odd, quarter(2 * n + 1, top, bot), quarter(2 * n, top, bot)) for n in range(Y // 128)]
        return jnp.where(upper, out[1], out[0])

    def side_terms():
        for copy in halo_o:
            copy.wait_recv()

        def put_oh(l, x):
            o_h[l] = x * mask_h
        unpack(halo_in.at[2, 0], halo_in.at[2, 1], put_oh)

        def body(l):
            a = s_m[l + 1]
            ks[l] = (d_m[l] * a - beside(a, s_h[l])) - 2.0 * (s_m[l] + s_m[l + 2])
            b = o_m[l + 1]
            ko = (d_m[l] * b - beside(b, o_h[l])) - 2.0 * (o_m[l] + o_m[l + 2])
            data[l] = kap_v[src(l)] * (2.0 * b * ko)
        each(L, 4, body)

    def quarters():
        def body(l):
            kap_q[l] = mine(kap_v[src(l)], kap_v[src(l + H)]) * (1.0 / probes)
            sub_q[l] = mine(data[l], data[l + H])
        each(H, 2, body)

    for j in range(1, STEPS):
        n = j - 1
        signal_if(here_sem.at[n], along_z(2 ** n))
        passes(lambda l: [r_m[l]], 1, m_m, f_m)
        dots(j - 1)
        side_dot(j - 1)
        if j == 1:
            side_terms()
        if j == 2:
            quarters()
        fill_t(j - 1)
        planes[2].wait_recv()
        finish_m(j, const_m, own_m, (pl_in[n, 0], pl_in[n, 1]), dp_m)
        inner_k(j)
        if j == STEPS - 1:
            side_dot(j)
            for i in range(len(PAIRS) + STEPS, N_ROWS):
                gram[i:i + 1] = jnp.zeros((1, 128), F32)
        beside_r = beside_outer if one_row(j - 1) else beside_rows

        def read_rh(g):
            return [x * mask_h for x in beside_r(xs_in.at[n, 0], xs_in.at[n, 1], g)]
        own_h = passes(read_rh, 8 if one_row(j - 1) else 4, m_h, f_h, rows)
        for copy in planes[:2]:
            copy.wait_recv()
        pl.semaphore_wait(here_sem.at[n], count(along_z(2 ** n)))
        send_t(j - 1)
        fp_h, gp_h = beyond(ed_in[n, 0], ed_in[n, 1])
        finish_h(j, const_h, own_h, (mask_h * fp_h, mask_h * gp_h))
        if j < STEPS - 1:
            own_m, planes, rows = advance(j)
        else:
            outer_dots(j)

    wide = lax.broadcasted_iota(jnp.int32, (N_ROWS, 128), 1) == lax.broadcasted_iota(jnp.int32, (N_ROWS, 128), 0)
    each_sum = jnp.sum(gram[...], axis=1, keepdims=True)
    packed = jnp.sum(jnp.where(wide, each_sum, 0.0), axis=0, keepdims=True)
    for copy in trace_parts[:probes - 1]:
        copy.wait_recv()
    red_out[...] = packed
    red_a[spot] = packed
    plane = [post(red_out, red_a.at[spot], dev) for dev in a_peers]
    fill_t(STEPS - 1)
    send_t(STEPS - 1)
    for copy in plane:
        copy.wait_recv()
    for p in range(probes):
        base = p * levels * x_chips
        part = red_a[base]
        for k in range(1, levels * x_chips):
            part = part + red_a[base + k]
        red_b[zc, p] = part
    before = list(started)
    line = [post(red_b.at[zc], red_b.at[zc], dev) for dev in b_peers]
    for copy in before:
        copy.wait_send()
    for copy in line:
        copy.wait_recv()
    total = None
    for p in range(probes):
        part = red_b[0, p]
        for k in range(1, z_chips):
            part = part + red_b[k, p]
        part = jnp.broadcast_to(part, (8, 128))
        total = part if p == 0 else jnp.where(sub_h == p, part, total)

    def column(n):
        return jnp.broadcast_to(total[:, n:n + 1], (8, 128))
    a = {pair: column(n) for pair, n in ROW.items()}
    c = [column(len(PAIRS) + j) for j in range(STEPS)]
    pivot = []
    ratio = {}
    for j in range(STEPS):
        pivot.append(1.0 / a[j, j])
        for i in range(j + 1, STEPS):
            ratio[j, i] = a[j, i] * pivot[j]
        for i in range(j + 1, STEPS):
            c[i] = c[i] - ratio[j, i] * c[j]
            for k in range(i, STEPS):
                a[i, k] = a[i, k] - ratio[j, i] * a[j, k]
    for j in range(STEPS - 1, -1, -1):
        c[j] = c[j] * pivot[j]
        for i in range(j + 1, STEPS):
            c[j] = c[j] - ratio[j, i] * c[i]
    weight = {(p, j): jnp.broadcast_to(c[j][p:p + 1], (8, 128)) for p in range(probes) for j in range(STEPS)}

    for copy in trace_parts[probes - 1:]:
        copy.wait_recv()

    def write(l):
        acc = None
        for j in range(STEPS):
            for p in range(probes):
                part = weight[p, j] * t_in[j, p, l]
                acc = part if acc is None else acc + part
        res = kap_q[l] * acc - sub_q[l]
        out_ref[src(l)] = res[:, :64]
        out_ref[src(l + H)] = pltpu.roll(res, 64, 1)[:, :64]
    each(H, 4, write)
    for copy in line:
        copy.wait_send()


def solution(mesh):
    probes, tiles, levels = (mesh.shape[a] for a in ("probe", "tile", "level"))
    x_chips = min(X_CHIPS, tiles)
    z_chips = tiles // x_chips

    def step(bits, kap, obs):
        _, L, rows, Y = bits.shape
        dims = (probes, tiles, levels, x_chips, L, Y)
        vm = lambda *lead: pltpu.VMEM((*lead, 8, Y), F32)
        dma = lambda n: pltpu.SemaphoreType.DMA((n,))
        G = L // 4
        n_sems = 9 + 7 * (STEPS - 1) + (probes * levels * x_chips - 1) + (z_chips - 1) + STEPS * (probes - 1)
        part = lambda *lead: pltpu.VMEM((*lead, L // 2, 8, 128), F32)
        scratch = [
            pltpu.VMEM((L, 8, Y), jnp.int32), vm(L), vm(L),
            vm(L + 2), vm(L), vm(L + 1), vm(L + 1), vm(L + 2), vm(L),
            vm(L + 1), vm(L + 1), vm(L), vm(L), vm(L), vm(L),
            vm(STEPS, L + 3), vm(L + 3), vm(STEPS, L + 2), vm(L), vm(L), vm(L), vm(L), vm(L),
            vm(3, 2, G), vm(3, 2, G), vm(STEPS - 1, 2, G), vm(STEPS - 1, 2, G),
            vm(7), vm(7), vm(2), vm(2, 2),
            vm(STEPS - 1, 2), vm(STEPS - 1, 2), vm(STEPS - 1), vm(STEPS - 1, 2),
            pltpu.VMEM((N_ROWS, 128), F32),
            pltpu.VMEM((1, 128), F32),
            pltpu.VMEM((probes * levels * x_chips, 1, 128), F32),
            pltpu.VMEM((z_chips, probes, 1, 128), F32),
            part(STEPS, probes), part(STEPS, probes), part(), part(), vm(L),
            dma(3), dma(n_sems), dma(n_sems), pltpu.SemaphoreType.REGULAR((STEPS - 1,)),
        ]
        return pl.pallas_call(
            functools.partial(kernel, dims),
            out_shape=pltpu.VMEM((L, rows, Y // probes), F32),
            in_specs=[pl.BlockSpec(memory_space=pl.ANY)] * 3,
            out_specs=pl.BlockSpec(memory_space=pltpu.VMEM),
            scratch_shapes=scratch,
            compiler_params=pltpu.CompilerParams(collective_id=0, has_side_effects=True),
        )(bits, kap, obs)

    return jax.shard_map(
        step,
        mesh=mesh,
        in_specs=(P("probe", "level", "tile", None), P("level", "tile", None), P("level", "tile", None)),
        out_specs=P("level", "tile", "probe"),
        check_vma=False,
    )
```
